32 devices in a mesh: fsdp: 8 (over z, y), ctx: 4 (over x, core).
Axes of the slice: x: 2, y: 2, z: 4, core: 2. Of those that a mesh axis runs over, the one named last changes fastest.
Arguments:
- tokens: bfloat16 [8, 1024, 2048], P('fsdp', 'ctx'), may hold values from -6 to 6
- norm_gain: bfloat16 [2048], P('fsdp'), may hold values from 0.5 to 1.5
- w_in: bfloat16 [2048, 8512], P('fsdp'), may hold values from -0.125 to 0.125
- conv_w: bfloat16 [4, 4352], P(None, 'fsdp'), may hold values from -3 to 3
- conv_b: bfloat16 [4352], P('fsdp'), may hold values from -0.5 to 0.5
- dt_bias: float32 [64], replicated, may hold values from -4.5 to -3
- a_log: float32 [64], replicated, may hold values from -7 to 0.5
- d_skip: float32 [64], replicated, may hold values from 0.5 to 2
- gate_gain: bfloat16 [4096], P('fsdp'), may hold values from 0.5 to 1.5
- w_out: bfloat16 [4096, 2048], P('fsdp'), may hold values from -0.09375 to 0.09375
- cotangent: bfloat16 [8, 1024, 2048], P('fsdp', 'ctx'), may hold values from -6 to 6
Outputs:
- output: bfloat16 [8, 1024, 2048], P('fsdp', 'ctx')
- grad_tokens: float32 [8, 1024, 2048], P('fsdp', 'ctx')
- grad_norm_gain: float32 [2048], P('fsdp')
- grad_w_in: float32 [2048, 8512], P('fsdp')
- grad_conv_w: float32 [4, 4352], P(None, 'fsdp')
- grad_conv_b: float32 [4352], P('fsdp')
- grad_dt_bias: float32 [64], replicated
- grad_a_log: float32 [64], replicated
- grad_d_skip: float32 [64], replicated
- grad_gate_gain: float32 [4096], P('fsdp')
- grad_w_out: float32 [4096, 2048], P('fsdp')
The draws below stay inside these ranges and needn't reach their ends.
All inputs are finite; a program needn't handle non-finite values.
Results may differ from the reference program's by a relative error of at most 0.0085.
The reference program's roundings to bfloat16 on the way count: a program that leaves them out, or rounds other values in their place, can miss the bound.
Values may be sent and summed in bfloat16 or wider, within the bound.
No kernel may reach another device: no remote copies, remote signals or barrier semaphores. Data moves between devices by JAX's collectives and lax.ppermute only.
A program may use at most 320 MiB of HBM per device.

```python
import jax
import jax.numpy as jnp
from jax import lax

D = 2048
HEADS = 64
HEADDIM = 64
STATE = 128
KW = 4
GROUP = 256
DI = 4096
CONV = 4352
NPROJ = 8512
LENGTH = 1024
SEQS = 8


def steps_of(rng, extent, split, smallest, top_value):
    def one(dim, shards_of):
        heights = jax.random.uniform(jax.random.fold_in(jax.random.fold_in(rng, 6), dim), (shards_of,), jnp.float32, smallest / len(split), top_value / len(split))
        return jnp.repeat(jnp.exp(heights), extent[dim] // shards_of).reshape((-1,) + (1,) * (len(extent) - dim - 1))

    level = one(*split[0])
    for cut in split[1:]:
        level = level * one(*cut)
    return level


def noise(own_key, dims, spread, reach, cuts=(), dtype=jnp.bfloat16):
    level = steps_of(own_key, dims, cuts, -0.22, 0.18) if cuts else 1.0
    array = jax.random.normal(own_key, dims, jnp.float32) * spread * level
    return jnp.minimum(jnp.maximum(array, -reach), reach).astype(dtype)


def setup_inputs(seed: int = 0) -> dict:
    key_list = jax.random.split(jax.random.key(seed), 12)
    tokens = noise(key_list[0], (SEQS, LENGTH, D), 1.0, 6.0, ((0, 8), (1, 4)))
    norm_gain = jnp.clip(1.0 + 0.1 * jax.random.normal(key_list[1], (D,), jnp.float32), 0.5, 1.5).astype(jnp.bfloat16)
    w_in = noise(key_list[2], (D, NPROJ), D ** -0.5, 0.125, ((0, 8),))
    conv_w = noise(key_list[3], (KW, CONV), KW ** -0.5, 3.0, ((1, 8),))
    conv_b = jnp.clip(jax.random.uniform(key_list[4], (CONV,), jnp.float32, -0.5, 0.5) * steps_of(key_list[4], (CONV,), ((0, 8),), -0.4, 0.0), -0.5, 0.5).astype(jnp.bfloat16)
    dt_bias = jnp.clip(jax.random.uniform(key_list[5], (HEADS,), jnp.float32, -4.5, -3.0), -4.5, -3.0)
    a_log = jnp.clip(jax.random.uniform(key_list[6], (HEADS,), jnp.float32, -7.0, 0.5), -7.0, 0.5)
    d_skip = jnp.clip(jax.random.uniform(key_list[7], (HEADS,), jnp.float32, 0.5, 2.0), 0.5, 2.0)
    gate_gain = jnp.clip(1.0 + 0.1 * jax.random.normal(key_list[8], (DI,), jnp.float32), 0.5, 1.5).astype(jnp.bfloat16)
    w_out = noise(key_list[9], (DI, D), DI ** -0.5, 0.09375, ((0, 8),))
    cotangent = noise(key_list[10], (SEQS, LENGTH, D), 1.0, 6.0, ((0, 8), (1, 4)))
    return {"tokens": tokens, "norm_gain": norm_gain, "w_in": w_in, "conv_w": conv_w, "conv_b": conv_b, "dt_bias": dt_bias, "a_log": a_log, "d_skip": d_skip, "gate_gain": gate_gain, "w_out": w_out, "cotangent": cotangent}


EPS = 1e-05
HIGH = lax.Precision.HIGHEST

@jax.custom_vjp
def low(v):
    return lax.optimization_barrier(v.astype(jnp.bfloat16)).astype(jnp.float32)

@jax.custom_vjp
def low_back(v):
    return v

def low_keep(v):
    return (low(v), None)

def low_pass(kept, grad):
    return (grad,)

def back_keep(v):
    return (v, None)

def back_low(kept, grad):
    return (low(grad),)
low.defvjp(low_keep, low_pass)
low_back.defvjp(back_keep, back_low)

def decay_matrix(cumulative):
    count = cumulative.shape[0]
    row_index = lax.broadcasted_iota(jnp.int32, (count, count), 0)
    col_index = lax.broadcasted_iota(jnp.int32, (count, count), 1)
    lower = (row_index >= col_index)[None]
    differ = cumulative.T[:, :, None] - cumulative.T[:, None, :]
    return jnp.where(lower, jnp.exp(jnp.where(lower, differ, 0.0)), 0.0)

def block_step(state, pieces, a_neg):
    x_block, b_block, c_block, step_sizes = pieces
    cumulative = jnp.cumsum(step_sizes * a_neg[None, :], axis=0)
    gram = low_back(jnp.einsum('in,jn->ij', c_block, b_block, precision=HIGH))
    step_cols = step_sizes.T[:, None, :]
    scores = low(gram[None] * decay_matrix(cumulative) * step_cols)
    intra = jnp.einsum('hij,jhp->ihp', scores, x_block, precision=HIGH)
    inner = low_back(jnp.einsum('in,hpn->ihp', c_block, low(state), precision=HIGH))
    tail_vals = jnp.exp(cumulative[-1][None, :] - cumulative) * step_sizes
    weighted = low(tail_vals.T[:, :, None] * b_block[None])
    local = low_back(jnp.einsum('jhp,hjn->hpn', x_block, weighted, precision=HIGH))
    new_state = jnp.exp(cumulative[-1])[:, None, None] * state + local
    return (new_state, intra + jnp.exp(cumulative)[:, :, None] * inner)

def layer(inputs, norm_gain, w_in, conv_w, conv_b, dt_bias, a_log, d_skip, gate_gain, w_out):
    length = inputs.shape[0]
    inner_width = HEADS * HEADDIM
    inverse = lax.rsqrt(lax.optimization_barrier(jnp.mean(inputs * inputs, axis=-1, keepdims=True)) + EPS)
    normed = low(inputs * inverse * norm_gain)
    proj = low_back(low(jnp.dot(normed, w_in, preferred_element_type=jnp.float32, precision=HIGH)))
    gate_z = proj[:, :inner_width]
    conv_in = proj[:, inner_width:inner_width + CONV]
    dt_raw = proj[:, inner_width + CONV:]
    padded = jnp.concatenate([jnp.zeros((KW - 1, CONV), jnp.float32), conv_in], axis=0)
    summed = conv_b[None, :] + conv_w[0][None, :] * padded[0:length]
    for offset in range(1, KW):
        summed = summed + conv_w[offset][None, :] * padded[offset:offset + length]
    act = low(jax.nn.silu(summed))
    xs = act[:, :inner_width].reshape(length, HEADS, HEADDIM)
    bs = act[:, inner_width:inner_width + STATE]
    cs = act[:, inner_width + STATE:]
    step_sizes = jax.nn.softplus(dt_raw + dt_bias[None, :])
    a_neg = -jnp.exp(a_log)
    blocks = length // GROUP
    stepper = jax.checkpoint(block_step)

    def scan_body(state, pieces):
        return stepper(state, pieces, a_neg)
    start = jnp.zeros((HEADS, HEADDIM, STATE), jnp.float32)
    pieces = (xs.reshape(blocks, GROUP, HEADS, HEADDIM), bs.reshape(blocks, GROUP, STATE), cs.reshape(blocks, GROUP, STATE), step_sizes.reshape(blocks, GROUP, HEADS))
    unused, outputs = lax.scan(scan_body, start, pieces)
    ssd_out = outputs.reshape(length, HEADS, HEADDIM) + d_skip[None, :, None] * xs
    ssd_out = low_back(ssd_out.reshape(length, inner_width))
    gated = ssd_out * jax.nn.silu(gate_z)
    inverse_two = lax.rsqrt(lax.optimization_barrier(jnp.mean(gated * gated, axis=-1, keepdims=True)) + EPS)
    mixed = low(gated * inverse_two * gate_gain)
    return inputs + jnp.dot(mixed, w_out, preferred_element_type=jnp.float32, precision=HIGH)

def reference(tokens, norm_gain, w_in, conv_w, conv_b, dt_bias, a_log, d_skip, gate_gain, w_out, cotangent):
    weights = (norm_gain.astype(jnp.float32), w_in.astype(jnp.float32), conv_w.astype(jnp.float32), conv_b.astype(jnp.float32), dt_bias.astype(jnp.float32), a_log.astype(jnp.float32), d_skip.astype(jnp.float32), gate_gain.astype(jnp.float32), w_out.astype(jnp.float32))

    def one_sequence(totals, pair):
        inputs, seed_grad = pair
        result, pullback = jax.vjp(layer, inputs.astype(jnp.float32), weights[0], weights[1], weights[2], weights[3], weights[4], weights[5], weights[6], weights[7], weights[8])
        grads = pullback(seed_grad.astype(jnp.float32))
        totals = jax.tree.map(lambda left, right: left + right, totals, tuple(grads[1:]))
        return (totals, (result.astype(jnp.bfloat16), grads[0]))
    zeros = jax.tree.map(jnp.zeros_like, weights)
    totals, results = lax.scan(one_sequence, zeros, (tokens, cotangent))
    return (results[0], results[1], totals[0], totals[1], totals[2], totals[3], totals[4], totals[5], totals[6], totals[7], totals[8])
```

```python
import jax
import jax.numpy as jnp
import numpy as np
from jax import lax
from jax.experimental import pallas as pl
from jax.experimental.layout import Layout, with_layout_constraint
from jax.experimental.pallas import tpu as pltpu
from jax.sharding import PartitionSpec as P

D = 2048
HEADS = 64
HEADDIM = 64
STATE = 128
KW = 4
GROUP = 256
DI = HEADS * HEADDIM
CONV = DI + 2 * STATE
PAIR = 2 * HEADDIM
EPS = 1e-05
SEG = 256
HALO = 8
VMEM_LIMIT = 56 * 1024 * 1024
F32 = jnp.float32
BF16 = jnp.bfloat16


def ring_place(index, n):
    return jnp.where(index % 2 == 0, index // 2, n - 1 - index // 2)


def ring_member(place, n):
    place = place % n
    return jnp.where(place < n // 2, 2 * place, 2 * (n - 1 - place) + 1)


def ring_routes(n):
    order = [2 * p if p < n // 2 else 2 * (n - 1 - p) + 1 for p in range(n)]
    forward = [(order[p], order[(p + 1) % n]) for p in range(n)]
    return forward, [(b, a) for a, b in forward]


def send(block, route):
    return lax.ppermute(block, "fsdp", route)


def after(value, *earlier):
    return lax.optimization_barrier((value, *earlier))[0]


def halves(rows):
    upper = -(-rows // 256) * 128 if rows % 128 == 0 else rows // 2
    return upper, rows - upper


class Gather:
    def __init__(self, block, n):
        self.forward, self.backward = ring_routes(n)
        self.block, self.n = block, n
        self.latest = (block, block)
        self.ahead, self.behind = [], []

    def hop(self, *gates):
        right, left = self.latest
        last = len(self.ahead) == self.n // 2 - 1
        if last:
            upper, _ = halves(self.block.shape[0])
            right, left = right[:upper], left[upper:]
        right, left = after((right, left), *gates)
        self.latest = send(right, self.forward), send(left, self.backward)
        if not last:
            self.behind.insert(0, self.latest[0])
            self.ahead.append(self.latest[1])

    def parts(self):
        return [self.block] + self.ahead + list(self.latest) + self.behind


class Reduce:
    def __init__(self, chunk, n):
        self.forward, self.backward = ring_routes(n)
        self.chunk, self.n, self.step = chunk, n, n // 2
        first = chunk(n // 2).astype(BF16)
        self.upper, _ = halves(first.shape[0])
        self.right, self.left = first[: self.upper], first[self.upper :]

    def hop(self, *gates):
        right, left = self.right, self.left
        if gates:
            right, left = after((right, left), *gates)
        self.latest = send(right, self.forward), send(left, self.backward)
        self.step -= 1

    def join(self):
        right, left = (part.astype(F32) for part in self.latest)
        if self.step == 0:
            return self.chunk(0).astype(F32) + right + left
        own_right = self.chunk(self.step).astype(F32)
        own_left = self.chunk(self.n - self.step).astype(F32)
        cut = self.upper
        if self.step == self.n // 2 - 1:
            right = jnp.concatenate([own_right[:cut] + right, own_right[cut:]], axis=0)
            left = jnp.concatenate([own_left[:cut], own_left[cut:] + left], axis=0)
        else:
            right, left = own_right + right, own_left + left
        self.right, self.left = right.astype(BF16), left.astype(BF16)


def barrier(value, *earlier):
    return lax.optimization_barrier((value, earlier))[0]


def next_hop(rings, inputs, *earlier):
    pairs, inputs = barrier(([(ring.right, ring.left) for ring in rings], inputs), *earlier)
    for ring, (ring.right, ring.left) in zip(rings, pairs):
        ring.hop()
    return inputs


def ctx_route(m, flip):
    return [(i, i ^ flip) for i in range(m)]


def far_share(block, m):
    return lax.ppermute(block, "ctx", ctx_route(m, 2))


def near_share(block, other, m):
    near = lax.ppermute(block, "ctx", ctx_route(m, 1))
    far = lax.ppermute(other, "ctx", ctx_route(m, 1))
    return [block, near, other, far]


def ctx_share(block, m):
    return near_share(block, far_share(block, m), m)


class CtxReduce:
    def __init__(self, share, m):
        self.m, place = m, lax.axis_index("ctx")
        self.core, self.across = place % 2, place // 2
        split = share.reshape((m // 2, 2) + share.shape[1:])
        self.kept = lax.dynamic_index_in_dim(split, self.core, 1, False)
        sent = lax.dynamic_index_in_dim(split, 1 - self.core, 1, False)
        self.near = lax.ppermute(sent, "ctx", ctx_route(m, 1))

    def middle(self):
        self.both = self.kept.astype(F32) + self.near.astype(F32)
        self.sent = lax.dynamic_index_in_dim(self.both, 1 - self.across, 0, False).astype(BF16)

    def send_far(self):
        self.far = lax.ppermute(self.sent, "ctx", ctx_route(self.m, 2))

    def total(self):
        return lax.dynamic_index_in_dim(self.both, self.across, 0, False) + self.far.astype(F32)


def ctx_reduce(share, m):
    whole = CtxReduce(share, m)
    whole.middle()
    whole.send_far()
    return whole.total()


def axis_sum(values, axis, n):
    flip = 1
    while flip < n:
        values = values + lax.ppermute(values, axis, ctx_route(n, flip))
        flip *= 2
    return values


def ctx_sum(values, m):
    for flip in (1, 2):
        values = values + lax.ppermute(values, "ctx", ctx_route(m, flip))
    return values


def nt(a, b):
    return lax.dot_general(a, b, (((1,), (1,)), ((), ())), preferred_element_type=F32)


def nn(a, b):
    return lax.dot_general(a, b, (((1,), (0,)), ((), ())), preferred_element_type=F32)


def tn(a, b):
    return lax.dot_general(a, b, (((0,), (0,)), ((), ())), preferred_element_type=F32)


def lanes(shape):
    return lax.broadcasted_iota(jnp.int32, shape, len(shape) - 1)


def busy(us, megabytes):
    return pl.CostEstimate(
        flops=int(us * 1e9), transcendentals=0, bytes_accessed=int(megabytes * 1e6)
    )


def softplus(v):
    return jnp.maximum(v, 0.0) + jnp.log1p(jnp.exp(-jnp.abs(v)))


def sigmoid(v):
    return 1.0 / (1.0 + jnp.exp(-v))


def ones_where(keep):
    row = lax.broadcasted_iota(jnp.int32, (GROUP, GROUP), 0)
    col = lax.broadcasted_iota(jnp.int32, (GROUP, GROUP), 1)
    return keep(row, col)


def exact(a, b):
    return lax.dot_general(
        a, b, (((1,), (0,)), ((), ())), preferred_element_type=F32, precision=lax.Precision.HIGHEST
    )


def tiles(width):
    return [slice(at, at + PAIR) for at in range(0, width, PAIR)]


def conv_tile(extended, taps_ref, cols):
    total = taps_ref[KW : KW + 1, cols]
    for k in range(KW):
        at = HALO - KW + 1 + k
        total = total + taps_ref[k : k + 1, cols] * extended[at : at + GROUP]
    return total


def by_segments(weights):
    n = D // SEG
    places = list(range(n // 2)) + [n // 2] * 2 + list(range(n // 2 + 1, n))
    at = [0] * len(places)
    at[n // 2 + 1] = weights[n // 2].shape[0]
    return list(zip(places, at, weights))


def project_into(out_ref, normed_ref, weights, total):
    whole = None
    for o, at, w in by_segments(weights):
        part = nt(normed_ref[:, o * SEG : (o + 1) * SEG], w[...])
        if o == D // SEG // 2:
            total[:, at : at + w.shape[0]] = part
        else:
            whole = part if whole is None else whole + part
    out_ref[...] = (whole + total[...]).astype(BF16)


def front(members_ref, tokens_ref, gain_ref, *refs):
    weights, (normed_ref, proj_ref, total) = refs[:-3], refs[-3:]
    tokens = tokens_ref[...].astype(F32)
    inv = lax.rsqrt(jnp.mean(tokens * tokens, axis=-1, keepdims=True) + EPS)
    for o in range(D // SEG):
        at = pl.multiple_of(members_ref[o] * SEG, SEG)
        cols = slice(o * SEG, (o + 1) * SEG)
        part = tokens_ref[:, pl.ds(at, SEG)].astype(F32) * inv * gain_ref[:, cols]
        normed_ref[:, cols] = part.astype(BF16)
    project_into(proj_ref, normed_ref, weights, total)


def resident(array, grid_args=1):
    zeros = (0,) * array.ndim
    if grid_args == 2:
        return pl.BlockSpec(array.shape, lambda i, t: zeros, pipeline_mode=pl.Buffered(1))
    return pl.BlockSpec(array.shape, lambda i: zeros, pipeline_mode=pl.Buffered(1))


def run_front(members, tokens, gain, weights):
    length, cols = tokens.shape[0], weights[0].shape[0]
    return pl.pallas_call(
        front,
        grid_spec=pltpu.PrefetchScalarGridSpec(
            num_scalar_prefetch=1,
            grid=(length // GROUP,),
            in_specs=[
                pl.BlockSpec((GROUP, D), lambda i, t: (i, 0)),
                pl.BlockSpec((1, D), lambda i, t: (0, 0)),
            ]
            + [resident(w, 2) for w in weights],
            out_specs=[
                pl.BlockSpec((GROUP, D), lambda i, t: (i, 0)),
                pl.BlockSpec((GROUP, cols), lambda i, t: (i, 0)),
            ],
            scratch_shapes=[pltpu.VMEM((GROUP, cols), F32)],
        ),
        out_shape=[
            jax.ShapeDtypeStruct((length, D), BF16),
            jax.ShapeDtypeStruct((length, cols), BF16),
        ],
        compiler_params=pltpu.CompilerParams(vmem_limit_bytes=VMEM_LIMIT),
        cost_estimate=busy(12, 18),
        name="front",
    )(members, tokens, gain, *weights)


def project(normed_ref, *refs):
    project_into(refs[-2], normed_ref, refs[:-2], refs[-1])


def run_project(normed, weights):
    length, cols = normed.shape[0], weights[0].shape[0]
    return pl.pallas_call(
        project,
        grid=(length // GROUP,),
        in_specs=[pl.BlockSpec((GROUP, D), lambda i: (i, 0))] + [resident(w) for w in weights],
        out_specs=pl.BlockSpec((GROUP, cols), lambda i: (i, 0)),
        out_shape=jax.ShapeDtypeStruct((length, cols), BF16),
        scratch_shapes=[pltpu.VMEM((GROUP, cols), F32)],
        compiler_params=pltpu.CompilerParams(vmem_limit_bytes=VMEM_LIMIT),
        cost_estimate=busy(8, 10),
        name="project",
    )(normed, *weights)


def mix_forward(
    proj_ref, taps_ref, heads_ref, skip_ref, act_ref, table_ref, y_ref, start_ref, state, halo
):
    pairs = state.shape[0]
    heads, width = 2 * pairs, pairs * PAIR
    core = width + 2 * STATE

    @pl.when(pl.program_id(0) == 0)
    def _():
        state[...] = jnp.zeros_like(state)
        halo[...] = jnp.zeros_like(halo)

    for cols in tiles(core):
        current = proj_ref[:, cols].astype(F32)
        conv = conv_tile(jnp.concatenate([halo[:, cols], current], axis=0), taps_ref, cols)
        act_ref[:, cols] = (conv * sigmoid(conv)).astype(BF16)
        halo[:, cols] = current[GROUP - HALO :]

    raw = proj_ref[:, core : core + PAIR].astype(F32).T[:heads]
    dt = softplus(raw + heads_ref[:heads, 0:1])
    upto = ones_where(lambda row, col: row <= col).astype(F32)
    cum = exact(dt * heads_ref[heads:, 0:1], upto)
    last = cum[:, GROUP - 1 :]
    growth = jnp.exp(cum)
    rows = jnp.concatenate([cum, dt, jnp.exp(last - cum) * dt, growth], axis=0)
    table_ref[0] = rows
    cols_of = rows.T
    bs, cs = act_ref[:, width : width + STATE], act_ref[:, width + STATE : core]
    gram = nt(cs, bs)
    bias = jnp.where(ones_where(lambda row, col: row >= col), 0.0, -1e30)
    bs_t = bs.astype(F32).T
    for g, cols in enumerate(tiles(width)):
        x = act_ref[:, cols]
        first = lanes(x.shape) < HEADDIM
        start = state[g]
        start_ref[0, g] = start
        inner = nn(cs, start.astype(BF16))
        parts, locals_ = [], []
        for e in range(2):
            h = 2 * g + e
            decay = jnp.exp(cols_of[:, h : h + 1] - rows[h : h + 1, :] + bias)
            scores = (gram * decay * rows[heads + h : heads + h + 1, :]).astype(BF16)
            parts.append(nn(scores, x))
            at = 2 * heads + h
            locals_.append(nn((bs_t * rows[at : at + 1, :]).astype(BF16), x))
        at = 3 * heads + 2 * g
        grow = jnp.where(first, cols_of[:, at : at + 1], cols_of[:, at + 1 : at + 2])
        y_ref[:, cols] = (
            jnp.where(first, parts[0], parts[1]) + grow * inner + skip_ref[:, cols] * x.astype(F32)
        )
        shrink = jnp.where(
            first[:1], growth[2 * g : 2 * g + 1, GROUP - 1 :], growth[2 * g + 1 : 2 * g + 2, GROUP - 1 :]
        )
        state[g] = shrink * start + jnp.where(first[:STATE], locals_[0], locals_[1])


def run_mix_forward(proj, taps, heads_in, skip, pairs):
    length = proj.shape[0]
    blocks, width = length // GROUP, pairs * PAIR
    core = width + 2 * STATE
    whole = lambda i: (0, 0)
    return pl.pallas_call(
        mix_forward,
        grid=(blocks,),
        in_specs=[
            pl.BlockSpec((GROUP, proj.shape[1]), lambda i: (i, 0)),
            pl.BlockSpec(taps.shape, whole),
            pl.BlockSpec(heads_in.shape, whole),
            pl.BlockSpec(skip.shape, whole),
        ],
        out_specs=[
            pl.BlockSpec((GROUP, core), lambda i: (i, 0)),
            pl.BlockSpec((1, 8 * pairs, GROUP), lambda i: (i, 0, 0)),
            pl.BlockSpec((GROUP, width), lambda i: (i, 0)),
            pl.BlockSpec((1, pairs, STATE, PAIR), lambda i: (i, 0, 0, 0)),
        ],
        out_shape=[
            jax.ShapeDtypeStruct((length, core), BF16),
            jax.ShapeDtypeStruct((blocks, 8 * pairs, GROUP), F32),
            jax.ShapeDtypeStruct((length, width), F32),
            jax.ShapeDtypeStruct((blocks, pairs, STATE, PAIR), F32),
        ],
        scratch_shapes=[pltpu.VMEM((pairs, STATE, PAIR), F32), pltpu.VMEM((HALO, core), F32)],
        compiler_params=pltpu.CompilerParams(vmem_limit_bytes=VMEM_LIMIT),
        cost_estimate=busy(18, 15),
        name="mix_forward",
    )(proj, taps, heads_in, skip)


def mix_backward(
    top, act_ref, proj_ref, prev_ref, taps_ref, heads_ref, skip_ref, table_ref, start_ref, dy_ref,
    carry_in, halo_in, held_ref, dx_ref, grads_ref, dheads_ref, carried, halo, columns, ends,
):
    pairs = carried.shape[0]
    heads, width = 2 * pairs, pairs * PAIR
    core = width + 2 * STATE
    step = pl.program_id(0)

    @pl.when(step == 0)
    def _():
        carried[...] = carry_in[...]
        halo[...] = halo_in[...]
        grads_ref[...] = jnp.zeros_like(grads_ref)
        dheads_ref[...] = jnp.zeros_like(dheads_ref)

    has_prev = jnp.where(top - step > 0, 1.0, 0.0)
    rows = table_ref[0]
    cols_of = rows.T
    bs, cs = act_ref[:, width : width + STATE], act_ref[:, width + STATE : core]
    bs_float = bs.astype(F32)
    cs_t = cs.astype(F32).T.astype(BF16)
    gram = nt(bs, cs)
    bias = jnp.where(ones_where(lambda row, col: row <= col), 0.0, -1e30)

    def conv_back(d_act, cols):
        before = prev_ref[:, cols].astype(F32)[prev_ref.shape[0] - HALO :] * has_prev
        extended = jnp.concatenate([before, proj_ref[:, cols].astype(F32)], axis=0)
        conv = conv_tile(extended, taps_ref, cols)
        sig = sigmoid(conv)
        d_conv = d_act * (sig * (1.0 + conv * (1.0 - sig)))
        onward = jnp.concatenate([d_conv, halo[:, cols]], axis=0)
        d_in = taps_ref[KW - 1 : KW, cols] * d_conv
        for k in range(KW - 1):
            at = KW - 1 - k
            d_in = d_in + taps_ref[k : k + 1, cols] * onward[at : at + GROUP]
        dx_ref[:, cols] = d_in.astype(BF16)
        for k in range(KW):
            at = HALO - KW + 1 + k
            grads_ref[k : k + 1, cols] += jnp.sum(
                d_conv * extended[at : at + GROUP], axis=0, keepdims=True
            )
        grads_ref[KW : KW + 1, cols] += jnp.sum(d_conv, axis=0, keepdims=True)
        halo[:, cols] = d_conv[:HALO]

    dgram = jnp.zeros((GROUP, GROUP), F32)
    db = jnp.zeros((GROUP, STATE), F32)
    dc = jnp.zeros((GROUP, STATE), F32)
    sums_j = []
    for g, cols in enumerate(tiles(width)):
        x, dy = act_ref[:, cols], dy_ref[:, cols]
        first = lanes(x.shape) < HEADDIM
        dy_float = dy.astype(F32)
        start, grad = start_ref[0, g], carried[g]
        start_low, grad_low = start.astype(BF16), grad.astype(BF16)
        inner = nn(cs, start_low)
        at = 3 * heads + 2 * g
        grow = jnp.where(first, cols_of[:, at : at + 1], cols_of[:, at + 1 : at + 2])
        d_inner = (dy_float * grow).astype(BF16)
        dc = dc + nt(d_inner, start_low)
        touched = dy_float * inner
        held = jnp.sum(grad * start, axis=0, keepdims=True)
        zero = jnp.zeros_like(x)
        parts = []
        for e in range(2):
            h = 2 * g + e
            own = first if e == 0 else jnp.logical_not(first)
            x_own = jnp.where(own, x, zero)
            dt_col = cols_of[:, heads + h : heads + h + 1]
            tail_col = cols_of[:, 2 * heads + h : 2 * heads + h + 1]
            decay = jnp.exp(rows[h : h + 1, :] - cols_of[:, h : h + 1] + bias)
            common = nt(x_own, dy) * decay
            scores = (gram * decay * dt_col).astype(BF16)
            dgram = dgram + common * dt_col
            linked = common * gram
            columns[:, heads + h : heads + h + 1] = jnp.sum(linked, axis=1, keepdims=True)
            sums_j.append(jnp.sum(linked * dt_col, axis=0, keepdims=True))
            parts.append(nn(scores, dy) + nn((bs_float * tail_col).astype(BF16), grad_low))
            d_weighted = nt(x_own, grad_low)
            db = db + d_weighted * tail_col
            columns[:, h : h + 1] = jnp.sum(d_weighted * bs_float, axis=1, keepdims=True)
            columns[:, 2 * heads + h : 2 * heads + h + 1] = jnp.sum(
                jnp.where(own, touched, 0.0), axis=1, keepdims=True
            )
            ends[h : h + 1, :] = jnp.where(own[:1], held, 0.0)
        conv_back(jnp.where(first, parts[0], parts[1]) + skip_ref[:, cols] * dy_float, cols)
        shrink = jnp.where(
            first[:1],
            rows[at : at + 1, GROUP - 1 :],
            rows[at + 1 : at + 2, GROUP - 1 :],
        )
        carried[g] = shrink * grad + nn(cs_t, d_inner)
    low = dgram.astype(BF16)
    conv_back(db + nn(low, cs), slice(width, width + STATE))
    conv_back(dc + tn(low, bs), slice(width + STATE, core))

    turned = columns[...].T
    d_tail, sum_i, touched = (turned[k * heads : (k + 1) * heads] for k in range(3))
    cum, dt, tail, growth = (rows[k * heads : (k + 1) * heads] for k in range(4))
    a_neg = heads_ref[heads:, 0:1]
    sum_j = jnp.concatenate(sums_j, axis=0)
    tail_log = d_tail * tail
    d_last = jnp.sum(tail_log, axis=1, keepdims=True)
    d_last = d_last + jnp.sum(ends[...], axis=1, keepdims=True) * growth[:, GROUP - 1 :]
    d_cum = touched * growth - tail_log + sum_j - dt * sum_i
    d_cum = d_cum + jnp.where(lanes(d_cum.shape) == GROUP - 1, d_last, 0.0)
    d_rate = exact(d_cum, ones_where(lambda row, col: row >= col).astype(F32))
    raw = proj_ref[:, core : core + PAIR].astype(F32).T[:heads]
    d_step = d_tail * jnp.exp(cum[:, GROUP - 1 :] - cum) + sum_i
    d_dt = (d_step + d_rate * a_neg) * sigmoid(raw + heads_ref[:heads, 0:1])
    dheads_ref[:heads, :] += d_dt
    dheads_ref[heads:, :] += d_rate * dt
    filled = jnp.concatenate([d_dt, jnp.zeros((PAIR - heads, GROUP), F32)], axis=0)
    dx_ref[:, core : core + PAIR] = filled.T.astype(BF16)


def run_mix_backward(span, top, act, proj, taps, heads_in, skip, table, starts, dy, carry, halo, held):
    pairs = carry.shape[0]
    heads, width = 2 * pairs, pairs * PAIR
    core = width + 2 * STATE
    whole = lambda i: (0, 0)
    block = lambda i: (top - i, 0)
    before = GROUP // 16
    return pl.pallas_call(
        lambda *refs: mix_backward(top, *refs),
        grid=(span,),
        in_specs=[
            pl.BlockSpec((GROUP, core), block),
            pl.BlockSpec((GROUP, proj.shape[1]), block),
            pl.BlockSpec((16, proj.shape[1]), lambda i: (jnp.maximum((top - i) * before - 1, 0), 0)),
            pl.BlockSpec(taps.shape, whole),
            pl.BlockSpec(heads_in.shape, whole),
            pl.BlockSpec(skip.shape, whole),
            pl.BlockSpec((1, 8 * pairs, GROUP), lambda i: (top - i, 0, 0)),
            pl.BlockSpec((1, pairs, STATE, PAIR), lambda i: (top - i, 0, 0, 0)),
            pl.BlockSpec((GROUP, width), block),
            pl.BlockSpec(carry.shape, lambda i: (0, 0, 0)),
            pl.BlockSpec(halo.shape, whole),
            pl.BlockSpec(memory_space=pl.ANY),
        ],
        out_specs=[
            pl.BlockSpec((GROUP, proj.shape[1]), block),
            pl.BlockSpec((8, core), whole),
            pl.BlockSpec((2 * heads, GROUP), whole),
            pl.BlockSpec(carry.shape, lambda i: (0, 0, 0)),
            pl.BlockSpec(halo.shape, whole),
        ],
        out_shape=[
            jax.ShapeDtypeStruct(proj.shape, BF16),
            jax.ShapeDtypeStruct((8, core), F32),
            jax.ShapeDtypeStruct((2 * heads, GROUP), F32),
            jax.ShapeDtypeStruct(carry.shape, F32),
            jax.ShapeDtypeStruct(halo.shape, F32),
        ],
        scratch_shapes=[pltpu.VMEM((GROUP, PAIR), F32), pltpu.VMEM((heads, PAIR), F32)],
        compiler_params=pltpu.CompilerParams(vmem_limit_bytes=VMEM_LIMIT),
        input_output_aliases={} if held is None else {11: 0},
        cost_estimate=busy(12 * span, 5 * span),
        name="mix_backward",
    )(act, proj, proj, taps, heads_in, skip, table, starts, dy, carry, halo, dy if held is None else held)


def gate_sums(seed_ref, w_ref, z_ref, y_ref, gain_ref, scaled_ref, sums_ref, squares, along):
    step = pl.program_id(0)

    @pl.when(step == 0)
    def _():
        squares[...] = jnp.zeros_like(squares)
        along[...] = jnp.zeros_like(along)

    scaled = nt(seed_ref[...], w_ref[...])
    scaled_ref[...] = scaled
    z = z_ref[...].astype(F32)
    gated = y_ref[...] * (z * sigmoid(z))
    square = gated * gated
    lean = scaled * gain_ref[...] * gated
    for cols in tiles(square.shape[1]):
        squares[...] += square[:, cols]
        along[...] += lean[:, cols]

    @pl.when(step == pl.num_programs(0) - 1)
    def _():
        spot = lanes(squares.shape)
        both = jnp.where(
            spot == 0,
            jnp.sum(squares[...], axis=1, keepdims=True),
            jnp.where(spot == 1, jnp.sum(along[...], axis=1, keepdims=True), 0.0),
        )
        sums_ref[...] = both.T[:8]


def run_gate_sums(seed, w_o, z, y, gain):
    length, width = y.shape
    tile = 2 * PAIR
    col = pl.BlockSpec((length, tile), lambda i: (0, i))
    return pl.pallas_call(
        gate_sums,
        grid=(width // tile,),
        in_specs=[
            pl.BlockSpec(seed.shape, lambda i: (0, 0), pipeline_mode=pl.Buffered(1)),
            pl.BlockSpec((tile, D), lambda i: (i, 0)),
            col,
            col,
            pl.BlockSpec((1, tile), lambda i: (0, i)),
        ],
        out_specs=[col, pl.BlockSpec((8, length), lambda i: (0, 0))],
        out_shape=[
            jax.ShapeDtypeStruct(y.shape, F32),
            jax.ShapeDtypeStruct((8, length), F32),
        ],
        scratch_shapes=[pltpu.VMEM((length, PAIR), F32)] * 2,
        compiler_params=pltpu.CompilerParams(vmem_limit_bytes=VMEM_LIMIT),
        cost_estimate=busy(11, 20),
        name="gate_sums",
    )(seed, w_o, z, y, gain)


def gate_back(sums_ref, scaled_ref, z_ref, y_ref, x_ref, gain_ref, mixed_ref, dy_ref, dz_ref, cols_ref, turned):
    @pl.when(pl.program_id(0) == 0)
    def _():
        inv = lax.rsqrt(sums_ref[0:1, :] / DI + EPS)
        slope = inv * inv * inv * (sums_ref[1:2, :] / DI)
        rest = jnp.zeros((PAIR - 2, sums_ref.shape[1]), F32)
        turned[...] = jnp.concatenate([inv, slope, rest], axis=0).T

    inv, slope = turned[:, 0:1], turned[:, 1:2]
    z, y, scaled, gain = z_ref[...].astype(F32), y_ref[...], scaled_ref[...], gain_ref[...]
    sig = sigmoid(z)
    silu = z * sig
    gated = y * silu
    normal = gated * inv
    mixed_ref[...] = (normal * gain).astype(BF16)
    d_gated = scaled * gain * inv - gated * slope
    dy = (d_gated * silu).astype(BF16)
    dy_ref[...] = dy
    dz_ref[...] = (d_gated * y * (sig * (1.0 + z * (1.0 - sig)))).astype(BF16)
    cols_ref[0:1, :] = jnp.sum(scaled * normal, axis=0, keepdims=True)
    cols_ref[1:2, :] = jnp.sum(dy.astype(F32) * x_ref[...].astype(F32), axis=0, keepdims=True)
    cols_ref[2:, :] = jnp.zeros_like(cols_ref[2:, :])


def run_gate_back(sums, scaled, z, y, x, gain):
    length, width = y.shape
    tile = PAIR
    col = pl.BlockSpec((length, tile), lambda i: (0, i))
    low = jax.ShapeDtypeStruct(y.shape, BF16)
    return pl.pallas_call(
        gate_back,
        grid=(width // tile,),
        in_specs=[
            pl.BlockSpec(sums.shape, lambda i: (0, 0)),
            col,
            col,
            col,
            col,
            pl.BlockSpec((1, tile), lambda i: (0, i)),
        ],
        out_specs=[col, col, col, pl.BlockSpec((8, tile), lambda i: (0, i))],
        out_shape=[low, low, low, jax.ShapeDtypeStruct((8, width), F32)],
        scratch_shapes=[pltpu.VMEM((length, PAIR), F32)],
        compiler_params=pltpu.CompilerParams(vmem_limit_bytes=VMEM_LIMIT),
        cost_estimate=busy(11, 20),
        name="gate_back",
    )(sums, scaled, z, y, x, gain)


def back_norm(members_ref, tokens_ref, dz_ref, dx_ref, *refs):
    parts, (dn_ref, gain_ref) = refs[:-2], refs[-2:]
    count = len(parts) // 2

    @pl.when(pl.program_id(0) == 0)
    def _():
        gain_ref[...] = jnp.zeros_like(gain_ref)

    tokens = tokens_ref[...].astype(F32)
    inv = lax.rsqrt(jnp.mean(tokens * tokens, axis=-1, keepdims=True) + EPS)
    sums = [None] * (D // SEG)
    for source, weights in ((dz_ref, parts[:count]), (dx_ref, parts[count:])):
        for o, at, w in by_segments(weights):
            part = nn(source[:, at : at + w.shape[0]], w[...])
            sums[o] = part if sums[o] is None else sums[o] + part
    for o, d_normed in enumerate(sums):
        at = pl.multiple_of(members_ref[o] * SEG, SEG)
        dn_ref[:, pl.ds(at, SEG)] = d_normed.astype(BF16)
        scaled = tokens_ref[:, pl.ds(at, SEG)].astype(F32) * inv
        gain_ref[0:1, pl.ds(at, SEG)] += jnp.sum(d_normed * scaled, axis=0, keepdims=True)


def run_back_norm(members, tokens, dz, dx, weights_z, weights_x):
    length = tokens.shape[0]
    row = lambda i, t: (i, 0)
    return pl.pallas_call(
        back_norm,
        grid_spec=pltpu.PrefetchScalarGridSpec(
            num_scalar_prefetch=1,
            grid=(length // GROUP,),
            in_specs=[
                pl.BlockSpec((GROUP, D), row),
                pl.BlockSpec((GROUP, dz.shape[1]), row),
                pl.BlockSpec((GROUP, dx.shape[1]), row),
            ]
            + [resident(w, 2) for w in weights_z + weights_x],
            out_specs=[pl.BlockSpec((GROUP, D), row), pl.BlockSpec((8, D), lambda i, t: (0, 0))],
        ),
        out_shape=[
            jax.ShapeDtypeStruct((length, D), BF16),
            jax.ShapeDtypeStruct((8, D), F32),
        ],
        compiler_params=pltpu.CompilerParams(vmem_limit_bytes=VMEM_LIMIT),
        cost_estimate=busy(18, 24),
        name="back_norm",
    )(members, tokens, dz, dx, *weights_z, *weights_x)


def put_pairs(place_ref, refs, out_ref, g):
    m = len(refs)
    for k, ref in enumerate(refs):
        to = pl.multiple_of((place_ref[0] ^ k) * PAIR, PAIR)
        out_ref[pl.ds(to, PAIR), :] = ref[pl.ds(pl.multiple_of(g * PAIR, PAIR), PAIR), :].astype(F32)


def assemble_z(place_ref, z0, z1, z2, z3, out_ref):
    put_pairs(place_ref, (z0, z1, z2, z3), out_ref, pl.program_id(0))


def assemble_x(place_ref, order_ref, held_ref, a0, a1, a2, a3, b0, b1, b2, b3, out_ref):
    step, last = pl.program_id(0), pl.num_programs(0) - 1
    early, late = (a0, a1, a2, a3), (b0, b1, b2, b3)
    cut = a0.shape[0] // PAIR
    width = last * PAIR - a0.shape[0]
    core = width + 2 * STATE

    @pl.when(step < cut)
    def _():
        put_pairs(place_ref, early, out_ref, step)

    @pl.when((step >= cut) & (step < last))
    def _():
        put_pairs(place_ref, late, out_ref, step - cut)

    @pl.when(step == last)
    def _():
        total = jnp.zeros((2 * STATE, out_ref.shape[1]), F32)
        steps = jnp.zeros((HEADS, out_ref.shape[1]), F32)
        for k, x in enumerate(late):
            total = total + x[width:core].astype(F32)
            steps = steps + nn(order_ref[place_ref[0] ^ k], x[core : core + PAIR])
        out_ref[: 2 * STATE] = total
        out_ref[2 * STATE : 2 * STATE + HEADS] = steps


def run_assemble_z(place, shares, columns):
    m, rows = len(shares), shares[0].shape[1]
    tile = m * PAIR
    return pl.pallas_call(
        assemble_z,
        grid_spec=pltpu.PrefetchScalarGridSpec(
            num_scalar_prefetch=1,
            grid=(DI // tile,),
            in_specs=[resident(s, 2) for s in shares],
            out_specs=pl.BlockSpec((tile, rows), lambda i, t: (i, 0)),
        ),
        out_shape=jax.ShapeDtypeStruct((columns, rows), F32),
        compiler_params=pltpu.CompilerParams(vmem_limit_bytes=VMEM_LIMIT),
        cost_estimate=busy(4, 6),
        name="assemble_z",
    )(place, *shares)


def run_assemble_x(place, order, held, shares_a, shares_b):
    m, rows = len(shares_a), shares_a[0].shape[1]
    tile = m * PAIR
    steps = DI // tile
    return pl.pallas_call(
        assemble_x,
        grid_spec=pltpu.PrefetchScalarGridSpec(
            num_scalar_prefetch=1,
            grid=(steps + 1,),
            in_specs=[resident(order, 2), pl.BlockSpec(memory_space=pl.ANY)]
            + [resident(s, 2) for s in shares_a + shares_b],
            out_specs=pl.BlockSpec((tile, rows), lambda i, t: (i + steps, 0)),
        ),
        out_shape=jax.ShapeDtypeStruct(held.shape, F32),
        input_output_aliases={2: 0},
        compiler_params=pltpu.CompilerParams(vmem_limit_bytes=VMEM_LIMIT),
        cost_estimate=busy(5, 6),
        name="assemble_x",
    )(place, order, held, *shares_a, *shares_b)


def body(
    tokens, norm_gain, w_in, conv_w, conv_b, dt_bias, a_log, d_skip, gate_gain, w_out, cotangent
):
    n, m = lax.axis_size("fsdp"), lax.axis_size("ctx")
    place = lax.axis_index("ctx")
    piece = tokens.shape[1]
    length = piece * m
    blocks = length // GROUP
    pairs = DI // PAIR // m
    width = pairs * PAIR
    heads = 2 * pairs
    rows = w_in.shape[0]
    core_cols = width + 2 * STATE
    head_cols = core_cols + heads
    ring = rows == SEG and (DI // PAIR) // n == m

    def of_pairs(array, axis):
        shape = array.shape
        each = shape[axis] // (pairs * m)
        split = array.reshape(shape[:axis] + (pairs, m, each) + shape[axis + 1 :])
        mine = lax.dynamic_index_in_dim(split, place, axis + 1, False)
        return mine.reshape(shape[:axis] + (pairs * each,) + shape[axis + 1 :])

    all_tokens = lax.all_gather(tokens[0], "ctx", axis=0, tiled=True)
    seed = lax.all_gather(cotangent[0], "ctx", axis=0, tiled=True)

    dt_bias_own, a_log_own, skip_own = (of_pairs(v, 0) for v in (dt_bias, a_log, d_skip))
    a_neg = -jnp.exp(a_log_own)
    heads_in = jnp.broadcast_to(jnp.concatenate([dt_bias_own, a_neg])[:, None], (2 * heads, 128))
    skip_row = jnp.repeat(skip_own, HEADDIM)[None, :]

    columns = w_in.T
    small = jnp.concatenate([norm_gain, gate_gain, conv_b, conv_w.reshape(-1)])
    small_rows = -(-small.shape[0] // rows)
    small = jnp.pad(small, (0, small_rows * rows - small.shape[0])).reshape(small_rows, rows)
    total_cols = core_cols + PAIR
    spare = total_cols - head_cols - small_rows
    block_x = jnp.concatenate(
        [
            of_pairs(columns[DI : 2 * DI], 0),
            columns[2 * DI : 2 * DI + 2 * STATE],
            of_pairs(columns[DI + CONV :], 0),
            small,
            jnp.zeros((spare, rows), BF16),
        ],
        axis=0,
    )
    block_z = of_pairs(columns[:DI], 0)
    if ring:
        me = ring_place(lax.axis_index("fsdp"), n)
        members = ring_member(me + jnp.arange(n), n)
        offsets = (ring_place(jnp.arange(n), n) - me) % n
        block_o = lax.dynamic_slice_in_dim(w_out, place * PAIR, PAIR, 0)
        ring_x, ring_z, ring_o = Gather(block_x, n), Gather(block_z, n), Gather(block_o, n)
        ring_x.hop(heads_in, skip_row)
        for _ in range(n // 2 - 3):
            ring_x.hop()
        ring_z.hop(*ring_x.latest)
        ring_x.hop()
        ring_x.hop()
        ring_z.hop(*ring_x.latest)
        ring_o.hop(*ring_x.latest)
        parts_x = ring_x.parts()
        far_tail = parts_x[n // 2 + 1]
        tails = [p[p.shape[0] - PAIR :] for p in parts_x[: n // 2] + [far_tail] + parts_x[n // 2 + 2 :]]
        tails = jnp.stack(tails)
        tails_ring, tails = tails, tails[offsets]
    else:
        members = jnp.arange(D // SEG)

        def split(whole):
            upper, _ = halves(whole.shape[0])
            parts = [whole[:, o * SEG : (o + 1) * SEG] for o in range(D // SEG)]
            middle = parts[len(parts) // 2]
            return parts[: len(parts) // 2] + [middle[:upper], middle[upper:]] + parts[len(parts) // 2 + 1 :]

        whole_x = lax.all_gather(block_x, "fsdp", axis=1, tiled=True)
        parts_x, parts_z = split(whole_x), split(lax.all_gather(block_z, "fsdp", axis=1, tiled=True))
        w_o = of_pairs(lax.all_gather(w_out, "fsdp", axis=0, tiled=True), 0)
        tails = whole_x[core_cols:].reshape(PAIR, n, rows).transpose(1, 0, 2)
        tails_ring = tails
    members = members.astype(jnp.int32)

    def flatten(tails):
        return tails[:, heads : heads + small_rows].reshape(n, small_rows * rows)

    flat = flatten(tails)
    sizes = (norm_gain.shape[0], gate_gain.shape[0], conv_b.shape[0], KW * conv_w.shape[1])
    cuts = [0]
    for size in sizes:
        cuts.append(cuts[-1] + size)
    norm_ring = flatten(tails_ring)[:, cuts[0] : cuts[1]].reshape(1, D).astype(F32)
    norm_full = flat[:, cuts[0] : cuts[1]].reshape(1, D).astype(F32)
    gate_full = of_pairs(flat[:, cuts[1] : cuts[2]].reshape(1, DI), 1).astype(F32)
    bias_full = flat[:, cuts[2] : cuts[3]].reshape(1, CONV)
    taps_full = flat[:, cuts[3] : cuts[4]].reshape(n, KW, -1).transpose(1, 0, 2).reshape(KW, CONV)
    taps_full = jnp.concatenate([taps_full, bias_full], axis=0)
    taps = jnp.concatenate([of_pairs(taps_full[:, :DI], 1), taps_full[:, DI:]], axis=1)
    taps = jnp.pad(taps.astype(F32), ((0, 8 - KW - 1), (0, 0)))

    normed, proj_x = run_front(members, all_tokens, norm_ring, parts_x)
    if ring:
        ring_z.hop(proj_x)
        ring_o.hop(proj_x)
    act, table, ssd, starts = run_mix_forward(proj_x, taps, heads_in, skip_row, pairs)
    if ring:
        for _ in range(n // 2 - 2):
            ring_o.hop(ssd)
        for _ in range(n // 2 - 3):
            ring_z.hop(ssd)
        parts_z = ring_z.parts()
        w_o = jnp.zeros((n, PAIR, D), BF16)
        where = [members[o] for o in range(n // 2)] + [members[n // 2]] * 2
        where += [members[o] for o in range(n // 2 + 1, n)]
        for at, part in enumerate(ring_o.parts()):
            row = halves(PAIR)[0] if at == n // 2 + 1 else 0
            w_o = lax.dynamic_update_slice(w_o, part[None], (where[at], row, 0))
        w_o = w_o.reshape(width, D)
    proj_z = run_project(normed, parts_z)

    scaled, sums = run_gate_sums(seed, w_o, proj_z, ssd, gate_full)
    sums = ctx_sum(sums, m)
    mixed, dy, d_z, gate_cols = run_gate_back(sums, scaled, proj_z, ssd, act, gate_full)
    d_gate_gain = gate_cols[0]
    d_skip_own = jnp.sum(gate_cols[1].reshape(heads, HEADDIM), axis=1)

    grads_o = tn(mixed, seed).astype(BF16)
    grads_z = tn(d_z, normed).astype(BF16)
    carry = jnp.zeros((pairs, STATE, PAIR), F32)
    halo = jnp.zeros((HALO, core_cols), F32)
    conv_grads, head_grads, top, d_x = 0.0, 0.0, blocks - 1, None
    if ring:
        sum_o = Reduce(lambda o: lax.dynamic_slice_in_dim(grads_o, members[o] * PAIR, PAIR, 0), n)
        sum_z = Reduce(lambda o: grads_z[:, o * SEG : (o + 1) * SEG], n)
        sum_o.hop()
        sum_z.hop()
    for at, span in enumerate((1, 2, 1)):
        if ring and at > 0:
            sum_o.join()
            if at == 1:
                sum_z.join()
            dy, carry = next_hop([sum_o, sum_z] if at == 1 else [sum_o], (dy, carry))
        d_x, conv_part, head_part, carry, halo = run_mix_backward(
            span, top, act, proj_x, taps, heads_in, skip_row, table, starts, dy, carry, halo, d_x
        )
        conv_grads, head_grads = conv_grads + conv_part, head_grads + head_part
        top -= span
    if ring:
        sum_o.join()
        sum_z.join()
        d_x, normed_late = next_hop([sum_z], (d_x, normed), sum_o.right, sum_o.left)
    else:
        normed_late = normed
    head_sums = jnp.sum(head_grads, axis=1)
    d_dt_bias, d_a_log = head_sums[:heads], head_sums[heads:] * a_neg
    grads_x = tn(d_x, normed_late).astype(BF16)

    def spread_pairs(mine):
        shape = mine.shape[:-1]
        whole = jnp.zeros(shape + (pairs, m, mine.shape[-1] // pairs), F32)
        whole = lax.dynamic_update_index_in_dim(
            whole, mine.reshape(shape + (pairs, -1)), place, len(shape) + 1
        )
        return whole.reshape(shape + (-1,))

    d_conv = jnp.concatenate(
        [spread_pairs(conv_grads[: KW + 1, :width]), conv_grads[: KW + 1, width:]], axis=1
    )
    by_member = d_conv.reshape(KW + 1, n, -1)
    small_grads = jnp.concatenate(
        [
            jnp.zeros((n, rows), F32),
            spread_pairs(d_gate_gain).reshape(n, -1),
            by_member[KW],
            by_member[:KW].transpose(1, 0, 2).reshape(n, -1),
        ],
        axis=1,
    )
    small_grads = jnp.pad(small_grads, ((0, 0), (0, small_rows * rows - small_grads.shape[1])))
    per_head = jnp.concatenate([d_dt_bias, d_a_log, d_skip_own])
    per_head = jnp.pad(per_head, (0, rows - per_head.shape[0]))
    small_grads = jnp.concatenate(
        [small_grads.reshape(n, small_rows, rows), jnp.broadcast_to(per_head, (n, 1, rows))], axis=1
    )

    def with_small(chunk, extra):
        return chunk.astype(F32) + jnp.pad(extra, ((chunk.shape[0] - PAIR + heads, spare - 1), (0, 0)))

    mixed_late, d_x_late = mixed, d_x
    if ring:
        small_ring = small_grads[members]
        cut = halves(total_cols)[0]
        sum_a = Reduce(lambda o: grads_x[:cut, o * SEG : (o + 1) * SEG], n)
        sum_b = Reduce(
            lambda o: with_small(grads_x[cut:, o * SEG : (o + 1) * SEG], small_ring[o]), n
        )
        sum_z.join()
        d_x_late = next_hop([sum_a, sum_b, sum_o], d_x, sum_z.right, sum_z.left)
    d_normed, d_gain = run_back_norm(members, all_tokens, d_z, d_x_late, parts_z, parts_x)
    if ring:
        sum_a.join()
        sum_b.join()
        part_o = sum_o.join().astype(BF16)
        d_normed, d_gain, mixed_late, part_o = next_hop(
            [sum_a, sum_b], (d_normed, d_gain, mixed, part_o), sum_z.right, sum_z.left
        )
    d_own = CtxReduce(d_normed.reshape(m, piece, D), m)
    d_own.middle()
    d_own.send_far()
    gain_sum = axis_sum(d_gain[0:1], "ctx", m)
    branch = nn(mixed_late, w_o).astype(BF16)
    if ring:
        sum_a.join()
        sum_b.join()
        branch, d_own.far, gain_sum, part_o = next_hop(
            [sum_a, sum_b, sum_z], (branch, d_own.far, gain_sum, part_o)
        )
    branch_own = CtxReduce(branch.reshape(m, piece, D), m)
    branch_own.middle()
    branch_own.send_far()
    gain_sum = axis_sum(gain_sum, "fsdp", n)
    own = tokens[0].astype(F32)
    inv = lax.rsqrt(jnp.mean(own * own, axis=-1, keepdims=True) + EPS)
    d_direct = d_own.total() * norm_full
    along = jnp.mean(d_direct * own, axis=-1, keepdims=True)
    grad_tokens = (cotangent[0].astype(F32) + d_direct * inv - own * (inv * inv * inv * along))[None]
    if ring:
        part_z = sum_z.join().astype(BF16)
        for at in range(n // 2 - 3):
            sum_a.join()
            sum_b.join()
            branch_own.far, gain_sum, part_o, part_z = next_hop(
                [sum_a, sum_b], (branch_own.far, gain_sum, part_o, part_z), grad_tokens
            )
        other_o, other_z = far_share(part_o, m), far_share(part_z, m)
    output = (tokens[0].astype(F32) + branch_own.total()).astype(BF16)[None]
    grad_gain = lax.dynamic_slice_in_dim(gain_sum[0], lax.axis_index("fsdp") * rows, rows, 0)
    place_ref = place.reshape(1).astype(jnp.int32)
    if ring:
        part_a, part_b = sum_a.join().astype(BF16), sum_b.join().astype(BF16)
        part_a, part_b, other_o, other_z = barrier(
            (part_a, part_b, other_o, other_z), output, grad_gain
        )
        other_a, other_b = far_share(part_a, m), far_share(part_b, m)
        shares_o, shares_z = near_share(part_o, other_o, m), near_share(part_z, other_z, m)
        held = run_assemble_z(place_ref, shares_z, w_in.shape[1])
        grad_w_out = jnp.zeros((m, PAIR, D), F32)
        for k in range(m):
            grad_w_out = lax.dynamic_update_slice(
                grad_w_out, shares_o[k].astype(F32)[None], (place ^ k, 0, 0)
            )
        grad_w_out = grad_w_out.reshape(w_out.shape)
        part_a, part_b, other_a, other_b, held, grad_w_out = barrier(
            (part_a, part_b, other_a, other_b, held, grad_w_out)
        )
        shares_x = [near_share(part_a, other_a, m), near_share(part_b, other_b, m)]
    else:
        part_z = lax.psum_scatter(grads_z.astype(F32), "fsdp", scatter_dimension=1, tiled=True)
        extra = small_grads.transpose(1, 0, 2).reshape(small_rows + 1, D)
        part_x = lax.psum_scatter(with_small(grads_x, extra), "fsdp", scatter_dimension=1, tiled=True)
        whole_o = jnp.zeros((pairs, m, PAIR, D), F32)
        whole_o = lax.dynamic_update_index_in_dim(
            whole_o, grads_o.astype(F32).reshape(pairs, PAIR, D), place, 1
        )
        grad_w_out = lax.psum_scatter(whole_o.reshape(DI, D), "fsdp", scatter_dimension=0, tiled=True)
        grad_w_out = lax.psum(grad_w_out, "ctx")
        held = run_assemble_z(place_ref, ctx_share(part_z.astype(BF16), m), w_in.shape[1])
        cut = halves(total_cols)[0]
        shares_x = [ctx_share(part.astype(BF16), m) for part in (part_x[:cut], part_x[cut:])]

    order = np.zeros((m, HEADS, PAIR), np.float32)
    for member in range(m):
        for h in range(heads):
            order[member, (h // 2) * 2 * m + 2 * member + h % 2, h] = 1.0
    grad_w_in = run_assemble_x(place_ref, jnp.asarray(order, BF16), held, *shares_x).T
    first = head_cols - cut
    tail = jnp.stack([share[first : first + small_rows + 1] for share in shares_x[1]]).astype(F32)
    summed = jnp.sum(tail[:, :small_rows], axis=0).reshape(-1)
    ends = tail[:, small_rows, : 3 * heads]
    per_head = jnp.zeros((m, 3 * heads), F32)
    for k in range(m):
        per_head = lax.dynamic_update_slice(per_head, ends[k : k + 1], (place ^ k, 0))
    per_head = per_head.reshape(m, 3, pairs, 2).transpose(1, 2, 0, 3).reshape(3, HEADS)
    return (
        output,
        grad_tokens,
        grad_gain,
        grad_w_in,
        summed[cuts[3] : cuts[4]].reshape(KW, -1),
        summed[cuts[2] : cuts[3]],
        per_head[0],
        per_head[1],
        per_head[2],
        summed[cuts[1] : cuts[2]],
        grad_w_out,
    )


def solution(mesh):
    in_specs = (
        P("fsdp", "ctx", None),
        P("fsdp"),
        P("fsdp", None),
        P(None, "fsdp"),
        P("fsdp"),
        P(),
        P(),
        P(),
        P("fsdp"),
        P("fsdp", None),
        P("fsdp", "ctx", None),
    )
    out_specs = (
        P("fsdp", "ctx", None),
        P("fsdp", "ctx", None),
        P("fsdp"),
        P("fsdp", None),
        P(None, "fsdp"),
        P("fsdp"),
        P(),
        P(),
        P(),
        P("fsdp"),
        P("fsdp", None),
    )
    return jax.shard_map(body, mesh=mesh, in_specs=in_specs, out_specs=out_specs, check_vma=False)
```

```python
import jax
import jax.numpy as jnp
import numpy as np
from jax import lax
from jax.experimental import pallas as pl
from jax.experimental.pallas import tpu as pltpu
from jax.sharding import PartitionSpec as P

D = 2048
HEADS = 64
HEADDIM = 64
STATE = 128
KW = 4
GROUP = 256
DI = HEADS * HEADDIM
CONV = DI + 2 * STATE
PAIR = 2 * HEADDIM
EPS = 1e-05
SEG = 256
HALO = 8
SMALL = 32
VMEM_LIMIT = 56 * 1024 * 1024
F32 = jnp.float32
BF16 = jnp.bfloat16


def ring_place(index, n):
    return jnp.where(index % 2 == 0, index // 2, n - 1 - index // 2)


def ring_member(place, n):
    place = place % n
    return jnp.where(place < n // 2, 2 * place, 2 * (n - 1 - place) + 1)


def ring_routes(n):
    order = [2 * p if p < n // 2 else 2 * (n - 1 - p) + 1 for p in range(n)]
    forward = [(order[p], order[(p + 1) % n]) for p in range(n)]
    return forward, [(b, a) for a, b in forward]


def send(block, route):
    return lax.ppermute(block, "fsdp", route)


def after(value, *earlier):
    return lax.optimization_barrier((value, *earlier))[0]


def halves(rows):
    upper = -(-rows // 256) * 128 if rows >= 512 else rows // 2
    return upper, rows - upper


class Gather:
    def __init__(self, block, n):
        self.forward, self.backward = ring_routes(n)
        self.block, self.n = block, n
        self.latest = (block, block)
        self.ahead, self.behind = [], []

    def load(self):
        right, left = self.latest
        if len(self.ahead) == self.n // 2 - 1:
            upper, _ = halves(self.block.shape[0])
            return right[:upper], left[upper:]
        return right, left

    def fire(self, right, left):
        last = len(self.ahead) == self.n // 2 - 1
        self.latest = send(right, self.forward), send(left, self.backward)
        if not last:
            self.behind.insert(0, self.latest[0])
            self.ahead.append(self.latest[1])

    def parts(self):
        return [self.block] + self.ahead + list(self.latest) + self.behind


class Reduce:
    def __init__(self, chunk, n):
        self.forward, self.backward = ring_routes(n)
        self.chunk, self.n, self.step = chunk, n, n // 2
        first = chunk(n // 2).astype(BF16)
        self.upper, _ = halves(first.shape[0])
        self.right, self.left = first[: self.upper], first[self.upper :]

    def load(self):
        return self.right, self.left

    def fire(self, right, left):
        self.latest = send(right, self.forward), send(left, self.backward)
        self.step -= 1

    def join(self):
        right, left = (part.astype(F32) for part in self.latest)
        if self.step == 0:
            return self.chunk(0).astype(F32) + right + left
        own_right = self.chunk(self.step).astype(F32)
        own_left = self.chunk(self.n - self.step).astype(F32)
        cut = self.upper
        if self.step == self.n // 2 - 1:
            right = jnp.concatenate([own_right[:cut] + right, own_right[cut:]], axis=0)
            left = jnp.concatenate([own_left[:cut], own_left[cut:] + left], axis=0)
        else:
            right, left = own_right + right, own_left + left
        self.right, self.left = right.astype(BF16), left.astype(BF16)


def barrier(value, *earlier):
    return lax.optimization_barrier((value, earlier))[0]


def next_hop(rings, inputs, *earlier):
    loads, inputs = barrier(([ring.load() for ring in rings], inputs), *earlier)
    for ring, load in zip(rings, loads):
        ring.fire(*load)
    return inputs


def arrivals(*rings):
    return sum((ring.latest for ring in rings), ())


def ctx_route(m, flip):
    return [(i, i ^ flip) for i in range(m)]


def far_share(block, m):
    return lax.ppermute(block, "ctx", ctx_route(m, 2))


def near_share(block, other, m):
    near = lax.ppermute(block, "ctx", ctx_route(m, 1))
    far = lax.ppermute(other, "ctx", ctx_route(m, 1))
    return [block, near, other, far]


def ctx_share(block, m):
    return near_share(block, far_share(block, m), m)


class CtxReduce:
    def __init__(self, share, m):
        self.m, place = m, lax.axis_index("ctx")
        self.core, self.across = place % 2, place // 2
        split = share.reshape((m // 2, 2) + share.shape[1:])
        self.kept = lax.dynamic_index_in_dim(split, self.core, 1, False)
        sent = lax.dynamic_index_in_dim(split, 1 - self.core, 1, False)
        self.near = lax.ppermute(sent, "ctx", ctx_route(m, 1))

    def middle(self):
        self.both = self.kept.astype(F32) + self.near.astype(F32)
        self.sent = lax.dynamic_index_in_dim(self.both, 1 - self.across, 0, False).astype(BF16)

    def send_far(self):
        self.far = lax.ppermute(self.sent, "ctx", ctx_route(self.m, 2))

    def total(self):
        return lax.dynamic_index_in_dim(self.both, self.across, 0, False) + self.far.astype(F32)


def ctx_sum(values, m):
    for flip in (1, 2):
        values = values + lax.ppermute(values, "ctx", ctx_route(m, flip))
    return values


def nt(a, b):
    return lax.dot_general(a, b, (((1,), (1,)), ((), ())), preferred_element_type=F32)


def nn(a, b):
    return lax.dot_general(a, b, (((1,), (0,)), ((), ())), preferred_element_type=F32)


def tn(a, b):
    return lax.dot_general(a, b, (((0,), (0,)), ((), ())), preferred_element_type=F32)


def lanes(shape):
    return lax.broadcasted_iota(jnp.int32, shape, len(shape) - 1)


def busy(us, megabytes):
    return pl.CostEstimate(
        flops=int(us * 1e9), transcendentals=0, bytes_accessed=int(megabytes * 1e6)
    )


def softplus(v):
    return jnp.maximum(v, 0.0) + jnp.log1p(jnp.exp(-jnp.abs(v)))


def sigmoid(v):
    return 1.0 / (1.0 + jnp.exp(-v))


def ones_where(keep):
    row = lax.broadcasted_iota(jnp.int32, (GROUP, GROUP), 0)
    col = lax.broadcasted_iota(jnp.int32, (GROUP, GROUP), 1)
    return keep(row, col)


def exact(a, b):
    return lax.dot_general(
        a, b, (((1,), (0,)), ((), ())), preferred_element_type=F32, precision=lax.Precision.HIGHEST
    )


def tiles(width):
    return [slice(at, at + PAIR) for at in range(0, width, PAIR)]


def conv_tile(extended, taps_ref, cols):
    total = taps_ref[KW : KW + 1, cols]
    for k in range(KW):
        at = HALO - KW + 1 + k
        total = total + taps_ref[k : k + 1, cols] * extended[at : at + GROUP]
    return total


def by_segments(weights):
    n = D // SEG
    places = list(range(n // 2)) + [n // 2] * 2 + list(range(n // 2 + 1, n))
    at = [0] * len(places)
    at[n // 2 + 1] = weights[n // 2].shape[0]
    return list(zip(places, at, weights))


def project_into(out_ref, normed_ref, weights, total):
    whole = None
    for o, at, w in by_segments(weights):
        part = nt(normed_ref[:, o * SEG : (o + 1) * SEG], w[...])
        if o == D // SEG // 2:
            total[:, at : at + w.shape[0]] = part
        else:
            whole = part if whole is None else whole + part
    out_ref[...] = (whole + total[...]).astype(BF16)


def pack(
    place_ref, columns_ref, out_ref, small_ref, x_ref, z_ref, o_ref, steps, rows, sems,
):
    place = place_ref[0]
    pairs, m = z_ref.shape[0] // PAIR, out_ref.shape[0] // PAIR
    core = pairs * PAIR + 2 * STATE
    copies = [
        (columns_ref.at[pl.ds(DI + CONV, HEADS)], steps),
        (columns_ref.at[pl.ds(2 * DI, 2 * STATE)], x_ref.at[pl.ds(pairs * PAIR, 2 * STATE)]),
        (out_ref.at[pl.ds(pl.multiple_of(place * PAIR, PAIR), PAIR)], o_ref),
    ]
    for g in range(pairs):
        here = pl.ds(g * PAIR, PAIR)
        for start, ref in ((DI, x_ref), (0, z_ref)):
            at = pl.multiple_of(start + (g * m + place) * PAIR, PAIR)
            copies.append((columns_ref.at[pl.ds(at, PAIR)], ref.at[here]))
    copies = [pltpu.make_async_copy(*pair, sems.at[k]) for k, pair in enumerate(copies)]
    for copy in copies:
        copy.start()
    rows[...] = jnp.zeros_like(rows)
    rows[SMALL : SMALL + small_ref.shape[0], :] = small_ref[...].astype(F32)
    copies[0].wait()
    want = lax.broadcasted_iota(jnp.int32, (2 * pairs, HEADS), 0)
    have = lax.broadcasted_iota(jnp.int32, (2 * pairs, HEADS), 1)
    head = (want % pairs) * 2 * m + 2 * place + want // pairs
    rows[: 2 * pairs, :] = nn((have == head).astype(BF16), steps[...])
    x_ref[core : core + PAIR, :] = rows[...].astype(BF16)
    for copy in copies[1:]:
        copy.wait()


def run_pack(place, columns, w_out, small, pairs):
    rows = columns.shape[1]
    core = pairs * PAIR + 2 * STATE
    anywhere = pl.BlockSpec(memory_space=pl.ANY)
    shapes = [(core + PAIR, rows), (pairs * PAIR, rows), (PAIR, D)]
    return pl.pallas_call(
        pack,
        grid_spec=pltpu.PrefetchScalarGridSpec(
            num_scalar_prefetch=1,
            grid=(1,),
            in_specs=[anywhere, anywhere, pl.BlockSpec(small.shape, lambda i, t: (0, 0))],
            out_specs=[pl.BlockSpec(shape, lambda i, t: (0, 0)) for shape in shapes],
            scratch_shapes=[
                pltpu.VMEM((HEADS, rows), BF16),
                pltpu.VMEM((PAIR, rows), F32),
                pltpu.SemaphoreType.DMA((2 * pairs + 3,)),
            ],
        ),
        out_shape=[jax.ShapeDtypeStruct(shape, BF16) for shape in shapes],
        compiler_params=pltpu.CompilerParams(vmem_limit_bytes=VMEM_LIMIT),
        name="pack",
    )(place, columns, w_out, small)


def collect(members_ref, *refs):
    out_ref = refs[-1]
    for o, ref in enumerate(refs[:-1]):
        out_ref[members_ref[o]] = ref[...].astype(F32)


def run_collect(members, parts):
    n = len(parts) - 1
    lasts = parts[: n // 2] + parts[n // 2 + 1 :]
    at = lambda part: (part.shape[0] - PAIR + SMALL) // 32
    return pl.pallas_call(
        collect,
        grid_spec=pltpu.PrefetchScalarGridSpec(
            num_scalar_prefetch=1,
            grid=(1,),
            in_specs=[pl.BlockSpec((32, SEG), lambda i, t, k=at(p): (k, 0)) for p in lasts],
            out_specs=pl.BlockSpec((n, 32, SEG), lambda i, t: (0, 0, 0)),
        ),
        out_shape=jax.ShapeDtypeStruct((n, 32, SEG), F32),
        compiler_params=pltpu.CompilerParams(vmem_limit_bytes=VMEM_LIMIT),
        name="collect",
    )(members, *lasts)


def front(members_ref, tokens_ref, *refs):
    weights, (normed_ref, proj_ref, total) = refs[:-3], refs[-3:]
    tokens = tokens_ref[...].astype(F32)
    inv = lax.rsqrt(jnp.mean(tokens * tokens, axis=-1, keepdims=True) + EPS)
    for o in range(D // SEG):
        at = pl.multiple_of(members_ref[o] * SEG, SEG)
        cols = slice(o * SEG, (o + 1) * SEG)
        last = weights[o if o < D // SEG // 2 else o + 1]
        row = last.shape[0] - PAIR + SMALL
        gain = last[row : row + 16, :].astype(F32)[0:1]
        part = tokens_ref[:, pl.ds(at, SEG)].astype(F32) * inv * gain
        normed_ref[:, cols] = part.astype(BF16)
    project_into(proj_ref, normed_ref, weights, total)


def resident(array, grid_args=1):
    zeros = (0,) * array.ndim
    if grid_args == 2:
        return pl.BlockSpec(array.shape, lambda i, t: zeros, pipeline_mode=pl.Buffered(1))
    return pl.BlockSpec(array.shape, lambda i: zeros, pipeline_mode=pl.Buffered(1))


def run_front(members, tokens, weights):
    length, cols = tokens.shape[0], weights[0].shape[0]
    return pl.pallas_call(
        front,
        grid_spec=pltpu.PrefetchScalarGridSpec(
            num_scalar_prefetch=1,
            grid=(length // GROUP,),
            in_specs=[
                pl.BlockSpec((GROUP, D), lambda i, t: (i, 0)),
            ]
            + [resident(w, 2) for w in weights],
            out_specs=[
                pl.BlockSpec((GROUP, D), lambda i, t: (i, 0)),
                pl.BlockSpec((GROUP, cols), lambda i, t: (i, 0)),
            ],
            scratch_shapes=[pltpu.VMEM((GROUP, cols), F32)],
        ),
        out_shape=[
            jax.ShapeDtypeStruct((length, D), BF16),
            jax.ShapeDtypeStruct((length, cols), BF16),
        ],
        compiler_params=pltpu.CompilerParams(vmem_limit_bytes=VMEM_LIMIT),
        cost_estimate=busy(12, 18),
        name="front",
    )(members, tokens, *weights)


def project(normed_ref, *refs):
    project_into(refs[-2], normed_ref, refs[:-2], refs[-1])


def run_project(normed, weights):
    length, cols = normed.shape[0], weights[0].shape[0]
    return pl.pallas_call(
        project,
        grid=(length // GROUP,),
        in_specs=[pl.BlockSpec((GROUP, D), lambda i: (i, 0))] + [resident(w) for w in weights],
        out_specs=pl.BlockSpec((GROUP, cols), lambda i: (i, 0)),
        out_shape=jax.ShapeDtypeStruct((length, cols), BF16),
        scratch_shapes=[pltpu.VMEM((GROUP, cols), F32)],
        compiler_params=pltpu.CompilerParams(vmem_limit_bytes=VMEM_LIMIT),
        cost_estimate=busy(8, 10),
        name="project",
    )(normed, *weights)


def spread_rows(ref, index, rows):
    count = rows.shape[0]
    ref[pl.ds(index, count), :] = rows[:, :128]
    ref[pl.ds(ref.shape[0] // 2 + index, count), :] = rows[:, 128:]


def all_rows(stack):
    half = stack.shape[0] // 2
    return jnp.concatenate([stack[:half], stack[half:]], axis=1)


def pair_rows(ref, g, pairs):
    half = 8 * pairs
    return jnp.concatenate(
        [ref[pl.ds(g, 8, stride=pairs), :], ref[pl.ds(half + g, 8, stride=pairs), :]], axis=1
    )


def high_low(v):
    high = v.astype(BF16)
    return high, (v - high.astype(F32)).astype(BF16)


def tri_units(back):
    units = []
    for r in range(GROUP // 64):
        for t in range(GROUP // 128):
            if (t >= r // 2) if back else (t <= r // 2):
                units.append((slice(64 * r, 64 * r + 64), slice(128 * t, 128 * t + 128), t == r // 2))
    return units


def diagonal(keep):
    row = lax.broadcasted_iota(jnp.int32, (128, 128), 0)
    col = lax.broadcasted_iota(jnp.int32, (128, 128), 1)
    return jnp.where(keep(row, col), 0.0, -1e30)


def mix_forward(
    proj_ref, taps_ref, heads_ref, skip_ref, act_ref, table_ref, y_ref, start_ref,
    state, halo, gram, bias, scores,
):
    pairs = state.shape[0]
    heads, width = 2 * pairs, pairs * PAIR
    core = width + 2 * STATE

    @pl.when(pl.program_id(0) == 0)
    def _():
        state[...] = jnp.zeros_like(state)
        halo[...] = jnp.zeros_like(halo)
        scores[...] = jnp.zeros_like(scores)
        bias[...] = diagonal(lambda row, col: row >= col)

    def activate(cols):
        current = proj_ref[:, cols].astype(F32)
        conv = conv_tile(jnp.concatenate([halo[:, cols], current], axis=0), taps_ref, cols)
        halo[:, cols] = current[GROUP - HALO :]
        act = (conv * sigmoid(conv)).astype(BF16)
        act_ref[:, cols] = act
        return act

    bs = activate(slice(width, width + STATE))
    cs = activate(slice(width + STATE, core))
    raw = proj_ref[:, core : core + PAIR].astype(F32).T[:heads]
    dt = softplus(raw + heads_ref[:heads, 0:1])
    upto = ones_where(lambda row, col: row <= col).astype(F32)
    cum = exact(dt * heads_ref[heads:, 0:1], upto)
    last = cum[:, GROUP - 1 :]
    table = jnp.concatenate([cum, dt, jnp.exp(last - cum) * dt, jnp.exp(cum)], axis=0)
    spread_rows(table_ref.at[0], 0, table)
    gram[...] = nt(cs, bs)
    bs_t = bs.astype(F32).T

    def one(g, unused):
        cols = pl.ds(pl.multiple_of(g * PAIR, PAIR), PAIR)
        rows = pair_rows(table_ref.at[0], g, pairs)
        turned = rows.T
        x = activate(cols)
        first = lanes(x.shape) < HEADDIM
        start = state[g]
        start_ref[0, g] = start
        inner = nn(cs, start.astype(BF16))
        parts, locals_ = [], []
        for e in range(2):
            for at, to, on in tri_units(False):
                differ = turned[at, e : e + 1] - rows[e : e + 1, to]
                if on:
                    differ = differ + bias[at.start % 128 : at.start % 128 + 64, :]
                decay = jnp.exp(differ)
                scores[e, at, to] = (gram[at, to] * decay * rows[2 + e : 3 + e, to]).astype(BF16)
            parts.append(nn(scores[e], x))
            locals_.append(nn((bs_t * rows[4 + e : 5 + e, :]).astype(BF16), x))
        grow = jnp.where(first, turned[:, 6:7], turned[:, 7:8])
        y_ref[:, cols] = (
            jnp.where(first, parts[0], parts[1]) + grow * inner + skip_ref[:, cols] * x.astype(F32)
        )
        shrink = jnp.where(first[:1], rows[6:7, GROUP - 1 :], rows[7:8, GROUP - 1 :])
        state[g] = shrink * start + jnp.where(first[:STATE], locals_[0], locals_[1])
        return unused

    lax.fori_loop(0, pairs, one, 0, unroll=2)


def run_mix_forward(proj, taps, heads_in, skip, pairs):
    length = proj.shape[0]
    blocks, width = length // GROUP, pairs * PAIR
    core = width + 2 * STATE
    whole = lambda i: (0, 0)
    return pl.pallas_call(
        mix_forward,
        grid=(blocks,),
        in_specs=[
            pl.BlockSpec((GROUP, proj.shape[1]), lambda i: (i, 0)),
            pl.BlockSpec(taps.shape, whole),
            pl.BlockSpec(heads_in.shape, whole),
            pl.BlockSpec(skip.shape, whole),
        ],
        out_specs=[
            pl.BlockSpec((GROUP, core), lambda i: (i, 0)),
            pl.BlockSpec((1, 16 * pairs, 128), lambda i: (i, 0, 0)),
            pl.BlockSpec((GROUP, width), lambda i: (i, 0)),
            pl.BlockSpec((1, pairs, STATE, PAIR), lambda i: (i, 0, 0, 0)),
        ],
        out_shape=[
            jax.ShapeDtypeStruct((length, core), BF16),
            jax.ShapeDtypeStruct((blocks, 16 * pairs, 128), F32),
            jax.ShapeDtypeStruct((length, width), F32),
            jax.ShapeDtypeStruct((blocks, pairs, STATE, PAIR), F32),
        ],
        scratch_shapes=[
            pltpu.VMEM((pairs, STATE, PAIR), F32),
            pltpu.VMEM((HALO, core), F32),
            pltpu.VMEM((GROUP, GROUP), F32),
            pltpu.VMEM((128, 128), F32),
            pltpu.VMEM((2, GROUP, GROUP), BF16),
        ],
        compiler_params=pltpu.CompilerParams(vmem_limit_bytes=VMEM_LIMIT),
        cost_estimate=busy(18, 15),
        name="mix_forward",
    )(proj, taps, heads_in, skip)


def mix_backward(
    top, act_ref, proj_ref, prev_ref, taps_ref, heads_ref, skip_ref, table_ref, start_ref, dy_ref,
    carry_in, halo_in, held_ref, dx_ref, grads_ref, dheads_ref, carried, halo,
    gram, dgram, bias, d_scores, scores, db, dc, found, ends,
):
    pairs = carried.shape[0]
    heads, width = 2 * pairs, pairs * PAIR
    core = width + 2 * STATE
    step = pl.program_id(0)

    @pl.when(step == 0)
    def _():
        carried[...] = carry_in[...]
        halo[...] = halo_in[...]
        grads_ref[...] = jnp.zeros_like(grads_ref)
        dheads_ref[...] = jnp.zeros_like(dheads_ref)
        scores[...] = jnp.zeros_like(scores)
        bias[...] = diagonal(lambda row, col: row <= col)

    has_prev = jnp.where(top - step > 0, 1.0, 0.0)
    bs, cs = act_ref[:, width : width + STATE], act_ref[:, width + STATE : core]
    bs_float = bs.astype(F32)
    cs_t = cs.astype(F32).T.astype(BF16)
    gram[...] = nt(bs, cs)
    for ref in (dgram, db, dc):
        ref[...] = jnp.zeros_like(ref)

    def conv_back(d_act, cols):
        before = prev_ref[:, cols].astype(F32)[prev_ref.shape[0] - HALO :] * has_prev
        extended = jnp.concatenate([before, proj_ref[:, cols].astype(F32)], axis=0)
        conv = conv_tile(extended, taps_ref, cols)
        sig = sigmoid(conv)
        d_conv = d_act * (sig * (1.0 + conv * (1.0 - sig)))
        onward = jnp.concatenate([d_conv, halo[:, cols]], axis=0)
        d_in = taps_ref[KW - 1 : KW, cols] * d_conv
        for k in range(KW - 1):
            at = KW - 1 - k
            d_in = d_in + taps_ref[k : k + 1, cols] * onward[at : at + GROUP]
        dx_ref[:, cols] = d_in.astype(BF16)
        sums = []
        for k in range(KW):
            at = HALO - KW + 1 + k
            sums.append(jnp.sum(d_conv * extended[at : at + GROUP], axis=0, keepdims=True))
        sums.append(jnp.sum(d_conv, axis=0, keepdims=True))
        sums.append(jnp.zeros((8 - KW - 1, sums[0].shape[1]), F32))
        grads_ref[:, cols] += jnp.concatenate(sums, axis=0)
        halo[:, cols] = d_conv[:HALO]

    def one(g, unused):
        cols = pl.ds(pl.multiple_of(g * PAIR, PAIR), PAIR)
        rows = pair_rows(table_ref.at[0], g, pairs)
        turned = rows.T
        x, dy = act_ref[:, cols], dy_ref[:, cols]
        first = lanes(x.shape) < HEADDIM
        dy_float = dy.astype(F32)
        start, grad = start_ref[0, g], carried[g]
        start_low, grad_low = start.astype(BF16), grad.astype(BF16)
        inner = nn(cs, start_low)
        grow = jnp.where(first, turned[:, 6:7], turned[:, 7:8])
        d_inner = (dy_float * grow).astype(BF16)
        dc[...] += nt(d_inner, start_low)
        touched = dy_float * inner
        held = jnp.sum(grad * start, axis=0, keepdims=True)
        zero = jnp.zeros_like(x)
        reach = nn(bs, grad_low)
        sent = x.astype(F32) * jnp.where(first, turned[:, 4:5], turned[:, 5:6])
        for half in high_low(sent):
            db[...] += nt(half, grad_low)
        parts, sums_j, linked = [], [], []
        for e in range(2):
            own = first if e == 0 else jnp.logical_not(first)
            d_scores[e] = nt(jnp.where(own, x, zero), dy)
            linked_i, linked_j = {}, {}
            for at, to, on in tri_units(True):
                dt_col = turned[at, 2 + e : 3 + e]
                differ = rows[e : e + 1, to] - turned[at, e : e + 1]
                if on:
                    differ = differ + bias[at.start % 128 : at.start % 128 + 64, :]
                decay = jnp.exp(differ)
                grown = gram[at, to] * decay
                d_score = d_scores[e, at, to]
                score = grown * dt_col
                scores[e, at, to] = score.astype(BF16)
                dgram[at, to] += d_score * decay * dt_col
                along_i = d_score * grown
                along_j = jnp.sum(d_score * score, axis=0, keepdims=True)
                key_i, key_j = at.start, to.start
                linked_i[key_i] = along_i if key_i not in linked_i else linked_i[key_i] + along_i
                linked_j[key_j] = along_j if key_j not in linked_j else linked_j[key_j] + along_j
            sums_j.append(jnp.concatenate([linked_j[k] for k in sorted(linked_j)], axis=1))
            linked.append(jnp.concatenate([linked_i[k] for k in sorted(linked_i)], axis=0))
            tail_col = turned[:, 4 + e : 5 + e]
            parts.append(nn(scores[e], dy) + nn((bs_float * tail_col).astype(BF16), grad_low))
        pick = lax.broadcasted_iota(jnp.int32, (8, 2 * PAIR), 0)
        lane = lanes((8, 2 * PAIR))
        by_head = (pick == lane // HEADDIM).astype(BF16)
        by_pair = (pick == 4 + lane // PAIR).astype(BF16)
        kept = jnp.zeros((8, GROUP), F32)
        for sums, select in (
            ((x.astype(F32) * reach, touched), by_head),
            (linked, by_pair),
        ):
            for half in high_low(jnp.concatenate(sums, axis=1)):
                kept = kept + nt(select, half)
        kept = jnp.concatenate([kept[:6]] + sums_j, axis=0)
        found[pl.ds(g, 8, stride=pairs), :] = kept[:, :128]
        found[pl.ds(8 * pairs + g, 8, stride=pairs), :] = kept[:, 128:]
        ends[pl.ds(g, 2, stride=pairs), :] = jnp.concatenate(
            [jnp.where(first[:1], held, 0.0), jnp.where(first[:1], 0.0, held)], axis=0
        )
        conv_back(jnp.where(first, parts[0], parts[1]) + skip_ref[:, cols] * dy_float, cols)
        shrink = jnp.where(first[:1], rows[6:7, GROUP - 1 :], rows[7:8, GROUP - 1 :])
        carried[g] = shrink * grad + nn(cs_t, d_inner)
        return unused

    lax.fori_loop(0, pairs, one, 0, unroll=2)
    low = dgram[...].astype(BF16)
    conv_back(db[...] + nn(low, cs), slice(width, width + STATE))
    conv_back(dc[...] + tn(low, bs), slice(width + STATE, core))

    rows, sums = all_rows(table_ref[0]), all_rows(found[...])
    d_tail, touched, sum_i, sum_j = (sums[k * heads : (k + 1) * heads] for k in range(4))
    cum, dt, tail, growth = (rows[k * heads : (k + 1) * heads] for k in range(4))
    a_neg = heads_ref[heads:, 0:1]
    tail_log = d_tail * tail
    d_last = jnp.sum(tail_log, axis=1, keepdims=True)
    d_last = d_last + jnp.sum(ends[...], axis=1, keepdims=True) * growth[:, GROUP - 1 :]
    d_cum = touched * growth - tail_log + sum_j - dt * sum_i
    d_cum = d_cum + jnp.where(lanes(d_cum.shape) == GROUP - 1, d_last, 0.0)
    d_rate = exact(d_cum, ones_where(lambda row, col: row >= col).astype(F32))
    raw = proj_ref[:, core : core + PAIR].astype(F32).T[:heads]
    d_step = d_tail * jnp.exp(cum[:, GROUP - 1 :] - cum) + sum_i
    d_dt = (d_step + d_rate * a_neg) * sigmoid(raw + heads_ref[:heads, 0:1])
    dheads_ref[:heads, :] += d_dt
    dheads_ref[heads:, :] += d_rate * dt
    filled = jnp.concatenate([d_dt, jnp.zeros((PAIR - heads, GROUP), F32)], axis=0)
    dx_ref[:, core : core + PAIR] = filled.T.astype(BF16)


def run_mix_backward(span, top, act, proj, taps, heads_in, skip, table, starts, dy, carry, halo, held):
    pairs = carry.shape[0]
    heads, width = 2 * pairs, pairs * PAIR
    core = width + 2 * STATE
    whole = lambda i: (0, 0)
    block = lambda i: (top - i, 0)
    before = GROUP // 16
    return pl.pallas_call(
        lambda *refs: mix_backward(top, *refs),
        grid=(span,),
        in_specs=[
            pl.BlockSpec((GROUP, core), block),
            pl.BlockSpec((GROUP, proj.shape[1]), block),
            pl.BlockSpec((16, proj.shape[1]), lambda i: (jnp.maximum((top - i) * before - 1, 0), 0)),
            pl.BlockSpec(taps.shape, whole),
            pl.BlockSpec(heads_in.shape, whole),
            pl.BlockSpec(skip.shape, whole),
            pl.BlockSpec((1, 16 * pairs, 128), lambda i: (top - i, 0, 0)),
            pl.BlockSpec((1, pairs, STATE, PAIR), lambda i: (top - i, 0, 0, 0)),
            pl.BlockSpec((GROUP, width), block),
            pl.BlockSpec(carry.shape, lambda i: (0, 0, 0)),
            pl.BlockSpec(halo.shape, whole),
            pl.BlockSpec(memory_space=pl.ANY),
        ],
        out_specs=[
            pl.BlockSpec((GROUP, proj.shape[1]), block),
            pl.BlockSpec((8, core), whole),
            pl.BlockSpec((2 * heads, GROUP), whole),
            pl.BlockSpec(carry.shape, lambda i: (0, 0, 0)),
            pl.BlockSpec(halo.shape, whole),
        ],
        out_shape=[
            jax.ShapeDtypeStruct(proj.shape, BF16),
            jax.ShapeDtypeStruct((8, core), F32),
            jax.ShapeDtypeStruct((2 * heads, GROUP), F32),
            jax.ShapeDtypeStruct(carry.shape, F32),
            jax.ShapeDtypeStruct(halo.shape, F32),
        ],
        scratch_shapes=[
            pltpu.VMEM((GROUP, GROUP), F32),
            pltpu.VMEM((GROUP, GROUP), F32),
            pltpu.VMEM((128, 128), F32),
            pltpu.VMEM((2, GROUP, GROUP), F32),
            pltpu.VMEM((2, GROUP, GROUP), BF16),
            pltpu.VMEM((GROUP, STATE), F32),
            pltpu.VMEM((GROUP, STATE), F32),
            pltpu.VMEM((8 * heads, 128), F32),
            pltpu.VMEM((heads, PAIR), F32),
        ],
        compiler_params=pltpu.CompilerParams(vmem_limit_bytes=VMEM_LIMIT),
        input_output_aliases={} if held is None else {11: 0},
        cost_estimate=busy(12 * span, 5 * span),
        name="mix_backward",
    )(act, proj, proj, taps, heads_in, skip, table, starts, dy, carry, halo, dy if held is None else held)


def gate_sums(members_ref, seed_ref, z_ref, y_ref, gain_ref, *refs):
    parts, (w_ref, scaled_ref, sums_ref, squares, along) = refs[:-5], refs[-5:]
    step, n = pl.program_id(0), len(refs[:-5]) - 1

    @pl.when(step == 0)
    def _():
        squares[...] = jnp.zeros_like(squares)
        along[...] = jnp.zeros_like(along)
        places = list(range(n // 2)) + [n // 2] * 2 + list(range(n // 2 + 1, n))
        for k, (o, part) in enumerate(zip(places, parts)):
            at = pl.multiple_of(members_ref[o] * PAIR, PAIR)
            if k == n // 2 + 1:
                at = at + PAIR - part.shape[0]
            w_ref[pl.ds(at, part.shape[0]), :] = part[...]

    tile = z_ref.shape[1]
    scaled = nt(seed_ref[...], w_ref[pl.ds(pl.multiple_of(step * tile, tile), tile), :])
    scaled_ref[...] = scaled
    z = z_ref[...].astype(F32)
    gated = y_ref[...] * (z * sigmoid(z))
    square = gated * gated
    lean = scaled * gain_ref[...] * gated
    for cols in tiles(square.shape[1]):
        squares[...] += square[:, cols]
        along[...] += lean[:, cols]

    @pl.when(step == pl.num_programs(0) - 1)
    def _():
        spot = lanes(squares.shape)
        both = jnp.where(
            spot == 0,
            jnp.sum(squares[...], axis=1, keepdims=True),
            jnp.where(spot == 1, jnp.sum(along[...], axis=1, keepdims=True), 0.0),
        )
        sums_ref[...] = both.T[:8]


def run_gate_sums(members, seed, parts, z, y, gain):
    length, width = y.shape
    tile = 2 * PAIR
    col = pl.BlockSpec((length, tile), lambda i, t: (0, i))
    return pl.pallas_call(
        gate_sums,
        grid_spec=pltpu.PrefetchScalarGridSpec(
            num_scalar_prefetch=1,
            grid=(width // tile,),
            in_specs=[resident(seed, 2), col, col, pl.BlockSpec((1, tile), lambda i, t: (0, i))]
            + [resident(part, 2) for part in parts],
            out_specs=[
                pl.BlockSpec((width, D), lambda i, t: (0, 0)),
                col,
                pl.BlockSpec((8, length), lambda i, t: (0, 0)),
            ],
            scratch_shapes=[pltpu.VMEM((length, PAIR), F32)] * 2,
        ),
        out_shape=[
            jax.ShapeDtypeStruct((width, D), BF16),
            jax.ShapeDtypeStruct(y.shape, F32),
            jax.ShapeDtypeStruct((8, length), F32),
        ],
        compiler_params=pltpu.CompilerParams(vmem_limit_bytes=VMEM_LIMIT),
        cost_estimate=busy(11, 20),
        name="gate_sums",
    )(members, seed, z, y, gain, *parts)


def gate_back(sums_ref, scaled_ref, z_ref, y_ref, x_ref, gain_ref, mixed_ref, dy_ref, dz_ref, cols_ref, turned):
    @pl.when(pl.program_id(0) == 0)
    def _():
        inv = lax.rsqrt(sums_ref[0:1, :] / DI + EPS)
        slope = inv * inv * inv * (sums_ref[1:2, :] / DI)
        rest = jnp.zeros((PAIR - 2, sums_ref.shape[1]), F32)
        turned[...] = jnp.concatenate([inv, slope, rest], axis=0).T

    inv, slope = turned[:, 0:1], turned[:, 1:2]
    z, y, scaled, gain = z_ref[...].astype(F32), y_ref[...], scaled_ref[...], gain_ref[...]
    sig = sigmoid(z)
    silu = z * sig
    gated = y * silu
    normal = gated * inv
    mixed_ref[...] = (normal * gain).astype(BF16)
    d_gated = scaled * gain * inv - gated * slope
    dy = (d_gated * silu).astype(BF16)
    dy_ref[...] = dy
    dz_ref[...] = (d_gated * y * (sig * (1.0 + z * (1.0 - sig)))).astype(BF16)
    cols_ref[0:1, :] = jnp.sum(scaled * normal, axis=0, keepdims=True)
    cols_ref[1:2, :] = jnp.sum(dy.astype(F32) * x_ref[...].astype(F32), axis=0, keepdims=True)
    cols_ref[2:, :] = jnp.zeros_like(cols_ref[2:, :])


def run_gate_back(sums, scaled, z, y, x, gain):
    length, width = y.shape
    tile = PAIR
    col = pl.BlockSpec((length, tile), lambda i: (0, i))
    low = jax.ShapeDtypeStruct(y.shape, BF16)
    return pl.pallas_call(
        gate_back,
        grid=(width // tile,),
        in_specs=[
            pl.BlockSpec(sums.shape, lambda i: (0, 0)),
            col,
            col,
            col,
            col,
            pl.BlockSpec((1, tile), lambda i: (0, i)),
        ],
        out_specs=[col, col, col, pl.BlockSpec((8, tile), lambda i: (0, i))],
        out_shape=[low, low, low, jax.ShapeDtypeStruct((8, width), F32)],
        scratch_shapes=[pltpu.VMEM((length, PAIR), F32)],
        compiler_params=pltpu.CompilerParams(vmem_limit_bytes=VMEM_LIMIT),
        cost_estimate=busy(11, 20),
        name="gate_back",
    )(sums, scaled, z, y, x, gain)


def back_norm(members_ref, tokens_ref, dz_ref, dx_ref, *refs):
    parts, (dn_ref, gain_ref) = refs[:-2], refs[-2:]
    count = len(parts) // 2

    @pl.when(pl.program_id(0) == 0)
    def _():
        gain_ref[...] = jnp.zeros_like(gain_ref)

    tokens = tokens_ref[...].astype(F32)
    inv = lax.rsqrt(jnp.mean(tokens * tokens, axis=-1, keepdims=True) + EPS)
    sums = [None] * (D // SEG)
    for source, weights in ((dz_ref, parts[:count]), (dx_ref, parts[count:])):
        for o, at, w in by_segments(weights):
            part = nn(source[:, at : at + w.shape[0]], w[...])
            sums[o] = part if sums[o] is None else sums[o] + part
    for o, d_normed in enumerate(sums):
        at = pl.multiple_of(members_ref[o] * SEG, SEG)
        dn_ref[:, pl.ds(at, SEG)] = d_normed.astype(BF16)
        scaled = tokens_ref[:, pl.ds(at, SEG)].astype(F32) * inv
        gain_ref[0:1, pl.ds(at, SEG)] += jnp.sum(d_normed * scaled, axis=0, keepdims=True)


def run_back_norm(members, tokens, dz, dx, weights_z, weights_x):
    length = tokens.shape[0]
    row = lambda i, t: (i, 0)
    return pl.pallas_call(
        back_norm,
        grid_spec=pltpu.PrefetchScalarGridSpec(
            num_scalar_prefetch=1,
            grid=(length // GROUP,),
            in_specs=[
                pl.BlockSpec((GROUP, D), row),
                pl.BlockSpec((GROUP, dz.shape[1]), row),
                pl.BlockSpec((GROUP, dx.shape[1]), row),
            ]
            + [resident(w, 2) for w in weights_z + weights_x],
            out_specs=[pl.BlockSpec((GROUP, D), row), pl.BlockSpec((8, D), lambda i, t: (0, 0))],
        ),
        out_shape=[
            jax.ShapeDtypeStruct((length, D), BF16),
            jax.ShapeDtypeStruct((8, D), F32),
        ],
        compiler_params=pltpu.CompilerParams(vmem_limit_bytes=VMEM_LIMIT),
        cost_estimate=busy(18, 24),
        name="back_norm",
    )(members, tokens, dz, dx, *weights_z, *weights_x)


def put_pairs(place_ref, refs, out_ref, g):
    m = len(refs)
    for k, ref in enumerate(refs):
        to = pl.multiple_of((place_ref[0] ^ k) * PAIR, PAIR)
        out_ref[pl.ds(to, PAIR), :] = ref[pl.ds(pl.multiple_of(g * PAIR, PAIR), PAIR), :].astype(F32)


def assemble_z(place_ref, z0, z1, z2, z3, out_ref):
    put_pairs(place_ref, (z0, z1, z2, z3), out_ref, pl.program_id(0))


def assemble_a(place_ref, held_ref, a0, a1, a2, a3, out_ref):
    put_pairs(place_ref, (a0, a1, a2, a3), out_ref, pl.program_id(0))


def assemble_b(place_ref, order_ref, held_ref, b0, b1, b2, b3, out_ref):
    step, last = pl.program_id(0), pl.num_programs(0) - 1
    refs = (b0, b1, b2, b3)
    width = last * PAIR
    core = width + 2 * STATE

    @pl.when(step < last)
    def _():
        put_pairs(place_ref, refs, out_ref, step)

    @pl.when(step == last)
    def _():
        total = jnp.zeros((2 * STATE, out_ref.shape[1]), F32)
        steps = jnp.zeros((HEADS, out_ref.shape[1]), F32)
        for k, x in enumerate(refs):
            total = total + x[width:core].astype(F32)
            steps = steps + nn(order_ref[place_ref[0] ^ k], x[core : core + PAIR])
        out_ref[: 2 * STATE] = total
        out_ref[2 * STATE : 2 * STATE + HEADS] = steps


def run_assemble_z(place, shares, columns):
    m, rows = len(shares), shares[0].shape[1]
    tile = m * PAIR
    return pl.pallas_call(
        assemble_z,
        grid_spec=pltpu.PrefetchScalarGridSpec(
            num_scalar_prefetch=1,
            grid=(DI // tile,),
            in_specs=[resident(s, 2) for s in shares],
            out_specs=pl.BlockSpec((tile, rows), lambda i, t: (i, 0)),
        ),
        out_shape=jax.ShapeDtypeStruct((columns, rows), F32),
        compiler_params=pltpu.CompilerParams(vmem_limit_bytes=VMEM_LIMIT),
        cost_estimate=busy(4, 6),
        name="assemble_z",
    )(place, *shares)


def run_assemble_b(place, order, held, shares, count):
    m, rows = len(shares), shares[0].shape[1]
    tile = m * PAIR
    first = 2 * (DI // tile) - count
    return pl.pallas_call(
        assemble_b,
        grid_spec=pltpu.PrefetchScalarGridSpec(
            num_scalar_prefetch=1,
            grid=(count + 1,),
            in_specs=[resident(order, 2), pl.BlockSpec(memory_space=pl.ANY)]
            + [resident(s, 2) for s in shares],
            out_specs=pl.BlockSpec((tile, rows), lambda i, t: (i + first, 0)),
        ),
        out_shape=jax.ShapeDtypeStruct(held.shape, F32),
        input_output_aliases={2: 0},
        compiler_params=pltpu.CompilerParams(vmem_limit_bytes=VMEM_LIMIT),
        cost_estimate=busy(3, 2),
        name="assemble_b",
    )(place, order, held, *shares)


def run_assemble_a(place, held, shares):
    m, rows = len(shares), shares[0].shape[1]
    tile = m * PAIR
    return pl.pallas_call(
        assemble_a,
        grid_spec=pltpu.PrefetchScalarGridSpec(
            num_scalar_prefetch=1,
            grid=(shares[0].shape[0] // PAIR,),
            in_specs=[pl.BlockSpec(memory_space=pl.ANY)] + [resident(s, 2) for s in shares],
            out_specs=pl.BlockSpec((tile, rows), lambda i, t: (i + DI // tile, 0)),
        ),
        out_shape=jax.ShapeDtypeStruct(held.shape, F32),
        input_output_aliases={1: 0},
        compiler_params=pltpu.CompilerParams(vmem_limit_bytes=VMEM_LIMIT),
        cost_estimate=busy(4, 5),
        name="assemble_a",
    )(place, held, *shares)


def body(
    tokens, norm_gain, w_in, conv_w, conv_b, dt_bias, a_log, d_skip, gate_gain, w_out, cotangent
):
    n, m = lax.axis_size("fsdp"), lax.axis_size("ctx")
    place = lax.axis_index("ctx")
    piece = tokens.shape[1]
    length = piece * m
    blocks = length // GROUP
    pairs = DI // PAIR // m
    width = pairs * PAIR
    heads = 2 * pairs
    rows = w_in.shape[0]
    core_cols = width + 2 * STATE
    head_cols = core_cols + heads
    ring = rows == SEG and (DI // PAIR) // n == m

    def of_pairs(array, axis):
        shape = array.shape
        each = shape[axis] // (pairs * m)
        split = array.reshape(shape[:axis] + (pairs, m, each) + shape[axis + 1 :])
        mine = lax.dynamic_index_in_dim(split, place, axis + 1, False)
        return mine.reshape(shape[:axis] + (pairs * each,) + shape[axis + 1 :])

    def of_heads(array):
        mine = of_pairs(array, 0)
        split = mine.reshape((pairs, 2) + mine.shape[1:]).swapaxes(0, 1)
        return split.reshape(mine.shape)

    all_tokens = lax.all_gather(tokens[0], "ctx", axis=0, tiled=True)
    seed = lax.all_gather(cotangent[0], "ctx", axis=0, tiled=True)

    dt_bias_own, a_log_own = of_heads(dt_bias), of_heads(a_log)
    skip_own = of_pairs(d_skip, 0)
    a_neg = -jnp.exp(a_log_own)
    heads_in = jnp.broadcast_to(jnp.concatenate([dt_bias_own, a_neg])[:, None], (2 * heads, 128))
    skip_row = jnp.repeat(skip_own, HEADDIM)[None, :]

    columns = w_in.T
    total_cols = core_cols + PAIR
    cut = halves(total_cols)[0]
    place_ref = place.reshape(1).astype(jnp.int32)
    smalls = [norm_gain[None], gate_gain[None], conv_b[None], conv_w]
    small_rows = [-(-v.shape[1] // SEG) for v in smalls]

    def split(whole):
        upper, _ = halves(whole.shape[0])
        parts = [whole[:, o * SEG : (o + 1) * SEG] for o in range(D // SEG)]
        middle = parts[len(parts) // 2]
        return parts[: len(parts) // 2] + [middle[:upper], middle[upper:]] + parts[len(parts) // 2 + 1 :]

    if ring:
        me = ring_place(lax.axis_index("fsdp"), n)
        members = ring_member(me + jnp.arange(n), n).astype(jnp.int32)
        padded = [jnp.pad(v, ((0, 0), (0, k * SEG - v.shape[1]))) for v, k in zip(smalls, small_rows)]
        small = jnp.concatenate([v.reshape(-1) for v in padded]).reshape(-1, SEG)
        block_x, block_z, block_o = run_pack(place_ref, columns, w_out, small, pairs)
        ring_x, ring_z, ring_o = Gather(block_x, n), Gather(block_z, n), Gather(block_o, n)
        next_hop([ring_x], (), heads_in, skip_row)
        for _ in range(n // 2 - 3):
            next_hop([ring_x], ())
        next_hop([ring_x, ring_z], ())
        next_hop([ring_x], (), *arrivals(ring_z))
        parts_x = ring_x.parts()
        all_tokens = next_hop([ring_z, ring_o], all_tokens, *arrivals(ring_x))
    else:
        members = jnp.arange(D // SEG, dtype=jnp.int32)
        block_x = jnp.concatenate(
            [
                of_pairs(columns[DI : 2 * DI], 0),
                columns[2 * DI : 2 * DI + 2 * STATE],
                of_heads(columns[DI + CONV :]),
                jnp.zeros((PAIR - heads, rows), BF16),
            ],
            axis=0,
        )
        whole_x = lax.all_gather(block_x, "fsdp", axis=1, tiled=True)
        norm_whole = lax.all_gather(norm_gain[None], "fsdp", axis=1, tiled=True)
        at = core_cols + SMALL
        whole_x = jnp.concatenate([whole_x[:at], norm_whole, whole_x[at + 1 :]], axis=0)
        parts_x, parts_z = split(whole_x), split(lax.all_gather(of_pairs(columns[:DI], 0), "fsdp", axis=1, tiled=True))
        w_o = of_pairs(lax.all_gather(w_out, "fsdp", axis=0, tiled=True), 0)
        parts_o = [w_o[o * PAIR : (o + 1) * PAIR] for o in range(pairs)]
        middle, upper = parts_o[pairs // 2], halves(PAIR)[0]
        parts_o = parts_o[: pairs // 2] + [middle[:upper], middle[upper:]] + parts_o[pairs // 2 + 1 :]

    if ring:
        kept = run_collect(members, parts_x)
        spans, at = [], 0
        for v, each in zip(smalls, small_rows):
            here = kept[:, at : at + v.shape[0] * each].reshape(n, v.shape[0], each * SEG)
            spans.append(here[:, :, : v.shape[1]].transpose(1, 0, 2).reshape(v.shape[0], -1))
            at += v.shape[0] * each
        norm_full, gate_full, bias_full, taps_full = spans
    else:
        norm_full, gate_full, bias_full, taps_full = (
            lax.all_gather(v, "fsdp", axis=1, tiled=True).astype(F32) for v in smalls
        )
    gate_full = of_pairs(gate_full, 1)
    taps_full = jnp.concatenate([taps_full, bias_full], axis=0)
    taps = jnp.concatenate([of_pairs(taps_full[:, :DI], 1), taps_full[:, DI:]], axis=1)
    taps = jnp.pad(taps, ((0, 8 - KW - 1), (0, 0)))

    normed, proj_x = run_front(members, all_tokens, parts_x)
    if ring:
        proj_x = next_hop([ring_z, ring_o], proj_x, *arrivals(ring_z, ring_o))
    act, table, ssd, starts = run_mix_forward(proj_x, taps, heads_in, skip_row, pairs)
    normed_z = normed
    if ring:
        for _ in range(n // 2 - 3):
            next_hop([ring_z, ring_o], (), ssd, *arrivals(ring_z, ring_o))
        normed_z = next_hop([ring_o], normed, *arrivals(ring_z))
        parts_z, parts_o = ring_z.parts(), ring_o.parts()
    proj_z = run_project(normed_z, parts_z)

    w_o, scaled, sums = run_gate_sums(members, seed, parts_o, proj_z, ssd, gate_full)
    sums = ctx_sum(sums, m)
    mixed, dy, d_z, gate_cols = run_gate_back(sums, scaled, proj_z, ssd, act, gate_full)

    grads_o = tn(mixed, seed).astype(BF16)
    carry = jnp.zeros((pairs, STATE, PAIR), F32)
    halo = jnp.zeros((HALO, core_cols), F32)
    conv_grads, head_grads, top, d_x, d_z_late, mixed_late = [], [], blocks - 1, None, d_z, mixed
    if ring:
        sum_o = Reduce(lambda o: lax.dynamic_slice_in_dim(grads_o, members[o] * PAIR, PAIR, 0), n)
        d_z_late, mixed_late = next_hop([sum_o], (d_z, mixed))
    grads_z = tn(d_z_late, normed).astype(BF16)
    branch = nn(mixed_late, w_o).astype(BF16)
    if ring:
        sum_z = Reduce(lambda o: grads_z[:, o * SEG : (o + 1) * SEG], n)
    for at in range(2):
        if ring:
            sum_o.join()
            if at > 0:
                sum_z.join()
                branch_own.middle()
                dy, carry, branch_own.sent = next_hop(
                    [sum_o, sum_z], (dy, carry, branch_own.sent)
                )
                branch_own.send_far()
            else:
                dy, carry, branch = next_hop([sum_o, sum_z], (dy, carry, branch))
                branch_own = CtxReduce(branch.reshape(m, piece, D), m)
        span = blocks // 2
        d_x, conv_part, head_part, carry, halo = run_mix_backward(
            span, top, act, proj_x, taps, heads_in, skip_row, table, starts, dy, carry, halo, d_x
        )
        conv_grads.append(conv_part)
        head_grads.append(head_part)
        top -= span
    normed_late = normed
    if ring:
        sum_o.join()
        sum_z.join()
        d_x, normed_late, conv_grads, head_grads, gate_cols, branch_own.far = next_hop(
            [sum_o, sum_z], (d_x, normed, conv_grads, head_grads, gate_cols, branch_own.far)
        )
    else:
        branch_own = CtxReduce(branch.reshape(m, piece, D), m)
        branch_own.middle()
        branch_own.send_far()
    grads_x = tn(d_x, normed_late).astype(BF16)
    d_normed, d_gain = run_back_norm(
        members, all_tokens, d_z, after(d_x, grads_x), parts_z, parts_x
    )
    if ring:
        part_o = sum_o.join().astype(BF16)
        sum_z.join()
        sum_a = Reduce(lambda o: grads_x[:cut, o * SEG : (o + 1) * SEG], n)
        sum_b = Reduce(lambda o: grads_x[cut:, o * SEG : (o + 1) * SEG], n)
        d_normed, d_gain, part_o, conv_grads, head_grads, gate_cols, branch_own.far = next_hop(
            [sum_a, sum_b, sum_z],
            (d_normed, d_gain, part_o, conv_grads, head_grads, gate_cols, branch_own.far),
        )
    d_own = CtxReduce(d_normed.reshape(m, piece, D), m)
    d_own.middle()
    d_own.send_far()

    head_sums = jnp.sum(head_grads[0] + head_grads[1], axis=1)
    d_skip_own = jnp.sum(gate_cols[1].reshape(pairs, 2, HEADDIM), axis=2).T.reshape(heads)
    per_head = jnp.concatenate([head_sums[:heads], head_sums[heads:] * a_neg, d_skip_own])
    conv_grads = (conv_grads[0] + conv_grads[1])[: KW + 1]
    lines = [conv_grads, gate_cols[0:1], d_gain[0:1], per_head[None]]
    wide = max(line.shape[1] for line in lines)
    small = jnp.concatenate(
        [jnp.pad(line, ((0, 0), (0, wide - line.shape[1]))) for line in lines], axis=0
    )
    flip = 1
    steps = []
    while flip < n:
        steps.append(flip)
        flip *= 2

    def small_step(small):
        if steps:
            small = small + lax.ppermute(small, "fsdp", ctx_route(n, steps.pop()))
        return small

    small = small_step(small)
    if ring:
        sum_a.join()
        sum_b.join()
        part_z = sum_z.join().astype(BF16)
        d_own.far, small, part_o, part_z, branch_own.far = next_hop(
            [sum_a, sum_b], (d_own.far, small, part_o, part_z, branch_own.far)
        )
        other_o = far_share(part_o, m)
    small = small_step(small)
    output = (tokens[0].astype(F32) + branch_own.total()).astype(BF16)[None]
    if ring:
        sum_a.join()
        sum_b.join()
        small, other_o, part_z, d_own.far = next_hop(
            [sum_a, sum_b], (small, other_o, part_z, d_own.far), output
        )
        shares_o, other_z = near_share(part_o, other_o, m), far_share(part_z, m)
    while steps:
        small = small_step(small)
    own = tokens[0].astype(F32)
    inv = lax.rsqrt(jnp.mean(own * own, axis=-1, keepdims=True) + EPS)
    d_direct = d_own.total() * norm_full
    along = jnp.mean(d_direct * own, axis=-1, keepdims=True)
    grad_tokens = (cotangent[0].astype(F32) + d_direct * inv - own * (inv * inv * inv * along))[None]
    if ring:
        for at in range(n // 2 - 3):
            sum_a.join()
            sum_b.join()
            small, shares_o, part_z, other_z = next_hop(
                [sum_a, sum_b], (small, shares_o, part_z, other_z), grad_tokens
            )
    smalls_of = ctx_share(small, m)
    by_place = jnp.zeros((m,) + small.shape, F32)
    for k in range(m):
        by_place = lax.dynamic_update_slice(by_place, smalls_of[k][None], (place ^ k, 0, 0))
    mine = lax.axis_index("fsdp")

    def own_columns(rows_first, rows_last, extra):
        part = by_place[:, rows_first:rows_last, :width].reshape(m, -1, pairs, PAIR)
        whole = part.transpose(1, 2, 0, 3).reshape(-1, DI)
        if extra:
            shared = jnp.sum(by_place[:, rows_first:rows_last, width:core_cols], axis=0)
            whole = jnp.concatenate([whole, shared], axis=1)
        each = whole.shape[1] // n
        return lax.dynamic_slice_in_dim(whole, mine * each, each, 1)

    grad_conv = own_columns(0, KW + 1, True)
    grad_conv_w, grad_conv_b = grad_conv[:KW], grad_conv[KW]
    grad_gate_gain = own_columns(KW + 1, KW + 2, False)[0]
    grad_gain = jnp.sum(by_place[:, KW + 2, :D], axis=0)
    grad_gain = lax.dynamic_slice_in_dim(grad_gain, mine * rows, rows, 0)
    per_head = by_place[:, KW + 3, : 3 * heads]
    per_head = per_head.reshape(m, 3, 2, pairs).transpose(1, 3, 0, 2).reshape(3, HEADS)
    small_outputs = (grad_gain, grad_conv_w, grad_conv_b, per_head, grad_gate_gain)
    if ring:
        shares_z = near_share(part_z, other_z, m)
        held = run_assemble_z(place_ref, shares_z, w_in.shape[1])
        grad_w_out = jnp.zeros((m, PAIR, D), F32)
        for k in range(m):
            grad_w_out = lax.dynamic_update_slice(
                grad_w_out, shares_o[k].astype(F32)[None], (place ^ k, 0, 0)
            )
        grad_w_out = grad_w_out.reshape(w_out.shape)
        part_b, part_a = sum_b.join().astype(BF16), sum_a.join().astype(BF16)
        part_a, part_b, held, small_outputs = barrier((part_a, part_b, held, small_outputs), grad_w_out)
    else:
        part_z = lax.psum_scatter(grads_z.astype(F32), "fsdp", scatter_dimension=1, tiled=True)
        part_x = lax.psum_scatter(grads_x.astype(F32), "fsdp", scatter_dimension=1, tiled=True)
        whole_o = jnp.zeros((pairs, m, PAIR, D), F32)
        whole_o = lax.dynamic_update_index_in_dim(
            whole_o, grads_o.astype(F32).reshape(pairs, PAIR, D), place, 1
        )
        grad_w_out = lax.psum_scatter(whole_o.reshape(DI, D), "fsdp", scatter_dimension=0, tiled=True)
        grad_w_out = lax.psum(grad_w_out, "ctx")
        held = run_assemble_z(place_ref, ctx_share(part_z.astype(BF16), m), w_in.shape[1])
        part_a, part_b = part_x[:cut].astype(BF16), part_x[cut:].astype(BF16)
    other_b, other_a = far_share(part_b, m), far_share(part_a, m)
    grad_gain, grad_conv_w, grad_conv_b, per_head, grad_gate_gain = small_outputs
    order = np.zeros((m, HEADS, PAIR), np.float32)
    for member in range(m):
        for h in range(heads):
            order[member, (h % pairs) * 2 * m + 2 * member + h // pairs, h] = 1.0
    shares_b = near_share(part_b, other_b, m)
    held = run_assemble_b(place_ref, jnp.asarray(order, BF16), held, shares_b, pairs - cut // PAIR)
    shares_a = near_share(part_a, other_a, m)
    grad_w_in = run_assemble_a(place_ref, held, shares_a)
    return (
        output,
        grad_tokens,
        grad_gain,
        grad_w_in.T,
        grad_conv_w,
        grad_conv_b,
        per_head[0],
        per_head[1],
        per_head[2],
        grad_gate_gain,
        grad_w_out,
    )


def solution(mesh):
    in_specs = (
        P("fsdp", "ctx", None),
        P("fsdp"),
        P("fsdp", None),
        P(None, "fsdp"),
        P("fsdp"),
        P(),
        P(),
        P(),
        P("fsdp"),
        P("fsdp", None),
        P("fsdp", "ctx", None),
    )
    out_specs = (
        P("fsdp", "ctx", None),
        P("fsdp", "ctx", None),
        P("fsdp"),
        P("fsdp", None),
        P(None, "fsdp"),
        P("fsdp"),
        P(),
        P(),
        P(),
        P("fsdp"),
        P("fsdp", None),
    )
    return jax.shard_map(body, mesh=mesh, in_specs=in_specs, out_specs=out_specs, check_vma=False)
```

```python
import jax
import jax.numpy as jnp
import numpy as np
from jax import lax
from jax.experimental import pallas as pl
from jax.experimental.pallas import tpu as pltpu
from jax.sharding import PartitionSpec as P

D = 2048
HEADS = 64
HEADDIM = 64
STATE = 128
KW = 4
GROUP = 256
DI = HEADS * HEADDIM
CONV = DI + 2 * STATE
PAIR = 2 * HEADDIM
EPS = 1e-05
SEG = 256
HALO = 8
SMALL = 32
TAIL = 32
VMEM_LIMIT = 56 * 1024 * 1024
F32 = jnp.float32
BF16 = jnp.bfloat16


def ring_place(index, n):
    return jnp.where(index % 2 == 0, index // 2, n - 1 - index // 2)


def ring_member(place, n):
    place = place % n
    return jnp.where(place < n // 2, 2 * place, 2 * (n - 1 - place) + 1)


def ring_routes(n):
    order = [2 * p if p < n // 2 else 2 * (n - 1 - p) + 1 for p in range(n)]
    forward = [(order[p], order[(p + 1) % n]) for p in range(n)]
    return forward, [(b, a) for a, b in forward]


def send(block, route):
    return lax.ppermute(block, "fsdp", route)


def after(value, *earlier):
    return lax.optimization_barrier((value, *earlier))[0]


def halves(rows):
    upper = -(-rows // 256) * 128 if rows >= 512 else rows // 2
    return upper, rows - upper


class Gather:
    def __init__(self, block, n):
        self.forward, self.backward = ring_routes(n)
        self.block, self.n = block, n
        self.latest = (block, block)
        self.ahead, self.behind = [], []

    def load(self):
        right, left = self.latest
        if len(self.ahead) == self.n // 2 - 1:
            upper, _ = halves(self.block.shape[0])
            return right[:upper], left[upper:]
        return right, left

    def fire(self, right, left):
        last = len(self.ahead) == self.n // 2 - 1
        self.latest = send(right, self.forward), send(left, self.backward)
        if not last:
            self.behind.insert(0, self.latest[0])
            self.ahead.append(self.latest[1])

    def parts(self):
        return [self.block] + self.ahead + list(self.latest) + self.behind


class Reduce:
    def __init__(self, chunk, n, pieces=None):
        self.forward, self.backward = ring_routes(n)
        self.chunk, self.n, self.step = chunk, n, n // 2
        if pieces is None:
            first = chunk(n // 2).astype(BF16)
            upper, _ = halves(first.shape[0])
            pieces = first[:upper], first[upper:]
        self.right, self.left = pieces
        self.upper = self.right.shape[0]

    def load(self):
        return self.right, self.left

    def fire(self, right, left):
        self.latest = send(right, self.forward), send(left, self.backward)
        self.step -= 1

    def join(self):
        right, left = (part.astype(F32) for part in self.latest)
        if self.step == 0:
            return self.chunk(0).astype(F32) + right + left
        own_right = self.chunk(self.step).astype(F32)
        own_left = self.chunk(self.n - self.step).astype(F32)
        cut = self.upper
        if self.step == self.n // 2 - 1:
            right = jnp.concatenate([own_right[:cut] + right, own_right[cut:]], axis=0)
            left = jnp.concatenate([own_left[:cut], own_left[cut:] + left], axis=0)
        else:
            right, left = own_right + right, own_left + left
        self.right, self.left = right.astype(BF16), left.astype(BF16)


def cut_in_two(grads_ref, right_ref, left_ref):
    upper = right_ref.shape[0]
    right_ref[...] = grads_ref[:upper]
    left_ref[...] = grads_ref[upper:]


def run_cut(grads, rows, block):
    shapes = [(half, SEG) for half in halves(rows)]
    return pl.pallas_call(
        cut_in_two,
        grid=(1,),
        in_specs=[pl.BlockSpec((rows, SEG), lambda i: (0, block))],
        out_specs=[pl.BlockSpec(shape, lambda i: (0, 0)) for shape in shapes],
        out_shape=[jax.ShapeDtypeStruct(shape, BF16) for shape in shapes],
        cost_estimate=busy(1, 1),
        name="cut_in_two",
    )(grads)


def barrier(value, *earlier):
    return lax.optimization_barrier((value, earlier))[0]


def next_hop(rings, inputs, *earlier):
    loads, inputs = barrier(([ring.load() for ring in rings], inputs), *earlier)
    for ring, load in zip(rings, loads):
        ring.fire(*load)
    return inputs


def arrivals(*rings):
    return sum((ring.latest for ring in rings), ())


def ctx_route(m, flip):
    return [(i, i ^ flip) for i in range(m)]


def far_share(block, m):
    return lax.ppermute(block, "ctx", ctx_route(m, 2))


def near_share(block, other, m):
    near = lax.ppermute(block, "ctx", ctx_route(m, 1))
    far = lax.ppermute(other, "ctx", ctx_route(m, 1))
    return [block, near, other, far]


def ctx_share(block, m):
    return near_share(block, far_share(block, m), m)


def gather_small(conv0, conv1, heads0, heads1, gate_ref, gain_ref, out_ref):
    out_ref[...] = jnp.zeros_like(out_ref)
    lines = [(conv0, k, conv1) for k in range(KW + 1)]
    lines += [(gate_ref, 0, None), (gate_ref, 1, None), (gain_ref, 0, None)]
    at = 0
    for ref, row, other in lines:
        for start in range(0, ref.shape[1], SEG):
            line = ref[row : row + 1, start : start + SEG]
            if other is not None:
                line = line + other[row : row + 1, start : start + SEG]
            out_ref[at : at + 1, :] = line
            at += 1
    at = out_ref.shape[0] - heads0.shape[0]
    out_ref[at:, :] = heads0[...] + heads1[...]


def run_gather_small(conv_grads, head_grads, gate_cols, d_gain):
    arrays = [*conv_grads, *head_grads, gate_cols, d_gain]
    lines = (KW + 1) * conv_grads[0].shape[1] + 2 * gate_cols.shape[1] + d_gain.shape[1]
    rows = -(-lines // SEG // 8) * 8 + head_grads[0].shape[0]
    return pl.pallas_call(
        gather_small,
        grid=(1,),
        in_specs=[pl.BlockSpec(v.shape, lambda i: (0, 0)) for v in arrays],
        out_specs=pl.BlockSpec((rows, SEG), lambda i: (0, 0)),
        out_shape=jax.ShapeDtypeStruct((rows, SEG), F32),
        cost_estimate=busy(1, 1),
        name="gather_small",
    )(*arrays)


class CtxReduce:
    def __init__(self, kept, given, m):
        self.m, place = m, lax.axis_index("ctx")
        self.core, self.across = place % 2, place // 2
        self.kept = kept
        self.near = lax.ppermute(given, "ctx", ctx_route(m, 1))

    def middle(self):
        self.both = self.kept.astype(F32) + self.near.astype(F32)
        self.sent = lax.dynamic_index_in_dim(self.both, 1 - self.across, 0, False).astype(BF16)

    def send_far(self):
        self.far = lax.ppermute(self.sent, "ctx", ctx_route(self.m, 2))

    def total(self):
        return lax.dynamic_index_in_dim(self.both, self.across, 0, False) + self.far.astype(F32)


def by_core(share, m):
    core = lax.axis_index("ctx") % 2
    split = share.reshape((m // 2, 2) + share.shape[1:])
    return (
        lax.dynamic_index_in_dim(split, core, 1, False),
        lax.dynamic_index_in_dim(split, 1 - core, 1, False),
    )


def ctx_sum(values, m):
    near, across, far = (lax.ppermute(values, "ctx", ctx_route(m, flip)) for flip in (1, 2, 3))
    return (values + near) + (across + far)


def nt(a, b):
    return lax.dot_general(a, b, (((1,), (1,)), ((), ())), preferred_element_type=F32)


def nn(a, b):
    return lax.dot_general(a, b, (((1,), (0,)), ((), ())), preferred_element_type=F32)


def tn(a, b):
    return lax.dot_general(a, b, (((0,), (0,)), ((), ())), preferred_element_type=F32)


def lanes(shape):
    return lax.broadcasted_iota(jnp.int32, shape, len(shape) - 1)


def busy(us, megabytes):
    return pl.CostEstimate(
        flops=int(us * 1e9), transcendentals=0, bytes_accessed=int(megabytes * 1e6)
    )


def softplus(v):
    return jnp.maximum(v, 0.0) + jnp.log1p(jnp.exp(-jnp.abs(v)))


def sigmoid(v):
    return 1.0 / (1.0 + jnp.exp(-v))


def ones_where(keep):
    row = lax.broadcasted_iota(jnp.int32, (GROUP, GROUP), 0)
    col = lax.broadcasted_iota(jnp.int32, (GROUP, GROUP), 1)
    return keep(row, col)


def exact(a, b):
    return lax.dot_general(
        a, b, (((1,), (0,)), ((), ())), preferred_element_type=F32, precision=lax.Precision.HIGHEST
    )


def tiles(width):
    return [slice(at, at + PAIR) for at in range(0, width, PAIR)]


def conv_tile(extended, taps_ref, cols):
    total = taps_ref[KW : KW + 1, cols]
    for k in range(KW):
        at = HALO - KW + 1 + k
        total = total + taps_ref[k : k + 1, cols] * extended[at : at + GROUP]
    return total


def by_segments(weights):
    n = D // SEG
    places = list(range(n // 2)) + [n // 2] * 2 + list(range(n // 2 + 1, n))
    at = [0] * len(places)
    at[n // 2 + 1] = weights[n // 2].shape[0]
    return list(zip(places, at, weights))


def project_into(out_ref, normed_ref, weights, total):
    whole = None
    for o, at, w in by_segments(weights):
        part = nt(normed_ref[:, o * SEG : (o + 1) * SEG], w[...])
        if o == D // SEG // 2:
            total[:, at : at + w.shape[0]] = part
        else:
            whole = part if whole is None else whole + part
    out_ref[...] = (whole + total[...]).astype(BF16)


def pack(
    place_ref, columns_ref, out_ref, small_ref, x_ref, z_ref, o_ref, steps, rows, sems,
):
    place = place_ref[0]
    pairs, m = z_ref.shape[0] // PAIR, out_ref.shape[0] // PAIR
    core = pairs * PAIR + 2 * STATE
    copies = [
        (columns_ref.at[pl.ds(DI + CONV, HEADS)], steps),
        (columns_ref.at[pl.ds(2 * DI, 2 * STATE)], x_ref.at[pl.ds(pairs * PAIR, 2 * STATE)]),
        (out_ref.at[pl.ds(pl.multiple_of(place * PAIR, PAIR), PAIR)], o_ref),
    ]
    for g in range(pairs):
        here = pl.ds(g * PAIR, PAIR)
        for start, ref in ((DI, x_ref), (0, z_ref)):
            at = pl.multiple_of(start + (g * m + place) * PAIR, PAIR)
            copies.append((columns_ref.at[pl.ds(at, PAIR)], ref.at[here]))
    copies = [pltpu.make_async_copy(*pair, sems.at[k]) for k, pair in enumerate(copies)]
    for copy in copies:
        copy.start()
    rows[...] = jnp.zeros_like(rows)
    rows[SMALL : SMALL + small_ref.shape[0], :] = small_ref[...].astype(F32)
    copies[0].wait()
    want = lax.broadcasted_iota(jnp.int32, (2 * pairs, HEADS), 0)
    have = lax.broadcasted_iota(jnp.int32, (2 * pairs, HEADS), 1)
    head = (want % pairs) * 2 * m + 2 * place + want // pairs
    rows[: 2 * pairs, :] = nn((have == head).astype(BF16), steps[...])
    x_ref[core : core + PAIR, :] = rows[...].astype(BF16)
    for copy in copies[1:]:
        copy.wait()


def run_pack(place, columns, w_out, small, pairs):
    rows = columns.shape[1]
    core = pairs * PAIR + 2 * STATE
    anywhere = pl.BlockSpec(memory_space=pl.ANY)
    shapes = [(core + PAIR, rows), (pairs * PAIR, rows), (PAIR, D)]
    return pl.pallas_call(
        pack,
        grid_spec=pltpu.PrefetchScalarGridSpec(
            num_scalar_prefetch=1,
            grid=(1,),
            in_specs=[anywhere, anywhere, pl.BlockSpec(small.shape, lambda i, t: (0, 0))],
            out_specs=[pl.BlockSpec(shape, lambda i, t: (0, 0)) for shape in shapes],
            scratch_shapes=[
                pltpu.VMEM((HEADS, rows), BF16),
                pltpu.VMEM((PAIR, rows), F32),
                pltpu.SemaphoreType.DMA((2 * pairs + 3,)),
            ],
        ),
        out_shape=[jax.ShapeDtypeStruct(shape, BF16) for shape in shapes],
        compiler_params=pltpu.CompilerParams(vmem_limit_bytes=VMEM_LIMIT),
        name="pack",
    )(place, columns, w_out, small)


def collect(members_ref, *refs):
    out_ref = refs[-1]
    for o, ref in enumerate(refs[:-1]):
        out_ref[members_ref[o]] = ref[...].astype(F32)


def run_collect(members, parts):
    n = len(parts) - 1
    lasts = parts[: n // 2] + parts[n // 2 + 1 :]
    at = lambda part: (part.shape[0] - PAIR + SMALL) // 32
    return pl.pallas_call(
        collect,
        grid_spec=pltpu.PrefetchScalarGridSpec(
            num_scalar_prefetch=1,
            grid=(1,),
            in_specs=[pl.BlockSpec((32, SEG), lambda i, t, k=at(p): (k, 0)) for p in lasts],
            out_specs=pl.BlockSpec((n, 32, SEG), lambda i, t: (0, 0, 0)),
        ),
        out_shape=jax.ShapeDtypeStruct((n, 32, SEG), F32),
        compiler_params=pltpu.CompilerParams(vmem_limit_bytes=VMEM_LIMIT),
        cost_estimate=busy(1, 1),
        name="collect",
    )(members, *lasts)


def front(members_ref, tokens_ref, *refs):
    weights, (normed_ref, proj_ref, total) = refs[:-3], refs[-3:]
    tokens = tokens_ref[...].astype(F32)
    inv = lax.rsqrt(jnp.mean(tokens * tokens, axis=-1, keepdims=True) + EPS)
    for o in range(D // SEG):
        at = pl.multiple_of(members_ref[o] * SEG, SEG)
        cols = slice(o * SEG, (o + 1) * SEG)
        last = weights[o if o < D // SEG // 2 else o + 1]
        row = last.shape[0] - PAIR + SMALL
        gain = last[row : row + 16, :].astype(F32)[0:1]
        part = tokens_ref[:, pl.ds(at, SEG)].astype(F32) * inv * gain
        normed_ref[:, cols] = part.astype(BF16)
    project_into(proj_ref, normed_ref, weights, total)


def resident(array, grid_args=1):
    zeros = (0,) * array.ndim
    maps = {1: lambda i: zeros, 2: lambda i, t: zeros, 3: lambda i, t, p: zeros}
    return pl.BlockSpec(array.shape, maps[grid_args], pipeline_mode=pl.Buffered(1))


def run_front(members, tokens, weights):
    length, cols = tokens.shape[0], weights[0].shape[0]
    return pl.pallas_call(
        front,
        grid_spec=pltpu.PrefetchScalarGridSpec(
            num_scalar_prefetch=1,
            grid=(length // GROUP,),
            in_specs=[
                pl.BlockSpec((GROUP, D), lambda i, t: (i, 0)),
            ]
            + [resident(w, 2) for w in weights],
            out_specs=[
                pl.BlockSpec((GROUP, D), lambda i, t: (i, 0)),
                pl.BlockSpec((GROUP, cols), lambda i, t: (i, 0)),
            ],
            scratch_shapes=[pltpu.VMEM((GROUP, cols), F32)],
        ),
        out_shape=[
            jax.ShapeDtypeStruct((length, D), BF16),
            jax.ShapeDtypeStruct((length, cols), BF16),
        ],
        compiler_params=pltpu.CompilerParams(vmem_limit_bytes=VMEM_LIMIT),
        cost_estimate=busy(12, 18),
        name="front",
    )(members, tokens, *weights)


def project(normed_ref, *refs):
    project_into(refs[-2], normed_ref, refs[:-2], refs[-1])


def run_project(normed, weights):
    length, cols = normed.shape[0], weights[0].shape[0]
    return pl.pallas_call(
        project,
        grid=(length // GROUP,),
        in_specs=[pl.BlockSpec((GROUP, D), lambda i: (i, 0))] + [resident(w) for w in weights],
        out_specs=pl.BlockSpec((GROUP, cols), lambda i: (i, 0)),
        out_shape=jax.ShapeDtypeStruct((length, cols), BF16),
        scratch_shapes=[pltpu.VMEM((GROUP, cols), F32)],
        compiler_params=pltpu.CompilerParams(vmem_limit_bytes=VMEM_LIMIT),
        cost_estimate=busy(8, 10),
        name="project",
    )(normed, *weights)


def spread_rows(ref, index, rows):
    count = rows.shape[0]
    ref[pl.ds(index, count), :] = rows[:, :128]
    ref[pl.ds(ref.shape[0] // 2 + index, count), :] = rows[:, 128:]


def all_rows(stack):
    half = stack.shape[0] // 2
    return jnp.concatenate([stack[:half], stack[half:]], axis=1)


def pair_rows(ref, g, pairs):
    half = 8 * pairs
    return jnp.concatenate(
        [ref[pl.ds(g, 8, stride=pairs), :], ref[pl.ds(half + g, 8, stride=pairs), :]], axis=1
    )


def high_low(v):
    high = v.astype(BF16)
    return high, (v - high.astype(F32)).astype(BF16)


def tri_units(back):
    units = []
    for r in range(GROUP // 64):
        for t in range(GROUP // 128):
            if (t >= r // 2) if back else (t <= r // 2):
                units.append((slice(64 * r, 64 * r + 64), slice(128 * t, 128 * t + 128), t == r // 2))
    return units


def diagonal(keep):
    row = lax.broadcasted_iota(jnp.int32, (128, 128), 0)
    col = lax.broadcasted_iota(jnp.int32, (128, 128), 1)
    return jnp.where(keep(row, col), 0.0, -1e30)


def mix_forward(
    proj_ref, taps_ref, heads_ref, skip_ref, act_ref, table_ref, y_ref, start_ref,
    state, halo, gram, bias, scores,
):
    pairs = state.shape[0]
    heads, width = 2 * pairs, pairs * PAIR
    core = width + 2 * STATE

    @pl.when(pl.program_id(0) == 0)
    def _():
        state[...] = jnp.zeros_like(state)
        halo[...] = jnp.zeros_like(halo)
        scores[...] = jnp.zeros_like(scores)
        bias[...] = diagonal(lambda row, col: row >= col)

    def activate(cols):
        current = proj_ref[:, cols].astype(F32)
        conv = conv_tile(jnp.concatenate([halo[:, cols], current], axis=0), taps_ref, cols)
        halo[:, cols] = current[GROUP - HALO :]
        act = (conv * sigmoid(conv)).astype(BF16)
        act_ref[:, cols] = act
        return act

    bs = activate(slice(width, width + STATE))
    cs = activate(slice(width + STATE, core))
    raw = proj_ref[:, core : core + PAIR].astype(F32).T[:heads]
    dt = softplus(raw + heads_ref[:heads, 0:1])
    upto = ones_where(lambda row, col: row <= col).astype(F32)
    cum = exact(dt * heads_ref[heads:, 0:1], upto)
    last = cum[:, GROUP - 1 :]
    table = jnp.concatenate([cum, dt, jnp.exp(last - cum) * dt, jnp.exp(cum)], axis=0)
    spread_rows(table_ref.at[0], 0, table)
    gram[...] = nt(cs, bs)
    bs_t = bs.astype(F32).T

    def one(g, unused):
        cols = pl.ds(pl.multiple_of(g * PAIR, PAIR), PAIR)
        rows = pair_rows(table_ref.at[0], g, pairs)
        turned = rows.T
        x = activate(cols)
        first = lanes(x.shape) < HEADDIM
        start = state[g]
        start_ref[0, g] = start
        inner = nn(cs, start.astype(BF16))
        parts, locals_ = [], []
        for e in range(2):
            for at, to, on in tri_units(False):
                differ = turned[at, e : e + 1] - rows[e : e + 1, to]
                if on:
                    differ = differ + bias[at.start % 128 : at.start % 128 + 64, :]
                decay = jnp.exp(differ)
                scores[e, at, to] = (gram[at, to] * decay * rows[2 + e : 3 + e, to]).astype(BF16)
            parts.append(nn(scores[e], x))
            locals_.append(nn((bs_t * rows[4 + e : 5 + e, :]).astype(BF16), x))
        grow = jnp.where(first, turned[:, 6:7], turned[:, 7:8])
        y_ref[:, cols] = (
            jnp.where(first, parts[0], parts[1]) + grow * inner + skip_ref[:, cols] * x.astype(F32)
        )
        shrink = jnp.where(first[:1], rows[6:7, GROUP - 1 :], rows[7:8, GROUP - 1 :])
        state[g] = shrink * start + jnp.where(first[:STATE], locals_[0], locals_[1])
        return unused

    lax.fori_loop(0, pairs, one, 0, unroll=2)


def run_mix_forward(proj, taps, heads_in, skip, pairs):
    length = proj.shape[0]
    blocks, width = length // GROUP, pairs * PAIR
    core = width + 2 * STATE
    whole = lambda i: (0, 0)
    return pl.pallas_call(
        mix_forward,
        grid=(blocks,),
        in_specs=[
            pl.BlockSpec((GROUP, proj.shape[1]), lambda i: (i, 0)),
            pl.BlockSpec(taps.shape, whole),
            pl.BlockSpec(heads_in.shape, whole),
            pl.BlockSpec(skip.shape, whole),
        ],
        out_specs=[
            pl.BlockSpec((GROUP, core), lambda i: (i, 0)),
            pl.BlockSpec((1, 16 * pairs, 128), lambda i: (i, 0, 0)),
            pl.BlockSpec((GROUP, width), lambda i: (i, 0)),
            pl.BlockSpec((1, pairs, STATE, PAIR), lambda i: (i, 0, 0, 0)),
        ],
        out_shape=[
            jax.ShapeDtypeStruct((length, core), BF16),
            jax.ShapeDtypeStruct((blocks, 16 * pairs, 128), F32),
            jax.ShapeDtypeStruct((length, width), F32),
            jax.ShapeDtypeStruct((blocks, pairs, STATE, PAIR), F32),
        ],
        scratch_shapes=[
            pltpu.VMEM((pairs, STATE, PAIR), F32),
            pltpu.VMEM((HALO, core), F32),
            pltpu.VMEM((GROUP, GROUP), F32),
            pltpu.VMEM((128, 128), F32),
            pltpu.VMEM((2, GROUP, GROUP), BF16),
        ],
        compiler_params=pltpu.CompilerParams(vmem_limit_bytes=VMEM_LIMIT),
        cost_estimate=busy(18, 15),
        name="mix_forward",
    )(proj, taps, heads_in, skip)


def mix_backward(
    top, follows, act_ref, proj_ref, prev_ref, taps_ref, heads_ref, skip_ref, table_ref, start_ref, dy_ref,
    carry_in, halo_in, held_ref, dx_ref, grads_ref, dheads_ref, carried, halo,
    gram, dgram, bias, d_scores, scores, db, dc, found, ends,
):
    pairs = carried.shape[0]
    heads, width = 2 * pairs, pairs * PAIR
    core = width + 2 * STATE
    step = pl.program_id(0)

    @pl.when(step == 0)
    def _():
        carried[...] = carry_in[...] if follows else jnp.zeros_like(carried)
        halo[...] = halo_in[...] if follows else jnp.zeros_like(halo)
        grads_ref[...] = jnp.zeros_like(grads_ref)
        dheads_ref[...] = jnp.zeros_like(dheads_ref)
        scores[...] = jnp.zeros_like(scores)
        bias[...] = diagonal(lambda row, col: row <= col)

    has_prev = jnp.where(top - step > 0, 1.0, 0.0)
    bs, cs = act_ref[:, width : width + STATE], act_ref[:, width + STATE : core]
    bs_float = bs.astype(F32)
    cs_t = cs.astype(F32).T.astype(BF16)
    gram[...] = nt(bs, cs)
    for ref in (dgram, db, dc):
        ref[...] = jnp.zeros_like(ref)

    def conv_back(d_act, cols):
        before = prev_ref[:, cols].astype(F32)[prev_ref.shape[0] - HALO :] * has_prev
        extended = jnp.concatenate([before, proj_ref[:, cols].astype(F32)], axis=0)
        conv = conv_tile(extended, taps_ref, cols)
        sig = sigmoid(conv)
        d_conv = d_act * (sig * (1.0 + conv * (1.0 - sig)))
        onward = jnp.concatenate([d_conv, halo[:, cols]], axis=0)
        d_in = taps_ref[KW - 1 : KW, cols] * d_conv
        for k in range(KW - 1):
            at = KW - 1 - k
            d_in = d_in + taps_ref[k : k + 1, cols] * onward[at : at + GROUP]
        dx_ref[:, cols] = d_in.astype(BF16)
        sums = []
        for k in range(KW):
            at = HALO - KW + 1 + k
            sums.append(jnp.sum(d_conv * extended[at : at + GROUP], axis=0, keepdims=True))
        sums.append(jnp.sum(d_conv, axis=0, keepdims=True))
        sums.append(jnp.zeros((8 - KW - 1, sums[0].shape[1]), F32))
        grads_ref[:, cols] += jnp.concatenate(sums, axis=0)
        halo[:, cols] = d_conv[:HALO]

    def one(g, unused):
        cols = pl.ds(pl.multiple_of(g * PAIR, PAIR), PAIR)
        rows = pair_rows(table_ref.at[0], g, pairs)
        turned = rows.T
        x, dy = act_ref[:, cols], dy_ref[:, cols]
        first = lanes(x.shape) < HEADDIM
        dy_float = dy.astype(F32)
        start, grad = start_ref[0, g], carried[g]
        start_low, grad_low = start.astype(BF16), grad.astype(BF16)
        inner = nn(cs, start_low)
        grow = jnp.where(first, turned[:, 6:7], turned[:, 7:8])
        d_inner = (dy_float * grow).astype(BF16)
        dc[...] += nt(d_inner, start_low)
        touched = dy_float * inner
        held = jnp.sum(grad * start, axis=0, keepdims=True)
        zero = jnp.zeros_like(x)
        reach = nn(bs, grad_low)
        sent = x.astype(F32) * jnp.where(first, turned[:, 4:5], turned[:, 5:6])
        for half in high_low(sent):
            db[...] += nt(half, grad_low)
        parts, sums_j, linked = [], [], []
        for e in range(2):
            own = first if e == 0 else jnp.logical_not(first)
            d_scores[e] = nt(jnp.where(own, x, zero), dy)
            linked_i, linked_j = {}, {}
            for at, to, on in tri_units(True):
                dt_col = turned[at, 2 + e : 3 + e]
                differ = rows[e : e + 1, to] - turned[at, e : e + 1]
                if on:
                    differ = differ + bias[at.start % 128 : at.start % 128 + 64, :]
                decay = jnp.exp(differ)
                grown = gram[at, to] * decay
                d_score = d_scores[e, at, to]
                score = grown * dt_col
                scores[e, at, to] = score.astype(BF16)
                dgram[at, to] += d_score * decay * dt_col
                along_i = d_score * grown
                along_j = jnp.sum(d_score * score, axis=0, keepdims=True)
                key_i, key_j = at.start, to.start
                linked_i[key_i] = along_i if key_i not in linked_i else linked_i[key_i] + along_i
                linked_j[key_j] = along_j if key_j not in linked_j else linked_j[key_j] + along_j
            sums_j.append(jnp.concatenate([linked_j[k] for k in sorted(linked_j)], axis=1))
            linked.append(jnp.concatenate([linked_i[k] for k in sorted(linked_i)], axis=0))
            tail_col = turned[:, 4 + e : 5 + e]
            parts.append(nn(scores[e], dy) + nn((bs_float * tail_col).astype(BF16), grad_low))
        pick = lax.broadcasted_iota(jnp.int32, (8, 2 * PAIR), 0)
        lane = lanes((8, 2 * PAIR))
        by_head = (pick == lane // HEADDIM).astype(BF16)
        by_pair = (pick == 4 + lane // PAIR).astype(BF16)
        kept = jnp.zeros((8, GROUP), F32)
        for sums, select in (
            ((x.astype(F32) * reach, touched), by_head),
            (linked, by_pair),
        ):
            for half in high_low(jnp.concatenate(sums, axis=1)):
                kept = kept + nt(select, half)
        kept = jnp.concatenate([kept[:6]] + sums_j, axis=0)
        found[pl.ds(g, 8, stride=pairs), :] = kept[:, :128]
        found[pl.ds(8 * pairs + g, 8, stride=pairs), :] = kept[:, 128:]
        ends[pl.ds(g, 2, stride=pairs), :] = jnp.concatenate(
            [jnp.where(first[:1], held, 0.0), jnp.where(first[:1], 0.0, held)], axis=0
        )
        conv_back(jnp.where(first, parts[0], parts[1]) + skip_ref[:, cols] * dy_float, cols)
        shrink = jnp.where(first[:1], rows[6:7, GROUP - 1 :], rows[7:8, GROUP - 1 :])
        carried[g] = shrink * grad + nn(cs_t, d_inner)
        return unused

    lax.fori_loop(0, pairs, one, 0, unroll=2)
    low = dgram[...].astype(BF16)
    conv_back(db[...] + nn(low, cs), slice(width, width + STATE))
    conv_back(dc[...] + tn(low, bs), slice(width + STATE, core))

    rows, sums = all_rows(table_ref[0]), all_rows(found[...])
    d_tail, touched, sum_i, sum_j = (sums[k * heads : (k + 1) * heads] for k in range(4))
    cum, dt, tail, growth = (rows[k * heads : (k + 1) * heads] for k in range(4))
    a_neg = heads_ref[heads:, 0:1]
    tail_log = d_tail * tail
    d_last = jnp.sum(tail_log, axis=1, keepdims=True)
    d_last = d_last + jnp.sum(ends[...], axis=1, keepdims=True) * growth[:, GROUP - 1 :]
    d_cum = touched * growth - tail_log + sum_j - dt * sum_i
    d_cum = d_cum + jnp.where(lanes(d_cum.shape) == GROUP - 1, d_last, 0.0)
    d_rate = exact(d_cum, ones_where(lambda row, col: row >= col).astype(F32))
    raw = proj_ref[:, core : core + PAIR].astype(F32).T[:heads]
    d_step = d_tail * jnp.exp(cum[:, GROUP - 1 :] - cum) + sum_i
    d_dt = (d_step + d_rate * a_neg) * sigmoid(raw + heads_ref[:heads, 0:1])
    dheads_ref[:heads, :] += d_dt
    dheads_ref[heads:, :] += d_rate * dt
    filled = jnp.concatenate([d_dt, jnp.zeros((PAIR - heads, GROUP), F32)], axis=0)
    dx_ref[:, core : core + PAIR] = filled.T.astype(BF16)


def run_mix_backward(span, top, act, proj, taps, heads_in, skip, table, starts, dy, before):
    pairs = starts.shape[1]
    follows = before is not None
    held, carry, halo = before if follows else (dy, skip[:, :128], skip[:, :128])
    heads, width = 2 * pairs, pairs * PAIR
    core = width + 2 * STATE
    whole = lambda i: (0, 0)
    block = lambda i: (top - i, 0)
    above = GROUP // 16
    return pl.pallas_call(
        lambda *refs: mix_backward(top, follows, *refs),
        grid=(span,),
        in_specs=[
            pl.BlockSpec((GROUP, core), block),
            pl.BlockSpec((GROUP, proj.shape[1]), block),
            pl.BlockSpec((16, proj.shape[1]), lambda i: (jnp.maximum((top - i) * above - 1, 0), 0)),
            pl.BlockSpec(taps.shape, whole),
            pl.BlockSpec(heads_in.shape, whole),
            pl.BlockSpec(skip.shape, whole),
            pl.BlockSpec((1, 16 * pairs, 128), lambda i: (top - i, 0, 0)),
            pl.BlockSpec((1, pairs, STATE, PAIR), lambda i: (top - i, 0, 0, 0)),
            pl.BlockSpec((GROUP, width), block),
            pl.BlockSpec(carry.shape, lambda i: (0,) * carry.ndim),
            pl.BlockSpec(halo.shape, whole),
            pl.BlockSpec(memory_space=pl.ANY),
        ],
        out_specs=[
            pl.BlockSpec((GROUP, proj.shape[1]), block),
            pl.BlockSpec((8, core), whole),
            pl.BlockSpec((2 * heads, GROUP), whole),
            pl.BlockSpec((pairs, STATE, PAIR), lambda i: (0, 0, 0)),
            pl.BlockSpec((HALO, core), whole),
        ],
        out_shape=[
            jax.ShapeDtypeStruct(proj.shape, BF16),
            jax.ShapeDtypeStruct((8, core), F32),
            jax.ShapeDtypeStruct((2 * heads, GROUP), F32),
            jax.ShapeDtypeStruct((pairs, STATE, PAIR), F32),
            jax.ShapeDtypeStruct((HALO, core), F32),
        ],
        scratch_shapes=[
            pltpu.VMEM((GROUP, GROUP), F32),
            pltpu.VMEM((GROUP, GROUP), F32),
            pltpu.VMEM((128, 128), F32),
            pltpu.VMEM((2, GROUP, GROUP), F32),
            pltpu.VMEM((2, GROUP, GROUP), BF16),
            pltpu.VMEM((GROUP, STATE), F32),
            pltpu.VMEM((GROUP, STATE), F32),
            pltpu.VMEM((8 * heads, 128), F32),
            pltpu.VMEM((heads, PAIR), F32),
        ],
        compiler_params=pltpu.CompilerParams(vmem_limit_bytes=VMEM_LIMIT),
        input_output_aliases={11: 0} if follows else {},
        cost_estimate=busy(12 * span, 5 * span),
        name="mix_backward",
    )(act, proj, proj, taps, heads_in, skip, table, starts, dy, carry, halo, held)


def gate_sums(members_ref, seed_ref, z_ref, y_ref, gain_ref, *refs):
    parts, (w_ref, scaled_ref, sums_ref, squares, along) = refs[:-5], refs[-5:]
    step, n = pl.program_id(0), len(refs[:-5]) - 1

    @pl.when(step == 0)
    def _():
        squares[...] = jnp.zeros_like(squares)
        along[...] = jnp.zeros_like(along)
        places = list(range(n // 2)) + [n // 2] * 2 + list(range(n // 2 + 1, n))
        for k, (o, part) in enumerate(zip(places, parts)):
            at = pl.multiple_of(members_ref[o] * PAIR, PAIR)
            if k == n // 2 + 1:
                at = at + PAIR - part.shape[0]
            w_ref[pl.ds(at, part.shape[0]), :] = part[...]

    tile = z_ref.shape[1]
    scaled = nt(seed_ref[...], w_ref[pl.ds(pl.multiple_of(step * tile, tile), tile), :])
    scaled_ref[...] = scaled
    z = z_ref[...].astype(F32)
    gated = y_ref[...] * (z * sigmoid(z))
    square = gated * gated
    lean = scaled * gain_ref[...] * gated
    for cols in tiles(square.shape[1]):
        squares[...] += square[:, cols]
        along[...] += lean[:, cols]

    @pl.when(step == pl.num_programs(0) - 1)
    def _():
        spot = lanes(squares.shape)
        both = jnp.where(
            spot == 0,
            jnp.sum(squares[...], axis=1, keepdims=True),
            jnp.where(spot == 1, jnp.sum(along[...], axis=1, keepdims=True), 0.0),
        )
        sums_ref[...] = both.T[:8]


def run_gate_sums(members, seed, parts, z, y, gain):
    length, width = y.shape
    tile = 2 * PAIR
    col = pl.BlockSpec((length, tile), lambda i, t: (0, i))
    return pl.pallas_call(
        gate_sums,
        grid_spec=pltpu.PrefetchScalarGridSpec(
            num_scalar_prefetch=1,
            grid=(width // tile,),
            in_specs=[resident(seed, 2), col, col, pl.BlockSpec((1, tile), lambda i, t: (0, i))]
            + [resident(part, 2) for part in parts],
            out_specs=[
                pl.BlockSpec((width, D), lambda i, t: (0, 0)),
                col,
                pl.BlockSpec((8, length), lambda i, t: (0, 0)),
            ],
            scratch_shapes=[pltpu.VMEM((length, PAIR), F32)] * 2,
        ),
        out_shape=[
            jax.ShapeDtypeStruct((width, D), BF16),
            jax.ShapeDtypeStruct(y.shape, F32),
            jax.ShapeDtypeStruct((8, length), F32),
        ],
        compiler_params=pltpu.CompilerParams(vmem_limit_bytes=VMEM_LIMIT),
        cost_estimate=busy(11, 20),
        name="gate_sums",
    )(members, seed, z, y, gain, *parts)


def gate_back(sums_ref, scaled_ref, z_ref, y_ref, x_ref, gain_ref, mixed_ref, dy_ref, dz_ref, cols_ref, turned):
    @pl.when(pl.program_id(0) == 0)
    def _():
        inv = lax.rsqrt(sums_ref[0:1, :] / DI + EPS)
        slope = inv * inv * inv * (sums_ref[1:2, :] / DI)
        rest = jnp.zeros((PAIR - 2, sums_ref.shape[1]), F32)
        both = jnp.concatenate([inv, slope, rest], axis=0).T
        turned[0] = jnp.broadcast_to(both[:, 0:1], turned.shape[1:])
        turned[1] = jnp.broadcast_to(both[:, 1:2], turned.shape[1:])

    inv, slope = turned[0], turned[1]
    z, y, scaled, gain = z_ref[...].astype(F32), y_ref[...], scaled_ref[...], gain_ref[...]
    sig = sigmoid(z)
    silu = z * sig
    gated = y * silu
    normal = gated * inv
    mixed_ref[...] = (normal * gain).astype(BF16)
    d_gated = scaled * gain * inv - gated * slope
    dy = (d_gated * silu).astype(BF16)
    dy_ref[...] = dy
    dz_ref[...] = (d_gated * y * (sig * (1.0 + z * (1.0 - sig)))).astype(BF16)
    cols_ref[0:1, :] = jnp.sum(scaled * normal, axis=0, keepdims=True)
    cols_ref[1:2, :] = jnp.sum(dy.astype(F32) * x_ref[...].astype(F32), axis=0, keepdims=True)
    cols_ref[2:, :] = jnp.zeros_like(cols_ref[2:, :])


def run_gate_back(sums, scaled, z, y, x, gain):
    length, width = y.shape
    tile = PAIR
    col = pl.BlockSpec((length, tile), lambda i: (0, i))
    low = jax.ShapeDtypeStruct(y.shape, BF16)
    return pl.pallas_call(
        gate_back,
        grid=(width // tile,),
        in_specs=[
            pl.BlockSpec(sums.shape, lambda i: (0, 0)),
            col,
            col,
            col,
            col,
            pl.BlockSpec((1, tile), lambda i: (0, i)),
        ],
        out_specs=[col, col, col, pl.BlockSpec((8, tile), lambda i: (0, i))],
        out_shape=[low, low, low, jax.ShapeDtypeStruct((8, width), F32)],
        scratch_shapes=[pltpu.VMEM((2, length, PAIR), F32)],
        compiler_params=pltpu.CompilerParams(vmem_limit_bytes=VMEM_LIMIT),
        cost_estimate=busy(11, 20),
        name="gate_back",
    )(sums, scaled, z, y, x, gain)


def keep_or_give(place_ref, value, keep_ref, give_ref):
    mine = place_ref[0] % 2 == pl.program_id(0) % 2

    @pl.when(mine)
    def _():
        keep_ref[0] = value

    @pl.when(jnp.logical_not(mine))
    def _():
        give_ref[0] = value


def back_norm(members_ref, place_ref, tokens_ref, dz_ref, dx_ref, *refs):
    parts, (keep_ref, give_ref, gain_ref, dn_ref) = refs[:-4], refs[-4:]
    count = len(parts) // 2

    @pl.when(pl.program_id(0) == 0)
    def _():
        gain_ref[...] = jnp.zeros_like(gain_ref)

    tokens = tokens_ref[...].astype(F32)
    inv = lax.rsqrt(jnp.mean(tokens * tokens, axis=-1, keepdims=True) + EPS)
    sums = [None] * (D // SEG)
    for source, weights in ((dz_ref, parts[:count]), (dx_ref, parts[count:])):
        for o, at, w in by_segments(weights):
            part = nn(source[:, at : at + w.shape[0]], w[...])
            sums[o] = part if sums[o] is None else sums[o] + part
    for o, d_normed in enumerate(sums):
        at = pl.multiple_of(members_ref[o] * SEG, SEG)
        dn_ref[:, pl.ds(at, SEG)] = d_normed.astype(BF16)
        scaled = tokens_ref[:, pl.ds(at, SEG)].astype(F32) * inv
        gain_ref[0:1, pl.ds(at, SEG)] += jnp.sum(d_normed * scaled, axis=0, keepdims=True)
    keep_or_give(place_ref, dn_ref[...], keep_ref, give_ref)


def run_back_norm(members, place, tokens, dz, dx, weights_z, weights_x):
    length = tokens.shape[0]
    row = lambda i, t, p: (i, 0)
    half = pl.BlockSpec((1, GROUP, D), lambda i, t, p: (i // 2, 0, 0))
    halves_shape = jax.ShapeDtypeStruct((length // GROUP // 2, GROUP, D), BF16)
    return pl.pallas_call(
        back_norm,
        grid_spec=pltpu.PrefetchScalarGridSpec(
            num_scalar_prefetch=2,
            grid=(length // GROUP,),
            in_specs=[
                pl.BlockSpec((GROUP, D), row),
                pl.BlockSpec((GROUP, dz.shape[1]), row),
                pl.BlockSpec((GROUP, dx.shape[1]), row),
            ]
            + [resident(w, 3) for w in weights_z + weights_x],
            out_specs=[half, half, pl.BlockSpec((8, D), lambda i, t, p: (0, 0))],
            scratch_shapes=[pltpu.VMEM((GROUP, D), BF16)],
        ),
        out_shape=[halves_shape, halves_shape, jax.ShapeDtypeStruct((8, D), F32)],
        compiler_params=pltpu.CompilerParams(vmem_limit_bytes=VMEM_LIMIT),
        cost_estimate=busy(18, 24),
        name="back_norm",
    )(members, place, tokens, dz, dx, *weights_z, *weights_x)


def assemble_o(place_ref, o0, o1, o2, o3, out_ref):
    for k, ref in enumerate((o0, o1, o2, o3)):

        @pl.when(pl.program_id(0) == k)
        def _():
            out_ref[...] = ref[...].astype(F32)


def run_assemble_o(place, shares):
    m, (rows, cols) = len(shares), shares[0].shape
    return pl.pallas_call(
        assemble_o,
        grid_spec=pltpu.PrefetchScalarGridSpec(
            num_scalar_prefetch=1,
            grid=(m,),
            in_specs=[resident(share, 2) for share in shares],
            out_specs=pl.BlockSpec((rows, cols), lambda i, t: (t[0] ^ i, 0)),
        ),
        out_shape=jax.ShapeDtypeStruct((m * rows, cols), F32),
        compiler_params=pltpu.CompilerParams(vmem_limit_bytes=VMEM_LIMIT),
        cost_estimate=busy(3, 3),
        name="assemble_o",
    )(place, *shares)


def put_pairs(place_ref, refs, out_ref, g):
    m = len(refs)
    for k, ref in enumerate(refs):
        to = pl.multiple_of((place_ref[0] ^ k) * PAIR, PAIR)
        out_ref[pl.ds(to, PAIR), :] = ref[pl.ds(pl.multiple_of(g * PAIR, PAIR), PAIR), :].astype(F32)


def assemble_z(place_ref, z0, z1, z2, z3, out_ref):
    put_pairs(place_ref, (z0, z1, z2, z3), out_ref, pl.program_id(0))


def assemble_a(place_ref, held_ref, a0, a1, a2, a3, out_ref):
    put_pairs(place_ref, (a0, a1, a2, a3), out_ref, pl.program_id(0))


def assemble_b(place_ref, order_ref, held_ref, b0, b1, b2, b3, out_ref):
    step, last = pl.program_id(0), pl.num_programs(0) - 1
    refs = (b0, b1, b2, b3)
    width = last * PAIR
    core = width + 2 * STATE

    @pl.when(step < last)
    def _():
        put_pairs(place_ref, refs, out_ref, step)

    @pl.when(step == last)
    def _():
        total = jnp.zeros((2 * STATE, out_ref.shape[1]), F32)
        steps = jnp.zeros((HEADS, out_ref.shape[1]), F32)
        for k, x in enumerate(refs):
            total = total + x[width:core].astype(F32)
            steps = steps + nn(order_ref[place_ref[0] ^ k], x[core : core + TAIL])
        out_ref[: 2 * STATE] = total
        out_ref[2 * STATE : 2 * STATE + HEADS] = steps


def run_assemble_z(place, shares, columns):
    m, rows = len(shares), shares[0].shape[1]
    tile = m * PAIR
    return pl.pallas_call(
        assemble_z,
        grid_spec=pltpu.PrefetchScalarGridSpec(
            num_scalar_prefetch=1,
            grid=(DI // tile,),
            in_specs=[resident(s, 2) for s in shares],
            out_specs=pl.BlockSpec((tile, rows), lambda i, t: (i, 0)),
        ),
        out_shape=jax.ShapeDtypeStruct((columns, rows), F32),
        compiler_params=pltpu.CompilerParams(vmem_limit_bytes=VMEM_LIMIT),
        cost_estimate=busy(4, 6),
        name="assemble_z",
    )(place, *shares)


def run_assemble_b(place, order, held, shares, count):
    m, rows = len(shares), shares[0].shape[1]
    tile = m * PAIR
    first = 2 * (DI // tile) - count
    return pl.pallas_call(
        assemble_b,
        grid_spec=pltpu.PrefetchScalarGridSpec(
            num_scalar_prefetch=1,
            grid=(count + 1,),
            in_specs=[resident(order, 2), pl.BlockSpec(memory_space=pl.ANY)]
            + [resident(s, 2) for s in shares],
            out_specs=pl.BlockSpec((tile, rows), lambda i, t: (i + first, 0)),
        ),
        out_shape=jax.ShapeDtypeStruct(held.shape, F32),
        input_output_aliases={2: 0},
        compiler_params=pltpu.CompilerParams(vmem_limit_bytes=VMEM_LIMIT),
        cost_estimate=busy(3, 2),
        name="assemble_b",
    )(place, order, held, *shares)


def run_assemble_a(place, held, shares):
    m, rows = len(shares), shares[0].shape[1]
    tile = m * PAIR
    return pl.pallas_call(
        assemble_a,
        grid_spec=pltpu.PrefetchScalarGridSpec(
            num_scalar_prefetch=1,
            grid=(shares[0].shape[0] // PAIR,),
            in_specs=[pl.BlockSpec(memory_space=pl.ANY)] + [resident(s, 2) for s in shares],
            out_specs=pl.BlockSpec((tile, rows), lambda i, t: (i + DI // tile, 0)),
        ),
        out_shape=jax.ShapeDtypeStruct(held.shape, F32),
        input_output_aliases={1: 0},
        compiler_params=pltpu.CompilerParams(vmem_limit_bytes=VMEM_LIMIT),
        cost_estimate=busy(4, 5),
        name="assemble_a",
    )(place, held, *shares)


def body(
    tokens, norm_gain, w_in, conv_w, conv_b, dt_bias, a_log, d_skip, gate_gain, w_out, cotangent
):
    n, m = lax.axis_size("fsdp"), lax.axis_size("ctx")
    place = lax.axis_index("ctx")
    piece = tokens.shape[1]
    length = piece * m
    blocks = length // GROUP
    pairs = DI // PAIR // m
    width = pairs * PAIR
    heads = 2 * pairs
    rows = w_in.shape[0]
    core_cols = width + 2 * STATE
    head_cols = core_cols + heads
    ring = rows == SEG and (DI // PAIR) // n == m

    def of_pairs(array, axis):
        shape = array.shape
        each = shape[axis] // (pairs * m)
        split = array.reshape(shape[:axis] + (pairs, m, each) + shape[axis + 1 :])
        mine = lax.dynamic_index_in_dim(split, place, axis + 1, False)
        return mine.reshape(shape[:axis] + (pairs * each,) + shape[axis + 1 :])

    def of_heads(array):
        mine = of_pairs(array, 0)
        split = mine.reshape((pairs, 2) + mine.shape[1:]).swapaxes(0, 1)
        return split.reshape(mine.shape)

    all_tokens = lax.all_gather(tokens[0], "ctx", axis=0, tiled=True)
    seed = lax.all_gather(cotangent[0], "ctx", axis=0, tiled=True)


    columns = w_in.T
    total_cols = core_cols + PAIR
    cut = halves(total_cols)[0]
    place_ref = place.reshape(1).astype(jnp.int32)
    smalls = [norm_gain[None], gate_gain[None], conv_b[None], conv_w]
    small_rows = [-(-v.shape[1] // SEG) for v in smalls]

    def split(whole):
        upper, _ = halves(whole.shape[0])
        parts = [whole[:, o * SEG : (o + 1) * SEG] for o in range(D // SEG)]
        middle = parts[len(parts) // 2]
        return parts[: len(parts) // 2] + [middle[:upper], middle[upper:]] + parts[len(parts) // 2 + 1 :]

    if ring:
        me = ring_place(lax.axis_index("fsdp"), n)
        members = ring_member(me + jnp.arange(n), n).astype(jnp.int32)
        padded = [jnp.pad(v, ((0, 0), (0, k * SEG - v.shape[1]))) for v, k in zip(smalls, small_rows)]
        small = jnp.concatenate([v.reshape(-1) for v in padded]).reshape(-1, SEG)
        block_x, block_z, block_o = run_pack(place_ref, columns, w_out, small, pairs)
        ring_x, ring_z, ring_o = Gather(block_x, n), Gather(block_z, n), Gather(block_o, n)
        next_hop([ring_x], ())
        dt_bias, a_log, d_skip = next_hop([ring_x], (dt_bias, a_log, d_skip))
        for _ in range(n // 2 - 4):
            next_hop([ring_x], ())
        next_hop([ring_x, ring_z], ())
        next_hop([ring_x], (), *arrivals(ring_z))
        parts_x = ring_x.parts()
        all_tokens, members_late, parts_late = next_hop(
            [ring_z, ring_o], (all_tokens, members, parts_x), *arrivals(ring_x)
        )
    else:
        members = jnp.arange(D // SEG, dtype=jnp.int32)
        block_x = jnp.concatenate(
            [
                of_pairs(columns[DI : 2 * DI], 0),
                columns[2 * DI : 2 * DI + 2 * STATE],
                of_heads(columns[DI + CONV :]),
                jnp.zeros((PAIR - heads, rows), BF16),
            ],
            axis=0,
        )
        whole_x = lax.all_gather(block_x, "fsdp", axis=1, tiled=True)
        norm_whole = lax.all_gather(norm_gain[None], "fsdp", axis=1, tiled=True)
        at = core_cols + SMALL
        whole_x = jnp.concatenate([whole_x[:at], norm_whole, whole_x[at + 1 :]], axis=0)
        parts_x, parts_z = split(whole_x), split(lax.all_gather(of_pairs(columns[:DI], 0), "fsdp", axis=1, tiled=True))
        w_o = of_pairs(lax.all_gather(w_out, "fsdp", axis=0, tiled=True), 0)
        parts_o = [w_o[o * PAIR : (o + 1) * PAIR] for o in range(pairs)]
        middle, upper = parts_o[pairs // 2], halves(PAIR)[0]
        parts_o = parts_o[: pairs // 2] + [middle[:upper], middle[upper:]] + parts_o[pairs // 2 + 1 :]

    if ring:
        kept = run_collect(members_late, parts_late)
        spans, at = [], 0
        for v, each in zip(smalls, small_rows):
            here = kept[:, at : at + v.shape[0] * each].reshape(n, v.shape[0], each * SEG)
            spans.append(here[:, :, : v.shape[1]].transpose(1, 0, 2).reshape(v.shape[0], -1))
            at += v.shape[0] * each
        norm_full, gate_full, bias_full, taps_full = spans
    else:
        norm_full, gate_full, bias_full, taps_full = (
            lax.all_gather(v, "fsdp", axis=1, tiled=True).astype(F32) for v in smalls
        )
    gate_full = of_pairs(gate_full, 1)
    taps_full = jnp.concatenate([taps_full, bias_full], axis=0)
    taps = jnp.concatenate([of_pairs(taps_full[:, :DI], 1), taps_full[:, DI:]], axis=1)
    taps = jnp.pad(taps, ((0, 8 - KW - 1), (0, 0)))

    dt_bias_own, a_log_own = of_heads(dt_bias), of_heads(a_log)
    skip_own = of_pairs(d_skip, 0)
    a_neg = -jnp.exp(a_log_own)
    heads_in = jnp.broadcast_to(jnp.concatenate([dt_bias_own, a_neg])[:, None], (2 * heads, 128))
    skip_row = jnp.repeat(skip_own, HEADDIM)[None, :]

    normed, proj_x = run_front(members, all_tokens, parts_x)
    if ring:
        proj_x = next_hop([ring_z, ring_o], proj_x, *arrivals(ring_z, ring_o))
    act, table, ssd, starts = run_mix_forward(proj_x, taps, heads_in, skip_row, pairs)
    normed_z = normed
    if ring:
        for _ in range(n // 2 - 3):
            next_hop([ring_z, ring_o], (), ssd, *arrivals(ring_z, ring_o))
        normed_z = next_hop([ring_o], normed, *arrivals(ring_z))
        parts_z, parts_o = ring_z.parts(), ring_o.parts()
    proj_z = run_project(normed_z, parts_z)

    w_o, scaled, sums = run_gate_sums(members, seed, parts_o, proj_z, ssd, gate_full)
    sums = ctx_sum(sums, m)
    mixed, dy, d_z, gate_cols = run_gate_back(sums, scaled, proj_z, ssd, act, gate_full)

    grads_o = tn(mixed, seed).astype(BF16)
    conv_grads, head_grads, top, before = [], [], blocks - 1, None
    d_z_late, mixed_late = d_z, mixed
    if ring:
        sum_o = Reduce(lambda o: lax.dynamic_slice_in_dim(grads_o, members[o] * PAIR, PAIR, 0), n)
        d_z_late, mixed_late = next_hop([sum_o], (d_z, mixed))
    grads_z = tn(d_z_late, normed).astype(BF16)
    branch = nn(mixed_late, w_o).astype(BF16)
    if ring:
        sum_z = Reduce(lambda o: grads_z[:, o * SEG : (o + 1) * SEG], n)
    for at in range(2):
        if ring:
            sum_o.join()
            if at > 0:
                sum_z.join()
                branch_own.middle()
                dy, before, branch_own.sent = next_hop(
                    [sum_o, sum_z], (dy, before, branch_own.sent)
                )
                branch_own.send_far()
            else:
                dy, branch = next_hop([sum_o, sum_z], (dy, branch))
                branch_own = CtxReduce(*by_core(branch.reshape(m, piece, D), m), m)
        span = blocks // 2
        d_x, conv_part, head_part, *before = run_mix_backward(
            span, top, act, proj_x, taps, heads_in, skip_row, table, starts, dy, before
        )
        before = (d_x, *before)
        conv_grads.append(conv_part)
        head_grads.append(head_part)
        top -= span
    normed_late = normed
    if ring:
        sum_o.join()
        sum_z.join()
        d_x, normed_late, branch_own.far = next_hop(
            [sum_o, sum_z], (d_x, normed, branch_own.far)
        )
    else:
        branch_own = CtxReduce(*by_core(branch.reshape(m, piece, D), m), m)
        branch_own.middle()
        branch_own.send_far()
    grads_x = tn(d_x, normed_late).astype(BF16)
    kept, given, d_gain = run_back_norm(
        members, place_ref, all_tokens, d_z, after(d_x, grads_x), parts_z, parts_x
    )
    small = run_gather_small(conv_grads, head_grads, gate_cols, d_gain)
    if ring:
        used = core_cols + TAIL
        sum_x = Reduce(
            lambda o: grads_x[:used, o * SEG : (o + 1) * SEG], n, run_cut(grads_x, used, n // 2)
        )
        part_o = sum_o.join().astype(BF16)
        sum_z.join()
        kept, given, small, part_o, branch_own.far = next_hop(
            [sum_x, sum_z], (kept, given, small, part_o, branch_own.far)
        )
    flip = 1
    steps = []
    while flip < n:
        steps.append(flip)
        flip *= 2

    def small_step(small):
        if steps:
            small = small + lax.ppermute(small, "fsdp", ctx_route(n, steps.pop()))
        return small

    d_own = CtxReduce(kept, given, m)
    d_own.middle()
    d_own.send_far()
    small = small_step(small)
    if ring:
        sum_x.join()
        part_z = sum_z.join().astype(BF16)
        d_own.far, small, part_o, part_z, branch_own.far = next_hop(
            [sum_x], (d_own.far, small, part_o, part_z, branch_own.far)
        )
        other_o = far_share(part_o, m)
    small = small_step(small)
    output = (tokens[0].astype(F32) + branch_own.total()).astype(BF16)[None]
    if ring:
        sum_x.join()
        small, other_o, part_z, d_own.far = next_hop(
            [sum_x], (small, other_o, part_z, d_own.far), output
        )
        shares_o, other_z = near_share(part_o, other_o, m), far_share(part_z, m)
        grad_w_out = run_assemble_o(place_ref, shares_o)
    small = small_step(small)
    own = tokens[0].astype(F32)
    inv = lax.rsqrt(jnp.mean(own * own, axis=-1, keepdims=True) + EPS)
    d_direct = d_own.total() * norm_full
    along = jnp.mean(d_direct * own, axis=-1, keepdims=True)
    grad_tokens = (cotangent[0].astype(F32) + d_direct * inv - own * (inv * inv * inv * along))[None]
    if ring:
        for at in range(n // 2 - 3):
            sum_x.join()
            small, part_z, other_z = next_hop(
                [sum_x], (small, part_z, other_z), grad_tokens, grad_w_out
            )
        shares_z = near_share(part_z, other_z, m)
        held = run_assemble_z(place_ref, shares_z, w_in.shape[1])
    while steps:
        small = small_step(small)
    smalls_of = ctx_share(small, m)
    if ring:
        part_x = sum_x.join().astype(BF16)
        part_a, part_b = part_x[:cut], part_x[cut:]
        part_a, part_b, smalls_of = barrier((part_a, part_b, smalls_of))
    by_place = jnp.zeros((m,) + small.shape, F32)
    for k in range(m):
        by_place = lax.dynamic_update_slice(by_place, smalls_of[k][None], (place ^ k, 0, 0))

    mine = lax.axis_index("fsdp")
    lines = [core_cols] * (KW + 1) + [width, width, D]
    found, at = [], 0
    for count in lines:
        found.append(by_place[:, at : at + count // SEG].reshape(m, 1, count))
        at += count // SEG
    conv_lines = jnp.concatenate(found[: KW + 1], axis=1)

    def interleaved(lines):
        return lines.reshape(m, -1, pairs, PAIR).transpose(1, 2, 0, 3).reshape(-1, DI)

    whole = jnp.concatenate(
        [interleaved(conv_lines[:, :, :width]), jnp.sum(conv_lines[:, :, width:], axis=0)], axis=1
    )
    each = conv_b.shape[0]
    grad_conv = lax.dynamic_slice_in_dim(whole, mine * each, each, 1)
    each = gate_gain.shape[0]
    grad_gate_gain = lax.dynamic_slice_in_dim(interleaved(found[KW + 1]), mine * each, each, 1)[0]
    grad_gain = lax.dynamic_slice_in_dim(jnp.sum(found[KW + 3], axis=0)[0], mine * rows, rows, 0)
    skips = jnp.sum(found[KW + 2].reshape(m, pairs, 2, HEADDIM), axis=3).reshape(m, 1, pairs, 2)
    of_steps = jnp.sum(by_place[:, by_place.shape[1] - 2 * heads :], axis=2)
    of_steps = of_steps.reshape(m, 2, 2, pairs).transpose(0, 1, 3, 2)
    per_head = jnp.concatenate([of_steps, skips], axis=1).transpose(1, 2, 0, 3).reshape(3, HEADS)
    grad_a_log = per_head[1] * -jnp.exp(a_log)
    if not ring:
        part_z = lax.psum_scatter(grads_z.astype(F32), "fsdp", scatter_dimension=1, tiled=True)
        part_x = lax.psum_scatter(grads_x.astype(F32), "fsdp", scatter_dimension=1, tiled=True)
        whole_o = jnp.zeros((pairs, m, PAIR, D), F32)
        whole_o = lax.dynamic_update_index_in_dim(
            whole_o, grads_o.astype(F32).reshape(pairs, PAIR, D), place, 1
        )
        grad_w_out = lax.psum_scatter(whole_o.reshape(DI, D), "fsdp", scatter_dimension=0, tiled=True)
        grad_w_out = lax.psum(grad_w_out, "ctx")
        held = run_assemble_z(place_ref, ctx_share(part_z.astype(BF16), m), w_in.shape[1])
        part_x = part_x.astype(BF16)
        part_a, part_b = part_x[:cut], part_x[cut : core_cols + TAIL]
    other_b, other_a = far_share(part_b, m), far_share(part_a, m)
    order = np.zeros((m, HEADS, TAIL), np.float32)
    for member in range(m):
        for h in range(heads):
            order[member, (h % pairs) * 2 * m + 2 * member + h // pairs, h] = 1.0
    shares_b = near_share(part_b, other_b, m)
    held = run_assemble_b(place_ref, jnp.asarray(order, BF16), held, shares_b, pairs - cut // PAIR)
    shares_a = near_share(part_a, other_a, m)
    grad_w_in = run_assemble_a(place_ref, held, shares_a)
    return (
        output,
        grad_tokens,
        grad_gain,
        grad_w_in.T,
        grad_conv[:KW],
        grad_conv[KW],
        per_head[0],
        grad_a_log,
        per_head[2],
        grad_gate_gain,
        grad_w_out,
    )


def solution(mesh):
    in_specs = (
        P("fsdp", "ctx", None),
        P("fsdp"),
        P("fsdp", None),
        P(None, "fsdp"),
        P("fsdp"),
        P(),
        P(),
        P(),
        P("fsdp"),
        P("fsdp", None),
        P("fsdp", "ctx", None),
    )
    out_specs = (
        P("fsdp", "ctx", None),
        P("fsdp", "ctx", None),
        P("fsdp"),
        P("fsdp", None),
        P(None, "fsdp"),
        P("fsdp"),
        P(),
        P(),
        P(),
        P("fsdp"),
        P("fsdp", None),
    )
    return jax.shard_map(body, mesh=mesh, in_specs=in_specs, out_specs=out_specs, check_vma=False)
```

```python
import jax
import jax.numpy as jnp
import numpy as np
from jax import lax
from jax.experimental import pallas as pl
from jax.experimental.pallas import tpu as pltpu
from jax.sharding import PartitionSpec as P

D = 2048
HEADS = 64
HEADDIM = 64
STATE = 128
KW = 4
GROUP = 256
DI = HEADS * HEADDIM
CONV = DI + 2 * STATE
PAIR = 2 * HEADDIM
EPS = 1e-05
SEG = 256
HALO = 8
SMALL = 32
TAIL = 32
ENDS = 64
VMEM_LIMIT = 56 * 1024 * 1024
F32 = jnp.float32
BF16 = jnp.bfloat16


def ring_place(index, n):
    return jnp.where(index % 2 == 0, index // 2, n - 1 - index // 2)


def ring_member(place, n):
    place = place % n
    return jnp.where(place < n // 2, 2 * place, 2 * (n - 1 - place) + 1)


def ring_routes(n):
    order = [2 * p if p < n // 2 else 2 * (n - 1 - p) + 1 for p in range(n)]
    forward = [(order[p], order[(p + 1) % n]) for p in range(n)]
    return forward, [(b, a) for a, b in forward]


def send(block, route):
    return lax.ppermute(block, "fsdp", route)


def after(value, *earlier):
    return lax.optimization_barrier((value, *earlier))[0]


def halves(rows):
    upper = -(-rows // 256) * 128 if rows >= 512 else rows // 2
    return upper, rows - upper


class Gather:
    def __init__(self, block, n):
        self.forward, self.backward = ring_routes(n)
        self.block, self.n = block, n
        self.latest = (block, block)
        self.ahead, self.behind = [], []

    def load(self):
        right, left = self.latest
        if len(self.ahead) == self.n // 2 - 1:
            upper, _ = halves(self.block.shape[0])
            return right[:upper], left[upper:]
        return right, left

    def fire(self, right, left):
        last = len(self.ahead) == self.n // 2 - 1
        self.latest = send(right, self.forward), send(left, self.backward)
        if not last:
            self.behind.insert(0, self.latest[0])
            self.ahead.append(self.latest[1])

    def parts(self):
        return [self.block] + self.ahead + list(self.latest) + self.behind


class Reduce:
    def __init__(self, chunk, n, pieces=None):
        self.forward, self.backward = ring_routes(n)
        self.chunk, self.n, self.step = chunk, n, n // 2
        if pieces is None:
            first = chunk(n // 2).astype(BF16)
            upper, _ = halves(first.shape[0])
            pieces = first[:upper], first[upper:]
        self.right, self.left = pieces
        self.upper = self.right.shape[0]

    def load(self):
        return self.right, self.left

    def fire(self, right, left):
        self.latest = send(right, self.forward), send(left, self.backward)
        self.step -= 1

    def join(self):
        right, left = (part.astype(F32) for part in self.latest)
        if self.step == 0:
            return self.chunk(0).astype(F32) + right + left
        own_right = self.chunk(self.step).astype(F32)
        own_left = self.chunk(self.n - self.step).astype(F32)
        cut = self.upper
        if self.step == self.n // 2 - 1:
            right = jnp.concatenate([own_right[:cut] + right, own_right[cut:]], axis=0)
            left = jnp.concatenate([own_left[:cut], own_left[cut:] + left], axis=0)
        else:
            right, left = own_right + right, own_left + left
        self.right, self.left = right.astype(BF16), left.astype(BF16)


def cut_in_two(grads_ref, right_ref, left_ref):
    upper = right_ref.shape[0]
    right_ref[...] = grads_ref[:upper]
    left_ref[...] = grads_ref[upper:]


def run_cut(grads, rows, block):
    shapes = [(half, SEG) for half in halves(rows)]
    return pl.pallas_call(
        cut_in_two,
        grid=(1,),
        in_specs=[pl.BlockSpec((rows, SEG), lambda i: (0, block))],
        out_specs=[pl.BlockSpec(shape, lambda i: (0, 0)) for shape in shapes],
        out_shape=[jax.ShapeDtypeStruct(shape, BF16) for shape in shapes],
        cost_estimate=busy(1, 1),
        name="cut_in_two",
    )(grads)


def barrier(value, *earlier):
    return lax.optimization_barrier((value, earlier))[0]


def next_hop(rings, inputs, *earlier):
    loads, inputs = barrier(([ring.load() for ring in rings], inputs), *earlier)
    for ring, load in zip(rings, loads):
        ring.fire(*load)
    return inputs


def arrivals(*rings):
    return sum((ring.latest for ring in rings), ())


def ctx_route(m, flip):
    return [(i, i ^ flip) for i in range(m)]


def far_share(block, m):
    return lax.ppermute(block, "ctx", ctx_route(m, 2))


def near_share(block, other, m):
    near = lax.ppermute(block, "ctx", ctx_route(m, 1))
    far = lax.ppermute(other, "ctx", ctx_route(m, 1))
    return [block, near, other, far]


def ctx_share(block, m):
    return near_share(block, far_share(block, m), m)


def gather_small(conv0, conv1, heads0, heads1, gate_ref, gain_ref, out_ref):
    out_ref[...] = jnp.zeros_like(out_ref)
    lines = [(conv0, k, conv1) for k in range(KW + 1)]
    lines += [(gate_ref, 0, None), (gate_ref, 1, None), (gain_ref, 0, None)]
    at = 0
    for ref, row, other in lines:
        for start in range(0, ref.shape[1], SEG):
            line = ref[row : row + 1, start : start + SEG]
            if other is not None:
                line = line + other[row : row + 1, start : start + SEG]
            out_ref[at : at + 1, :] = line
            at += 1
    at = out_ref.shape[0] - heads0.shape[0]
    out_ref[at:, :] = heads0[...] + heads1[...]


def run_gather_small(conv_grads, head_grads, gate_cols, d_gain):
    arrays = [*conv_grads, *head_grads, gate_cols, d_gain]
    lines = (KW + 1) * conv_grads[0].shape[1] + 2 * gate_cols.shape[1] + d_gain.shape[1]
    rows = -(-lines // SEG // 8) * 8 + head_grads[0].shape[0]
    return pl.pallas_call(
        gather_small,
        grid=(1,),
        in_specs=[pl.BlockSpec(v.shape, lambda i: (0, 0)) for v in arrays],
        out_specs=pl.BlockSpec((rows, SEG), lambda i: (0, 0)),
        out_shape=jax.ShapeDtypeStruct((rows, SEG), F32),
        cost_estimate=busy(1, 1),
        name="gather_small",
    )(*arrays)


class CtxReduce:
    def __init__(self, kept, given, m):
        self.m, place = m, lax.axis_index("ctx")
        self.core, self.across = place % 2, place // 2
        self.kept = kept
        self.near = lax.ppermute(given, "ctx", ctx_route(m, 1))

    def middle(self):
        self.both = self.kept.astype(F32) + self.near.astype(F32)
        self.sent = lax.dynamic_index_in_dim(self.both, 1 - self.across, 0, False).astype(BF16)

    def send_far(self):
        self.far = lax.ppermute(self.sent, "ctx", ctx_route(self.m, 2))

    def total(self):
        return lax.dynamic_index_in_dim(self.both, self.across, 0, False) + self.far.astype(F32)


def by_core(share, m):
    core = lax.axis_index("ctx") % 2
    split = share.reshape((m // 2, 2) + share.shape[1:])
    return (
        lax.dynamic_index_in_dim(split, core, 1, False),
        lax.dynamic_index_in_dim(split, 1 - core, 1, False),
    )


def ctx_sum(values, m):
    near, across, far = (lax.ppermute(values, "ctx", ctx_route(m, flip)) for flip in (1, 2, 3))
    return (values + near) + (across + far)


def nt(a, b):
    return lax.dot_general(a, b, (((1,), (1,)), ((), ())), preferred_element_type=F32)


def nn(a, b):
    return lax.dot_general(a, b, (((1,), (0,)), ((), ())), preferred_element_type=F32)


def tn(a, b):
    return lax.dot_general(a, b, (((0,), (0,)), ((), ())), preferred_element_type=F32)


def lanes(shape):
    return lax.broadcasted_iota(jnp.int32, shape, len(shape) - 1)


def busy(us, megabytes):
    return pl.CostEstimate(
        flops=int(us * 1e9), transcendentals=0, bytes_accessed=int(megabytes * 1e6)
    )


def softplus(v):
    return jnp.maximum(v, 0.0) + jnp.log1p(jnp.exp(-jnp.abs(v)))


def sigmoid(v):
    return 1.0 / (1.0 + jnp.exp(-v))


def ones_where(keep):
    row = lax.broadcasted_iota(jnp.int32, (GROUP, GROUP), 0)
    col = lax.broadcasted_iota(jnp.int32, (GROUP, GROUP), 1)
    return keep(row, col)


def exact(a, b):
    return lax.dot_general(
        a, b, (((1,), (0,)), ((), ())), preferred_element_type=F32, precision=lax.Precision.HIGHEST
    )


def tiles(width):
    return [slice(at, at + PAIR) for at in range(0, width, PAIR)]


def conv_tile(extended, taps_ref, cols):
    total = taps_ref[KW : KW + 1, cols]
    for k in range(KW):
        at = HALO - KW + 1 + k
        total = total + taps_ref[k : k + 1, cols] * extended[at : at + GROUP]
    return total


def by_segments(weights):
    n = D // SEG
    places = list(range(n // 2)) + [n // 2] * 2 + list(range(n // 2 + 1, n))
    at = [0] * len(places)
    at[n // 2 + 1] = weights[n // 2].shape[0]
    return list(zip(places, at, weights))


def project_into(out_ref, normed_ref, weights, total):
    whole = None
    for o, at, w in by_segments(weights):
        part = nt(normed_ref[:, o * SEG : (o + 1) * SEG], w[...])
        if o == D // SEG // 2:
            total[:, at : at + w.shape[0]] = part
        else:
            whole = part if whole is None else whole + part
    out_ref[...] = (whole + total[...]).astype(BF16)


def pack(
    place_ref, columns_ref, out_ref, small_ref, x_ref, z_ref, o_ref, steps, rows, sems,
):
    place = place_ref[0]
    pairs, m = z_ref.shape[0] // PAIR, out_ref.shape[0] // PAIR
    core = pairs * PAIR + 2 * STATE
    copies = [
        (columns_ref.at[pl.ds(DI + CONV, HEADS)], steps),
        (columns_ref.at[pl.ds(2 * DI, 2 * STATE)], x_ref.at[pl.ds(pairs * PAIR, 2 * STATE)]),
        (out_ref.at[pl.ds(pl.multiple_of(place * PAIR, PAIR), PAIR)], o_ref),
    ]
    for g in range(pairs):
        here = pl.ds(g * PAIR, PAIR)
        for start, ref in ((DI, x_ref), (0, z_ref)):
            at = pl.multiple_of(start + (g * m + place) * PAIR, PAIR)
            copies.append((columns_ref.at[pl.ds(at, PAIR)], ref.at[here]))
    copies = [pltpu.make_async_copy(*pair, sems.at[k]) for k, pair in enumerate(copies)]
    for copy in copies:
        copy.start()
    rows[...] = jnp.zeros_like(rows)
    rows[SMALL : SMALL + small_ref.shape[0], :] = small_ref[...].astype(F32)
    copies[0].wait()
    want = lax.broadcasted_iota(jnp.int32, (2 * pairs, HEADS), 0)
    have = lax.broadcasted_iota(jnp.int32, (2 * pairs, HEADS), 1)
    head = (want % pairs) * 2 * m + 2 * place + want // pairs
    rows[: 2 * pairs, :] = nn((have == head).astype(BF16), steps[...])
    x_ref[core : core + ENDS, :] = rows[...].astype(BF16)
    for copy in copies[1:]:
        copy.wait()


def run_pack(place, columns, w_out, small, pairs):
    rows = columns.shape[1]
    core = pairs * PAIR + 2 * STATE
    anywhere = pl.BlockSpec(memory_space=pl.ANY)
    shapes = [(core + ENDS, rows), (pairs * PAIR, rows), (PAIR, D)]
    return pl.pallas_call(
        pack,
        grid_spec=pltpu.PrefetchScalarGridSpec(
            num_scalar_prefetch=1,
            grid=(1,),
            in_specs=[anywhere, anywhere, pl.BlockSpec(small.shape, lambda i, t: (0, 0))],
            out_specs=[pl.BlockSpec(shape, lambda i, t: (0, 0)) for shape in shapes],
            scratch_shapes=[
                pltpu.VMEM((HEADS, rows), BF16),
                pltpu.VMEM((ENDS, rows), F32),
                pltpu.SemaphoreType.DMA((2 * pairs + 3,)),
            ],
        ),
        out_shape=[jax.ShapeDtypeStruct(shape, BF16) for shape in shapes],
        compiler_params=pltpu.CompilerParams(vmem_limit_bytes=VMEM_LIMIT),
        name="pack",
    )(place, columns, w_out, small)


def collect(members_ref, *refs):
    out_ref = refs[-1]
    for o, ref in enumerate(refs[:-1]):
        out_ref[members_ref[o]] = ref[...].astype(F32)


def run_collect(members, parts):
    n = len(parts) - 1
    lasts = parts[: n // 2] + parts[n // 2 + 1 :]
    at = lambda part: (part.shape[0] - ENDS + SMALL) // 32
    return pl.pallas_call(
        collect,
        grid_spec=pltpu.PrefetchScalarGridSpec(
            num_scalar_prefetch=1,
            grid=(1,),
            in_specs=[pl.BlockSpec((32, SEG), lambda i, t, k=at(p): (k, 0)) for p in lasts],
            out_specs=pl.BlockSpec((n, 32, SEG), lambda i, t: (0, 0, 0)),
        ),
        out_shape=jax.ShapeDtypeStruct((n, 32, SEG), F32),
        compiler_params=pltpu.CompilerParams(vmem_limit_bytes=VMEM_LIMIT),
        cost_estimate=busy(1, 1),
        name="collect",
    )(members, *lasts)


def front(members_ref, tokens_ref, *refs):
    weights, (normed_ref, proj_ref, total) = refs[:-3], refs[-3:]
    tokens = tokens_ref[...].astype(F32)
    inv = lax.rsqrt(jnp.mean(tokens * tokens, axis=-1, keepdims=True) + EPS)
    for o in range(D // SEG):
        at = pl.multiple_of(members_ref[o] * SEG, SEG)
        cols = slice(o * SEG, (o + 1) * SEG)
        last = weights[o if o < D // SEG // 2 else o + 1]
        row = last.shape[0] - ENDS + SMALL
        gain = last[row : row + 16, :].astype(F32)[0:1]
        part = tokens_ref[:, pl.ds(at, SEG)].astype(F32) * inv * gain
        normed_ref[:, cols] = part.astype(BF16)
    project_into(proj_ref, normed_ref, weights, total)


def resident(array, grid_args=1):
    zeros = (0,) * array.ndim
    maps = {1: lambda i: zeros, 2: lambda i, t: zeros, 3: lambda i, t, p: zeros}
    return pl.BlockSpec(array.shape, maps[grid_args], pipeline_mode=pl.Buffered(1))


def run_front(members, tokens, weights):
    length, cols = tokens.shape[0], weights[0].shape[0]
    return pl.pallas_call(
        front,
        grid_spec=pltpu.PrefetchScalarGridSpec(
            num_scalar_prefetch=1,
            grid=(length // GROUP,),
            in_specs=[
                pl.BlockSpec((GROUP, D), lambda i, t: (i, 0)),
            ]
            + [resident(w, 2) for w in weights],
            out_specs=[
                pl.BlockSpec((GROUP, D), lambda i, t: (i, 0)),
                pl.BlockSpec((GROUP, cols), lambda i, t: (i, 0)),
            ],
            scratch_shapes=[pltpu.VMEM((GROUP, cols), F32)],
        ),
        out_shape=[
            jax.ShapeDtypeStruct((length, D), BF16),
            jax.ShapeDtypeStruct((length, cols), BF16),
        ],
        compiler_params=pltpu.CompilerParams(vmem_limit_bytes=VMEM_LIMIT),
        cost_estimate=busy(12, 18),
        name="front",
    )(members, tokens, *weights)


def project(normed_ref, *refs):
    project_into(refs[-2], normed_ref, refs[:-2], refs[-1])


def run_project(normed, weights):
    length, cols = normed.shape[0], weights[0].shape[0]
    return pl.pallas_call(
        project,
        grid=(length // GROUP,),
        in_specs=[pl.BlockSpec((GROUP, D), lambda i: (i, 0))] + [resident(w) for w in weights],
        out_specs=pl.BlockSpec((GROUP, cols), lambda i: (i, 0)),
        out_shape=jax.ShapeDtypeStruct((length, cols), BF16),
        scratch_shapes=[pltpu.VMEM((GROUP, cols), F32)],
        compiler_params=pltpu.CompilerParams(vmem_limit_bytes=VMEM_LIMIT),
        cost_estimate=busy(8, 10),
        name="project",
    )(normed, *weights)


def spread_rows(ref, index, rows):
    count = rows.shape[0]
    ref[pl.ds(index, count), :] = rows[:, :128]
    ref[pl.ds(ref.shape[0] // 2 + index, count), :] = rows[:, 128:]


def all_rows(stack):
    half = stack.shape[0] // 2
    return jnp.concatenate([stack[:half], stack[half:]], axis=1)


def pair_rows(ref, g, pairs):
    half = 8 * pairs
    return jnp.concatenate(
        [ref[pl.ds(g, 8, stride=pairs), :], ref[pl.ds(half + g, 8, stride=pairs), :]], axis=1
    )


def high_low(v):
    high = v.astype(BF16)
    return high, (v - high.astype(F32)).astype(BF16)


def tri_units(back):
    units = []
    for r in range(GROUP // 64):
        for t in range(GROUP // 128):
            if (t >= r // 2) if back else (t <= r // 2):
                units.append((slice(64 * r, 64 * r + 64), slice(128 * t, 128 * t + 128), t == r // 2))
    return units


def diagonal(keep):
    row = lax.broadcasted_iota(jnp.int32, (128, 128), 0)
    col = lax.broadcasted_iota(jnp.int32, (128, 128), 1)
    return jnp.where(keep(row, col), 0.0, -1e30)


def mix_forward(
    proj_ref, taps_ref, heads_ref, skip_ref, act_ref, table_ref, y_ref, start_ref,
    state, halo, gram, bias, scores,
):
    pairs = state.shape[0]
    heads, width = 2 * pairs, pairs * PAIR
    core = width + 2 * STATE

    @pl.when(pl.program_id(0) == 0)
    def _():
        state[...] = jnp.zeros_like(state)
        halo[...] = jnp.zeros_like(halo)
        scores[...] = jnp.zeros_like(scores)
        bias[...] = diagonal(lambda row, col: row >= col)

    def activate(cols):
        current = proj_ref[:, cols].astype(F32)
        conv = conv_tile(jnp.concatenate([halo[:, cols], current], axis=0), taps_ref, cols)
        halo[:, cols] = current[GROUP - HALO :]
        act = (conv * sigmoid(conv)).astype(BF16)
        act_ref[:, cols] = act
        return act

    bs = activate(slice(width, width + STATE))
    cs = activate(slice(width + STATE, core))
    raw = proj_ref[:, core : core + ENDS].astype(F32).T[:heads]
    dt = softplus(raw + heads_ref[:heads, 0:1])
    upto = ones_where(lambda row, col: row <= col).astype(F32)
    cum = exact(dt * heads_ref[heads:, 0:1], upto)
    last = cum[:, GROUP - 1 :]
    table = jnp.concatenate([cum, dt, jnp.exp(last - cum) * dt, jnp.exp(cum)], axis=0)
    spread_rows(table_ref.at[0], 0, table)
    gram[...] = nt(cs, bs)
    bs_t = bs.astype(F32).T

    def one(g, unused):
        cols = pl.ds(pl.multiple_of(g * PAIR, PAIR), PAIR)
        rows = pair_rows(table_ref.at[0], g, pairs)
        turned = rows.T
        x = activate(cols)
        first = lanes(x.shape) < HEADDIM
        start = state[g]
        start_ref[0, g] = start
        inner = nn(cs, start.astype(BF16))
        parts, locals_ = [], []
        for e in range(2):
            for at, to, on in tri_units(False):
                differ = turned[at, e : e + 1] - rows[e : e + 1, to]
                if on:
                    differ = differ + bias[at.start % 128 : at.start % 128 + 64, :]
                decay = jnp.exp(differ)
                scores[e, at, to] = (gram[at, to] * decay * rows[2 + e : 3 + e, to]).astype(BF16)
            parts.append(nn(scores[e], x))
            locals_.append(nn((bs_t * rows[4 + e : 5 + e, :]).astype(BF16), x))
        grow = jnp.where(first, turned[:, 6:7], turned[:, 7:8])
        y_ref[:, cols] = (
            jnp.where(first, parts[0], parts[1]) + grow * inner + skip_ref[:, cols] * x.astype(F32)
        )
        shrink = jnp.where(first[:1], rows[6:7, GROUP - 1 :], rows[7:8, GROUP - 1 :])
        state[g] = shrink * start + jnp.where(first[:STATE], locals_[0], locals_[1])
        return unused

    lax.fori_loop(0, pairs, one, 0, unroll=2)


def run_mix_forward(proj, taps, heads_in, skip, pairs):
    length = proj.shape[0]
    blocks, width = length // GROUP, pairs * PAIR
    core = width + 2 * STATE
    whole = lambda i: (0, 0)
    return pl.pallas_call(
        mix_forward,
        grid=(blocks,),
        in_specs=[
            pl.BlockSpec((GROUP, proj.shape[1]), lambda i: (i, 0)),
            pl.BlockSpec(taps.shape, whole),
            pl.BlockSpec(heads_in.shape, whole),
            pl.BlockSpec(skip.shape, whole),
        ],
        out_specs=[
            pl.BlockSpec((GROUP, core), lambda i: (i, 0)),
            pl.BlockSpec((1, 16 * pairs, 128), lambda i: (i, 0, 0)),
            pl.BlockSpec((GROUP, width), lambda i: (i, 0)),
            pl.BlockSpec((1, pairs, STATE, PAIR), lambda i: (i, 0, 0, 0)),
        ],
        out_shape=[
            jax.ShapeDtypeStruct((length, core), BF16),
            jax.ShapeDtypeStruct((blocks, 16 * pairs, 128), F32),
            jax.ShapeDtypeStruct((length, width), F32),
            jax.ShapeDtypeStruct((blocks, pairs, STATE, PAIR), F32),
        ],
        scratch_shapes=[
            pltpu.VMEM((pairs, STATE, PAIR), F32),
            pltpu.VMEM((HALO, core), F32),
            pltpu.VMEM((GROUP, GROUP), F32),
            pltpu.VMEM((128, 128), F32),
            pltpu.VMEM((2, GROUP, GROUP), BF16),
        ],
        compiler_params=pltpu.CompilerParams(vmem_limit_bytes=VMEM_LIMIT),
        cost_estimate=busy(18, 15),
        name="mix_forward",
    )(proj, taps, heads_in, skip)


def mix_backward(
    top, follows, act_ref, proj_ref, prev_ref, taps_ref, heads_ref, skip_ref, table_ref, start_ref, dy_ref,
    carry_in, halo_in, held_ref, dx_ref, grads_ref, dheads_ref, carried, halo,
    gram, dgram, bias, d_scores, scores, db, dc, found, ends,
):
    pairs = carried.shape[0]
    heads, width = 2 * pairs, pairs * PAIR
    core = width + 2 * STATE
    step = pl.program_id(0)

    @pl.when(step == 0)
    def _():
        carried[...] = carry_in[...] if follows else jnp.zeros_like(carried)
        halo[...] = halo_in[...] if follows else jnp.zeros_like(halo)
        grads_ref[...] = jnp.zeros_like(grads_ref)
        dheads_ref[...] = jnp.zeros_like(dheads_ref)
        scores[...] = jnp.zeros_like(scores)
        bias[...] = diagonal(lambda row, col: row <= col)

    has_prev = jnp.where(top - step > 0, 1.0, 0.0)
    bs, cs = act_ref[:, width : width + STATE], act_ref[:, width + STATE : core]
    bs_float = bs.astype(F32)
    cs_t = cs.astype(F32).T.astype(BF16)
    gram[...] = nt(bs, cs)
    for ref in (dgram, db, dc):
        ref[...] = jnp.zeros_like(ref)

    def conv_back(d_act, cols):
        before = prev_ref[:, cols].astype(F32)[prev_ref.shape[0] - HALO :] * has_prev
        extended = jnp.concatenate([before, proj_ref[:, cols].astype(F32)], axis=0)
        conv = conv_tile(extended, taps_ref, cols)
        sig = sigmoid(conv)
        d_conv = d_act * (sig * (1.0 + conv * (1.0 - sig)))
        onward = jnp.concatenate([d_conv, halo[:, cols]], axis=0)
        d_in = taps_ref[KW - 1 : KW, cols] * d_conv
        for k in range(KW - 1):
            at = KW - 1 - k
            d_in = d_in + taps_ref[k : k + 1, cols] * onward[at : at + GROUP]
        dx_ref[:, cols] = d_in.astype(BF16)
        sums = []
        for k in range(KW):
            at = HALO - KW + 1 + k
            sums.append(jnp.sum(d_conv * extended[at : at + GROUP], axis=0, keepdims=True))
        sums.append(jnp.sum(d_conv, axis=0, keepdims=True))
        sums.append(jnp.zeros((8 - KW - 1, sums[0].shape[1]), F32))
        grads_ref[:, cols] += jnp.concatenate(sums, axis=0)
        halo[:, cols] = d_conv[:HALO]

    def one(g, unused):
        cols = pl.ds(pl.multiple_of(g * PAIR, PAIR), PAIR)
        rows = pair_rows(table_ref.at[0], g, pairs)
        turned = rows.T
        x, dy = act_ref[:, cols], dy_ref[:, cols]
        first = lanes(x.shape) < HEADDIM
        dy_float = dy.astype(F32)
        start, grad = start_ref[0, g], carried[g]
        start_low, grad_low = start.astype(BF16), grad.astype(BF16)
        inner = nn(cs, start_low)
        grow = jnp.where(first, turned[:, 6:7], turned[:, 7:8])
        d_inner = (dy_float * grow).astype(BF16)
        dc[...] += nt(d_inner, start_low)
        touched = dy_float * inner
        held = jnp.sum(grad * start, axis=0, keepdims=True)
        zero = jnp.zeros_like(x)
        reach = nn(bs, grad_low)
        sent = x.astype(F32) * jnp.where(first, turned[:, 4:5], turned[:, 5:6])
        for half in high_low(sent):
            db[...] += nt(half, grad_low)
        parts, sums_j, linked = [], [], []
        for e in range(2):
            own = first if e == 0 else jnp.logical_not(first)
            d_scores[e] = nt(jnp.where(own, x, zero), dy)
            linked_i, linked_j = {}, {}
            for at, to, on in tri_units(True):
                dt_col = turned[at, 2 + e : 3 + e]
                differ = rows[e : e + 1, to] - turned[at, e : e + 1]
                if on:
                    differ = differ + bias[at.start % 128 : at.start % 128 + 64, :]
                decay = jnp.exp(differ)
                grown = gram[at, to] * decay
                d_score = d_scores[e, at, to]
                score = grown * dt_col
                scores[e, at, to] = score.astype(BF16)
                dgram[at, to] += d_score * decay * dt_col
                along_i = d_score * grown
                along_j = jnp.sum(d_score * score, axis=0, keepdims=True)
                key_i, key_j = at.start, to.start
                linked_i[key_i] = along_i if key_i not in linked_i else linked_i[key_i] + along_i
                linked_j[key_j] = along_j if key_j not in linked_j else linked_j[key_j] + along_j
            sums_j.append(jnp.concatenate([linked_j[k] for k in sorted(linked_j)], axis=1))
            linked.append(jnp.concatenate([linked_i[k] for k in sorted(linked_i)], axis=0))
            tail_col = turned[:, 4 + e : 5 + e]
            parts.append(nn(scores[e], dy) + nn((bs_float * tail_col).astype(BF16), grad_low))
        pick = lax.broadcasted_iota(jnp.int32, (8, 2 * PAIR), 0)
        lane = lanes((8, 2 * PAIR))
        by_head = (pick == lane // HEADDIM).astype(BF16)
        by_pair = (pick == 4 + lane // PAIR).astype(BF16)
        kept = jnp.zeros((8, GROUP), F32)
        for sums, select in (
            ((x.astype(F32) * reach, touched), by_head),
            (linked, by_pair),
        ):
            for half in high_low(jnp.concatenate(sums, axis=1)):
                kept = kept + nt(select, half)
        kept = jnp.concatenate([kept[:6]] + sums_j, axis=0)
        found[pl.ds(g, 8, stride=pairs), :] = kept[:, :128]
        found[pl.ds(8 * pairs + g, 8, stride=pairs), :] = kept[:, 128:]
        ends[pl.ds(g, 2, stride=pairs), :] = jnp.concatenate(
            [jnp.where(first[:1], held, 0.0), jnp.where(first[:1], 0.0, held)], axis=0
        )
        conv_back(jnp.where(first, parts[0], parts[1]) + skip_ref[:, cols] * dy_float, cols)
        shrink = jnp.where(first[:1], rows[6:7, GROUP - 1 :], rows[7:8, GROUP - 1 :])
        carried[g] = shrink * grad + nn(cs_t, d_inner)
        return unused

    lax.fori_loop(0, pairs, one, 0, unroll=2)
    low = dgram[...].astype(BF16)
    conv_back(db[...] + nn(low, cs), slice(width, width + STATE))
    conv_back(dc[...] + tn(low, bs), slice(width + STATE, core))

    rows, sums = all_rows(table_ref[0]), all_rows(found[...])
    d_tail, touched, sum_i, sum_j = (sums[k * heads : (k + 1) * heads] for k in range(4))
    cum, dt, tail, growth = (rows[k * heads : (k + 1) * heads] for k in range(4))
    a_neg = heads_ref[heads:, 0:1]
    tail_log = d_tail * tail
    d_last = jnp.sum(tail_log, axis=1, keepdims=True)
    d_last = d_last + jnp.sum(ends[...], axis=1, keepdims=True) * growth[:, GROUP - 1 :]
    d_cum = touched * growth - tail_log + sum_j - dt * sum_i
    d_cum = d_cum + jnp.where(lanes(d_cum.shape) == GROUP - 1, d_last, 0.0)
    d_rate = exact(d_cum, ones_where(lambda row, col: row >= col).astype(F32))
    raw = proj_ref[:, core : core + ENDS].astype(F32).T[:heads]
    d_step = d_tail * jnp.exp(cum[:, GROUP - 1 :] - cum) + sum_i
    d_dt = (d_step + d_rate * a_neg) * sigmoid(raw + heads_ref[:heads, 0:1])
    dheads_ref[:heads, :] += d_dt
    dheads_ref[heads:, :] += d_rate * dt
    filled = jnp.concatenate([d_dt, jnp.zeros((ENDS - heads, GROUP), F32)], axis=0)
    dx_ref[:, core : core + ENDS] = filled.T.astype(BF16)


def run_mix_backward(span, top, act, proj, taps, heads_in, skip, table, starts, dy, before):
    pairs = starts.shape[1]
    follows = before is not None
    held, carry, halo = before if follows else (dy, skip[:, :128], skip[:, :128])
    heads, width = 2 * pairs, pairs * PAIR
    core = width + 2 * STATE
    whole = lambda i: (0, 0)
    block = lambda i: (top - i, 0)
    above = GROUP // 16
    return pl.pallas_call(
        lambda *refs: mix_backward(top, follows, *refs),
        grid=(span,),
        in_specs=[
            pl.BlockSpec((GROUP, core), block),
            pl.BlockSpec((GROUP, proj.shape[1]), block),
            pl.BlockSpec((16, proj.shape[1]), lambda i: (jnp.maximum((top - i) * above - 1, 0), 0)),
            pl.BlockSpec(taps.shape, whole),
            pl.BlockSpec(heads_in.shape, whole),
            pl.BlockSpec(skip.shape, whole),
            pl.BlockSpec((1, 16 * pairs, 128), lambda i: (top - i, 0, 0)),
            pl.BlockSpec((1, pairs, STATE, PAIR), lambda i: (top - i, 0, 0, 0)),
            pl.BlockSpec((GROUP, width), block),
            pl.BlockSpec(carry.shape, lambda i: (0,) * carry.ndim),
            pl.BlockSpec(halo.shape, whole),
            pl.BlockSpec(memory_space=pl.ANY),
        ],
        out_specs=[
            pl.BlockSpec((GROUP, proj.shape[1]), block),
            pl.BlockSpec((8, core), whole),
            pl.BlockSpec((2 * heads, GROUP), whole),
            pl.BlockSpec((pairs, STATE, PAIR), lambda i: (0, 0, 0)),
            pl.BlockSpec((HALO, core), whole),
        ],
        out_shape=[
            jax.ShapeDtypeStruct(proj.shape, BF16),
            jax.ShapeDtypeStruct((8, core), F32),
            jax.ShapeDtypeStruct((2 * heads, GROUP), F32),
            jax.ShapeDtypeStruct((pairs, STATE, PAIR), F32),
            jax.ShapeDtypeStruct((HALO, core), F32),
        ],
        scratch_shapes=[
            pltpu.VMEM((GROUP, GROUP), F32),
            pltpu.VMEM((GROUP, GROUP), F32),
            pltpu.VMEM((128, 128), F32),
            pltpu.VMEM((2, GROUP, GROUP), F32),
            pltpu.VMEM((2, GROUP, GROUP), BF16),
            pltpu.VMEM((GROUP, STATE), F32),
            pltpu.VMEM((GROUP, STATE), F32),
            pltpu.VMEM((8 * heads, 128), F32),
            pltpu.VMEM((heads, PAIR), F32),
        ],
        compiler_params=pltpu.CompilerParams(vmem_limit_bytes=VMEM_LIMIT),
        input_output_aliases={11: 0} if follows else {},
        cost_estimate=busy(12 * span, 5 * span),
        name="mix_backward",
    )(act, proj, proj, taps, heads_in, skip, table, starts, dy, carry, halo, held)


def gate_sums(members_ref, seed_ref, z_ref, y_ref, gain_ref, *refs):
    parts, (w_ref, scaled_ref, sums_ref, squares, along) = refs[:-5], refs[-5:]
    step, n = pl.program_id(0), len(refs[:-5]) - 1

    @pl.when(step == 0)
    def _():
        squares[...] = jnp.zeros_like(squares)
        along[...] = jnp.zeros_like(along)
        places = list(range(n // 2)) + [n // 2] * 2 + list(range(n // 2 + 1, n))
        for k, (o, part) in enumerate(zip(places, parts)):
            at = pl.multiple_of(members_ref[o] * PAIR, PAIR)
            if k == n // 2 + 1:
                at = at + PAIR - part.shape[0]
            w_ref[pl.ds(at, part.shape[0]), :] = part[...]

    tile = z_ref.shape[1]
    scaled = nt(seed_ref[...], w_ref[pl.ds(pl.multiple_of(step * tile, tile), tile), :])
    scaled_ref[...] = scaled
    z = z_ref[...].astype(F32)
    gated = y_ref[...] * (z * sigmoid(z))
    square = gated * gated
    lean = scaled * gain_ref[...] * gated
    for cols in tiles(square.shape[1]):
        squares[...] += square[:, cols]
        along[...] += lean[:, cols]

    @pl.when(step == pl.num_programs(0) - 1)
    def _():
        spot = lanes(squares.shape)
        both = jnp.where(
            spot == 0,
            jnp.sum(squares[...], axis=1, keepdims=True),
            jnp.where(spot == 1, jnp.sum(along[...], axis=1, keepdims=True), 0.0),
        )
        sums_ref[...] = both.T[:8]


def run_gate_sums(members, seed, parts, z, y, gain):
    length, width = y.shape
    tile = 2 * PAIR
    col = pl.BlockSpec((length, tile), lambda i, t: (0, i))
    return pl.pallas_call(
        gate_sums,
        grid_spec=pltpu.PrefetchScalarGridSpec(
            num_scalar_prefetch=1,
            grid=(width // tile,),
            in_specs=[resident(seed, 2), col, col, pl.BlockSpec((1, tile), lambda i, t: (0, i))]
            + [resident(part, 2) for part in parts],
            out_specs=[
                pl.BlockSpec((width, D), lambda i, t: (0, 0)),
                col,
                pl.BlockSpec((8, length), lambda i, t: (0, 0)),
            ],
            scratch_shapes=[pltpu.VMEM((length, PAIR), F32)] * 2,
        ),
        out_shape=[
            jax.ShapeDtypeStruct((width, D), BF16),
            jax.ShapeDtypeStruct(y.shape, F32),
            jax.ShapeDtypeStruct((8, length), F32),
        ],
        compiler_params=pltpu.CompilerParams(vmem_limit_bytes=VMEM_LIMIT),
        cost_estimate=busy(11, 20),
        name="gate_sums",
    )(members, seed, z, y, gain, *parts)


def gate_back(sums_ref, scaled_ref, z_ref, y_ref, x_ref, gain_ref, mixed_ref, dy_ref, dz_ref, cols_ref, turned):
    @pl.when(pl.program_id(0) == 0)
    def _():
        inv = lax.rsqrt(sums_ref[0:1, :] / DI + EPS)
        slope = inv * inv * inv * (sums_ref[1:2, :] / DI)
        rest = jnp.zeros((PAIR - 2, sums_ref.shape[1]), F32)
        both = jnp.concatenate([inv, slope, rest], axis=0).T
        turned[0] = jnp.broadcast_to(both[:, 0:1], turned.shape[1:])
        turned[1] = jnp.broadcast_to(both[:, 1:2], turned.shape[1:])

    inv, slope = turned[0], turned[1]
    z, y, scaled, gain = z_ref[...].astype(F32), y_ref[...], scaled_ref[...], gain_ref[...]
    sig = sigmoid(z)
    silu = z * sig
    gated = y * silu
    normal = gated * inv
    mixed_ref[...] = (normal * gain).astype(BF16)
    d_gated = scaled * gain * inv - gated * slope
    dy = (d_gated * silu).astype(BF16)
    dy_ref[...] = dy
    dz_ref[...] = (d_gated * y * (sig * (1.0 + z * (1.0 - sig)))).astype(BF16)
    cols_ref[0:1, :] = jnp.sum(scaled * normal, axis=0, keepdims=True)
    cols_ref[1:2, :] = jnp.sum(dy.astype(F32) * x_ref[...].astype(F32), axis=0, keepdims=True)
    cols_ref[2:, :] = jnp.zeros_like(cols_ref[2:, :])


def run_gate_back(sums, scaled, z, y, x, gain):
    length, width = y.shape
    tile = PAIR
    col = pl.BlockSpec((length, tile), lambda i: (0, i))
    low = jax.ShapeDtypeStruct(y.shape, BF16)
    return pl.pallas_call(
        gate_back,
        grid=(width // tile,),
        in_specs=[
            pl.BlockSpec(sums.shape, lambda i: (0, 0)),
            col,
            col,
            col,
            col,
            pl.BlockSpec((1, tile), lambda i: (0, i)),
        ],
        out_specs=[col, col, col, pl.BlockSpec((8, tile), lambda i: (0, i))],
        out_shape=[low, low, low, jax.ShapeDtypeStruct((8, width), F32)],
        scratch_shapes=[pltpu.VMEM((2, length, PAIR), F32)],
        compiler_params=pltpu.CompilerParams(vmem_limit_bytes=VMEM_LIMIT),
        cost_estimate=busy(11, 20),
        name="gate_back",
    )(sums, scaled, z, y, x, gain)


def keep_or_give(place_ref, value, keep_ref, give_ref):
    mine = place_ref[0] % 2 == pl.program_id(0) % 2

    @pl.when(mine)
    def _():
        keep_ref[0] = value

    @pl.when(jnp.logical_not(mine))
    def _():
        give_ref[0] = value


def back_norm(members_ref, place_ref, tokens_ref, dz_ref, dx_ref, *refs):
    parts, (keep_ref, give_ref, gain_ref, dn_ref) = refs[:-4], refs[-4:]
    count = len(parts) // 2

    @pl.when(pl.program_id(0) == 0)
    def _():
        gain_ref[...] = jnp.zeros_like(gain_ref)

    tokens = tokens_ref[...].astype(F32)
    inv = lax.rsqrt(jnp.mean(tokens * tokens, axis=-1, keepdims=True) + EPS)
    sums = [None] * (D // SEG)
    for source, weights in ((dz_ref, parts[:count]), (dx_ref, parts[count:])):
        for o, at, w in by_segments(weights):
            part = nn(source[:, at : at + w.shape[0]], w[...])
            sums[o] = part if sums[o] is None else sums[o] + part
    for o, d_normed in enumerate(sums):
        at = pl.multiple_of(members_ref[o] * SEG, SEG)
        dn_ref[:, pl.ds(at, SEG)] = d_normed.astype(BF16)
        scaled = tokens_ref[:, pl.ds(at, SEG)].astype(F32) * inv
        gain_ref[0:1, pl.ds(at, SEG)] += jnp.sum(d_normed * scaled, axis=0, keepdims=True)
    keep_or_give(place_ref, dn_ref[...], keep_ref, give_ref)


def run_back_norm(members, place, tokens, dz, dx, weights_z, weights_x):
    length = tokens.shape[0]
    row = lambda i, t, p: (i, 0)
    half = pl.BlockSpec((1, GROUP, D), lambda i, t, p: (i // 2, 0, 0))
    halves_shape = jax.ShapeDtypeStruct((length // GROUP // 2, GROUP, D), BF16)
    return pl.pallas_call(
        back_norm,
        grid_spec=pltpu.PrefetchScalarGridSpec(
            num_scalar_prefetch=2,
            grid=(length // GROUP,),
            in_specs=[
                pl.BlockSpec((GROUP, D), row),
                pl.BlockSpec((GROUP, dz.shape[1]), row),
                pl.BlockSpec((GROUP, dx.shape[1]), row),
            ]
            + [resident(w, 3) for w in weights_z + weights_x],
            out_specs=[half, half, pl.BlockSpec((8, D), lambda i, t, p: (0, 0))],
            scratch_shapes=[pltpu.VMEM((GROUP, D), BF16)],
        ),
        out_shape=[halves_shape, halves_shape, jax.ShapeDtypeStruct((8, D), F32)],
        compiler_params=pltpu.CompilerParams(vmem_limit_bytes=VMEM_LIMIT),
        cost_estimate=busy(18, 24),
        name="back_norm",
    )(members, place, tokens, dz, dx, *weights_z, *weights_x)


def assemble_o(place_ref, o0, o1, o2, o3, out_ref):
    for k, ref in enumerate((o0, o1, o2, o3)):

        @pl.when(pl.program_id(0) == k)
        def _():
            out_ref[...] = ref[...].astype(F32)


def run_assemble_o(place, shares):
    m, (rows, cols) = len(shares), shares[0].shape
    return pl.pallas_call(
        assemble_o,
        grid_spec=pltpu.PrefetchScalarGridSpec(
            num_scalar_prefetch=1,
            grid=(m,),
            in_specs=[resident(share, 2) for share in shares],
            out_specs=pl.BlockSpec((rows, cols), lambda i, t: (t[0] ^ i, 0)),
        ),
        out_shape=jax.ShapeDtypeStruct((m * rows, cols), F32),
        compiler_params=pltpu.CompilerParams(vmem_limit_bytes=VMEM_LIMIT),
        cost_estimate=busy(3, 3),
        name="assemble_o",
    )(place, *shares)


def put_pairs(place_ref, refs, out_ref, g):
    m = len(refs)
    for k, ref in enumerate(refs):
        to = pl.multiple_of((place_ref[0] ^ k) * PAIR, PAIR)
        out_ref[pl.ds(to, PAIR), :] = ref[pl.ds(pl.multiple_of(g * PAIR, PAIR), PAIR), :].astype(F32)


def assemble_z(place_ref, z0, z1, z2, z3, out_ref):
    put_pairs(place_ref, (z0, z1, z2, z3), out_ref, pl.program_id(0))


def assemble_a(place_ref, held_ref, a0, a1, a2, a3, out_ref):
    put_pairs(place_ref, (a0, a1, a2, a3), out_ref, pl.program_id(0))


def assemble_b(place_ref, order_ref, held_ref, b0, b1, b2, b3, out_ref):
    step, last = pl.program_id(0), pl.num_programs(0) - 1
    refs = (b0, b1, b2, b3)
    width = last * PAIR
    core = width + 2 * STATE

    @pl.when(step < last)
    def _():
        put_pairs(place_ref, refs, out_ref, step)

    @pl.when(step == last)
    def _():
        total = jnp.zeros((2 * STATE, out_ref.shape[1]), F32)
        steps = jnp.zeros((HEADS, out_ref.shape[1]), F32)
        for k, x in enumerate(refs):
            total = total + x[width:core].astype(F32)
            steps = steps + nn(order_ref[place_ref[0] ^ k], x[core : core + TAIL])
        out_ref[: 2 * STATE] = total
        out_ref[2 * STATE : 2 * STATE + HEADS] = steps


def run_assemble_z(place, shares, columns):
    m, rows = len(shares), shares[0].shape[1]
    tile = m * PAIR
    return pl.pallas_call(
        assemble_z,
        grid_spec=pltpu.PrefetchScalarGridSpec(
            num_scalar_prefetch=1,
            grid=(DI // tile,),
            in_specs=[resident(s, 2) for s in shares],
            out_specs=pl.BlockSpec((tile, rows), lambda i, t: (i, 0)),
        ),
        out_shape=jax.ShapeDtypeStruct((columns, rows), F32),
        compiler_params=pltpu.CompilerParams(vmem_limit_bytes=VMEM_LIMIT),
        cost_estimate=busy(4, 6),
        name="assemble_z",
    )(place, *shares)


def run_assemble_b(place, order, held, shares, count):
    m, rows = len(shares), shares[0].shape[1]
    tile = m * PAIR
    first = 2 * (DI // tile) - count
    return pl.pallas_call(
        assemble_b,
        grid_spec=pltpu.PrefetchScalarGridSpec(
            num_scalar_prefetch=1,
            grid=(count + 1,),
            in_specs=[resident(order, 2), pl.BlockSpec(memory_space=pl.ANY)]
            + [resident(s, 2) for s in shares],
            out_specs=pl.BlockSpec((tile, rows), lambda i, t: (i + first, 0)),
        ),
        out_shape=jax.ShapeDtypeStruct(held.shape, F32),
        input_output_aliases={2: 0},
        compiler_params=pltpu.CompilerParams(vmem_limit_bytes=VMEM_LIMIT),
        cost_estimate=busy(3, 2),
        name="assemble_b",
    )(place, order, held, *shares)


def run_assemble_a(place, held, shares):
    m, rows = len(shares), shares[0].shape[1]
    tile = m * PAIR
    return pl.pallas_call(
        assemble_a,
        grid_spec=pltpu.PrefetchScalarGridSpec(
            num_scalar_prefetch=1,
            grid=(shares[0].shape[0] // PAIR,),
            in_specs=[pl.BlockSpec(memory_space=pl.ANY)] + [resident(s, 2) for s in shares],
            out_specs=pl.BlockSpec((tile, rows), lambda i, t: (i + DI // tile, 0)),
        ),
        out_shape=jax.ShapeDtypeStruct(held.shape, F32),
        input_output_aliases={1: 0},
        compiler_params=pltpu.CompilerParams(vmem_limit_bytes=VMEM_LIMIT),
        cost_estimate=busy(4, 5),
        name="assemble_a",
    )(place, held, *shares)


def body(
    tokens, norm_gain, w_in, conv_w, conv_b, dt_bias, a_log, d_skip, gate_gain, w_out, cotangent
):
    n, m = lax.axis_size("fsdp"), lax.axis_size("ctx")
    place = lax.axis_index("ctx")
    piece = tokens.shape[1]
    length = piece * m
    blocks = length // GROUP
    pairs = DI // PAIR // m
    width = pairs * PAIR
    heads = 2 * pairs
    rows = w_in.shape[0]
    core_cols = width + 2 * STATE
    head_cols = core_cols + heads
    ring = rows == SEG and (DI // PAIR) // n == m

    def of_pairs(array, axis):
        shape = array.shape
        each = shape[axis] // (pairs * m)
        split = array.reshape(shape[:axis] + (pairs, m, each) + shape[axis + 1 :])
        mine = lax.dynamic_index_in_dim(split, place, axis + 1, False)
        return mine.reshape(shape[:axis] + (pairs * each,) + shape[axis + 1 :])

    def of_heads(array):
        mine = of_pairs(array, 0)
        split = mine.reshape((pairs, 2) + mine.shape[1:]).swapaxes(0, 1)
        return split.reshape(mine.shape)

    all_tokens = lax.all_gather(tokens[0], "ctx", axis=0, tiled=True)
    seed = lax.all_gather(cotangent[0], "ctx", axis=0, tiled=True)


    columns = w_in.T
    total_cols = core_cols + ENDS
    cut = halves(total_cols)[0]
    place_ref = place.reshape(1).astype(jnp.int32)
    smalls = [norm_gain[None], gate_gain[None], conv_b[None], conv_w]
    small_rows = [-(-v.shape[1] // SEG) for v in smalls]

    def split(whole):
        upper, _ = halves(whole.shape[0])
        parts = [whole[:, o * SEG : (o + 1) * SEG] for o in range(D // SEG)]
        middle = parts[len(parts) // 2]
        return parts[: len(parts) // 2] + [middle[:upper], middle[upper:]] + parts[len(parts) // 2 + 1 :]

    if ring:
        me = ring_place(lax.axis_index("fsdp"), n)
        members = ring_member(me + jnp.arange(n), n).astype(jnp.int32)
        padded = [jnp.pad(v, ((0, 0), (0, k * SEG - v.shape[1]))) for v, k in zip(smalls, small_rows)]
        small = jnp.concatenate([v.reshape(-1) for v in padded]).reshape(-1, SEG)
        block_x, block_z, block_o = run_pack(place_ref, columns, w_out, small, pairs)
        ring_x, ring_z, ring_o = Gather(block_x, n), Gather(block_z, n), Gather(block_o, n)
        next_hop([ring_x], ())
        dt_bias, a_log, d_skip = next_hop([ring_x], (dt_bias, a_log, d_skip))
        for _ in range(n // 2 - 4):
            next_hop([ring_x], ())
        next_hop([ring_x, ring_z], ())
        next_hop([ring_x], (), *arrivals(ring_z))
        parts_x = ring_x.parts()
        all_tokens, members_late, parts_late = next_hop(
            [ring_z, ring_o], (all_tokens, members, parts_x), *arrivals(ring_x)
        )
    else:
        members = jnp.arange(D // SEG, dtype=jnp.int32)
        block_x = jnp.concatenate(
            [
                of_pairs(columns[DI : 2 * DI], 0),
                columns[2 * DI : 2 * DI + 2 * STATE],
                of_heads(columns[DI + CONV :]),
                jnp.zeros((ENDS - heads, rows), BF16),
            ],
            axis=0,
        )
        whole_x = lax.all_gather(block_x, "fsdp", axis=1, tiled=True)
        norm_whole = lax.all_gather(norm_gain[None], "fsdp", axis=1, tiled=True)
        at = core_cols + SMALL
        whole_x = jnp.concatenate([whole_x[:at], norm_whole, whole_x[at + 1 :]], axis=0)
        parts_x, parts_z = split(whole_x), split(lax.all_gather(of_pairs(columns[:DI], 0), "fsdp", axis=1, tiled=True))
        w_o = of_pairs(lax.all_gather(w_out, "fsdp", axis=0, tiled=True), 0)
        parts_o = [w_o[o * PAIR : (o + 1) * PAIR] for o in range(pairs)]
        middle, upper = parts_o[pairs // 2], halves(PAIR)[0]
        parts_o = parts_o[: pairs // 2] + [middle[:upper], middle[upper:]] + parts_o[pairs // 2 + 1 :]

    if ring:
        kept = run_collect(members_late, parts_late)
        spans, at = [], 0
        for v, each in zip(smalls, small_rows):
            here = kept[:, at : at + v.shape[0] * each].reshape(n, v.shape[0], each * SEG)
            spans.append(here[:, :, : v.shape[1]].transpose(1, 0, 2).reshape(v.shape[0], -1))
            at += v.shape[0] * each
        norm_full, gate_full, bias_full, taps_full = spans
    else:
        norm_full, gate_full, bias_full, taps_full = (
            lax.all_gather(v, "fsdp", axis=1, tiled=True).astype(F32) for v in smalls
        )
    gate_full = of_pairs(gate_full, 1)
    taps_full = jnp.concatenate([taps_full, bias_full], axis=0)
    taps = jnp.concatenate([of_pairs(taps_full[:, :DI], 1), taps_full[:, DI:]], axis=1)
    taps = jnp.pad(taps, ((0, 8 - KW - 1), (0, 0)))

    dt_bias_own, a_log_own = of_heads(dt_bias), of_heads(a_log)
    skip_own = of_pairs(d_skip, 0)
    a_neg = -jnp.exp(a_log_own)
    heads_in = jnp.broadcast_to(jnp.concatenate([dt_bias_own, a_neg])[:, None], (2 * heads, 128))
    skip_row = jnp.repeat(skip_own, HEADDIM)[None, :]

    normed, proj_x = run_front(members, all_tokens, parts_x)
    if ring:
        proj_x = next_hop([ring_z, ring_o], proj_x, *arrivals(ring_z, ring_o))
    act, table, ssd, starts = run_mix_forward(proj_x, taps, heads_in, skip_row, pairs)
    normed_z = normed
    if ring:
        for _ in range(n // 2 - 3):
            next_hop([ring_z, ring_o], (), ssd, *arrivals(ring_z, ring_o))
        normed_z = next_hop([ring_o], normed, *arrivals(ring_z))
        parts_z, parts_o = ring_z.parts(), ring_o.parts()
    proj_z = run_project(normed_z, parts_z)

    w_o, scaled, sums = run_gate_sums(members, seed, parts_o, proj_z, ssd, gate_full)
    sums = ctx_sum(sums, m)
    mixed, dy, d_z, gate_cols = run_gate_back(sums, scaled, proj_z, ssd, act, gate_full)

    grads_o = tn(mixed, seed).astype(BF16)
    conv_grads, head_grads, top, before = [], [], blocks - 1, None
    d_z_late, mixed_late = d_z, mixed
    if ring:
        sum_o = Reduce(lambda o: lax.dynamic_slice_in_dim(grads_o, members[o] * PAIR, PAIR, 0), n)
        d_z_late, mixed_late = next_hop([sum_o], (d_z, mixed))
    grads_z = tn(d_z_late, normed).astype(BF16)
    branch = nn(mixed_late, w_o).astype(BF16)
    if ring:
        sum_z = Reduce(lambda o: grads_z[:, o * SEG : (o + 1) * SEG], n)
    for at in range(2):
        if ring:
            sum_o.join()
            if at > 0:
                sum_z.join()
                branch_own.middle()
                dy, before, branch_own.sent = next_hop(
                    [sum_o, sum_z], (dy, before, branch_own.sent)
                )
                branch_own.send_far()
            else:
                dy, branch = next_hop([sum_o, sum_z], (dy, branch))
                branch_own = CtxReduce(*by_core(branch.reshape(m, piece, D), m), m)
        span = blocks // 2
        d_x, conv_part, head_part, *before = run_mix_backward(
            span, top, act, proj_x, taps, heads_in, skip_row, table, starts, dy, before
        )
        before = (d_x, *before)
        conv_grads.append(conv_part)
        head_grads.append(head_part)
        top -= span
    normed_late = normed
    if ring:
        sum_o.join()
        sum_z.join()
        d_x, normed_late, branch_own.far = next_hop(
            [sum_o, sum_z], (d_x, normed, branch_own.far)
        )
    else:
        branch_own = CtxReduce(*by_core(branch.reshape(m, piece, D), m), m)
        branch_own.middle()
        branch_own.send_far()
    grads_x = tn(d_x, normed_late).astype(BF16)
    kept, given, d_gain = run_back_norm(
        members, place_ref, all_tokens, d_z, after(d_x, grads_x), parts_z, parts_x
    )
    small = run_gather_small(conv_grads, head_grads, gate_cols, d_gain)
    if ring:
        used = core_cols + TAIL
        sum_x = Reduce(
            lambda o: grads_x[:used, o * SEG : (o + 1) * SEG], n, run_cut(grads_x, used, n // 2)
        )
        part_o = sum_o.join().astype(BF16)
        sum_z.join()
        kept, given, small, part_o, branch_own.far = next_hop(
            [sum_x, sum_z], (kept, given, small, part_o, branch_own.far)
        )
    flip = 1
    steps = []
    while flip < n:
        steps.append(flip)
        flip *= 2

    def small_step(small):
        if steps:
            small = small + lax.ppermute(small, "fsdp", ctx_route(n, steps.pop()))
        return small

    d_own = CtxReduce(kept, given, m)
    d_own.middle()
    d_own.send_far()
    small = small_step(small)
    if ring:
        sum_x.join()
        part_z = sum_z.join().astype(BF16)
        d_own.far, small, part_o, part_z, branch_own.far = next_hop(
            [sum_x], (d_own.far, small, part_o, part_z, branch_own.far)
        )
        other_o = far_share(part_o, m)
    small = small_step(small)
    output = (tokens[0].astype(F32) + branch_own.total()).astype(BF16)[None]
    if ring:
        sum_x.join()
        small, other_o, part_z, d_own.far = next_hop(
            [sum_x], (small, other_o, part_z, d_own.far), output
        )
        shares_o, other_z = near_share(part_o, other_o, m), far_share(part_z, m)
        grad_w_out = run_assemble_o(place_ref, shares_o)
    small = small_step(small)
    own = tokens[0].astype(F32)
    inv = lax.rsqrt(jnp.mean(own * own, axis=-1, keepdims=True) + EPS)
    d_direct = d_own.total() * norm_full
    along = jnp.mean(d_direct * own, axis=-1, keepdims=True)
    grad_tokens = (cotangent[0].astype(F32) + d_direct * inv - own * (inv * inv * inv * along))[None]
    if ring:
        for at in range(n // 2 - 3):
            sum_x.join()
            small, part_z, other_z = next_hop(
                [sum_x], (small, part_z, other_z), grad_tokens, grad_w_out
            )
        shares_z = near_share(part_z, other_z, m)
        held = run_assemble_z(place_ref, shares_z, w_in.shape[1])
    while steps:
        small = small_step(small)
    smalls_of = ctx_share(small, m)
    if ring:
        part_x = sum_x.join().astype(BF16)
        part_a, part_b = part_x[:cut], part_x[cut:]
        part_a, part_b, smalls_of = barrier((part_a, part_b, smalls_of))
    by_place = jnp.zeros((m,) + small.shape, F32)
    for k in range(m):
        by_place = lax.dynamic_update_slice(by_place, smalls_of[k][None], (place ^ k, 0, 0))

    mine = lax.axis_index("fsdp")
    lines = [core_cols] * (KW + 1) + [width, width, D]
    found, at = [], 0
    for count in lines:
        found.append(by_place[:, at : at + count // SEG].reshape(m, 1, count))
        at += count // SEG
    conv_lines = jnp.concatenate(found[: KW + 1], axis=1)

    def interleaved(lines):
        return lines.reshape(m, -1, pairs, PAIR).transpose(1, 2, 0, 3).reshape(-1, DI)

    whole = jnp.concatenate(
        [interleaved(conv_lines[:, :, :width]), jnp.sum(conv_lines[:, :, width:], axis=0)], axis=1
    )
    each = conv_b.shape[0]
    grad_conv = lax.dynamic_slice_in_dim(whole, mine * each, each, 1)
    each = gate_gain.shape[0]
    grad_gate_gain = lax.dynamic_slice_in_dim(interleaved(found[KW + 1]), mine * each, each, 1)[0]
    grad_gain = lax.dynamic_slice_in_dim(jnp.sum(found[KW + 3], axis=0)[0], mine * rows, rows, 0)
    skips = jnp.sum(found[KW + 2].reshape(m, pairs, 2, HEADDIM), axis=3).reshape(m, 1, pairs, 2)
    of_steps = jnp.sum(by_place[:, by_place.shape[1] - 2 * heads :], axis=2)
    of_steps = of_steps.reshape(m, 2, 2, pairs).transpose(0, 1, 3, 2)
    per_head = jnp.concatenate([of_steps, skips], axis=1).transpose(1, 2, 0, 3).reshape(3, HEADS)
    grad_a_log = per_head[1] * -jnp.exp(a_log)
    if not ring:
        part_z = lax.psum_scatter(grads_z.astype(F32), "fsdp", scatter_dimension=1, tiled=True)
        part_x = lax.psum_scatter(grads_x.astype(F32), "fsdp", scatter_dimension=1, tiled=True)
        whole_o = jnp.zeros((pairs, m, PAIR, D), F32)
        whole_o = lax.dynamic_update_index_in_dim(
            whole_o, grads_o.astype(F32).reshape(pairs, PAIR, D), place, 1
        )
        grad_w_out = lax.psum_scatter(whole_o.reshape(DI, D), "fsdp", scatter_dimension=0, tiled=True)
        grad_w_out = lax.psum(grad_w_out, "ctx")
        held = run_assemble_z(place_ref, ctx_share(part_z.astype(BF16), m), w_in.shape[1])
        part_x = part_x.astype(BF16)
        part_a, part_b = part_x[:cut], part_x[cut : core_cols + TAIL]
    other_b, other_a = far_share(part_b, m), far_share(part_a, m)
    order = np.zeros((m, HEADS, TAIL), np.float32)
    for member in range(m):
        for h in range(heads):
            order[member, (h % pairs) * 2 * m + 2 * member + h // pairs, h] = 1.0
    shares_b = near_share(part_b, other_b, m)
    held = run_assemble_b(place_ref, jnp.asarray(order, BF16), held, shares_b, pairs - cut // PAIR)
    shares_a = near_share(part_a, other_a, m)
    grad_w_in = run_assemble_a(place_ref, held, shares_a)
    return (
        output,
        grad_tokens,
        grad_gain,
        grad_w_in.T,
        grad_conv[:KW],
        grad_conv[KW],
        per_head[0],
        grad_a_log,
        per_head[2],
        grad_gate_gain,
        grad_w_out,
    )


def solution(mesh):
    in_specs = (
        P("fsdp", "ctx", None),
        P("fsdp"),
        P("fsdp", None),
        P(None, "fsdp"),
        P("fsdp"),
        P(),
        P(),
        P(),
        P("fsdp"),
        P("fsdp", None),
        P("fsdp", "ctx", None),
    )
    out_specs = (
        P("fsdp", "ctx", None),
        P("fsdp", "ctx", None),
        P("fsdp"),
        P("fsdp", None),
        P(None, "fsdp"),
        P("fsdp"),
        P(),
        P(),
        P(),
        P("fsdp"),
        P("fsdp", None),
    )
    return jax.shard_map(body, mesh=mesh, in_specs=in_specs, out_specs=out_specs, check_vma=False)
```

```python
import jax
import jax.numpy as jnp
import numpy as np
from jax import lax
from jax.experimental import pallas as pl
from jax.experimental.pallas import tpu as pltpu
from jax.sharding import PartitionSpec as P

D = 2048
HEADS = 64
HEADDIM = 64
STATE = 128
KW = 4
GROUP = 256
DI = HEADS * HEADDIM
CONV = DI + 2 * STATE
PAIR = 2 * HEADDIM
EPS = 1e-05
SEG = 256
HALO = 8
SMALL = 32
TAIL = 32
ENDS = 64
VMEM_LIMIT = 56 * 1024 * 1024
F32 = jnp.float32
BF16 = jnp.bfloat16


def ring_place(index, n):
    return jnp.where(index % 2 == 0, index // 2, n - 1 - index // 2)


def ring_member(place, n):
    place = place % n
    return jnp.where(place < n // 2, 2 * place, 2 * (n - 1 - place) + 1)


def ring_routes(n):
    order = [2 * p if p < n // 2 else 2 * (n - 1 - p) + 1 for p in range(n)]
    forward = [(order[p], order[(p + 1) % n]) for p in range(n)]
    return forward, [(b, a) for a, b in forward]


def send(block, route):
    return lax.ppermute(block, "fsdp", route)


def after(value, *earlier):
    return lax.optimization_barrier((value, *earlier))[0]


def halves(rows):
    upper = -(-rows // 256) * 128 if rows >= 512 else rows // 2
    return upper, rows - upper


class Gather:
    def __init__(self, block, n):
        self.forward, self.backward = ring_routes(n)
        self.block, self.n = block, n
        self.latest = (block, block)
        self.ahead, self.behind = [], []

    def load(self):
        right, left = self.latest
        if len(self.ahead) == self.n // 2 - 1:
            upper, _ = halves(self.block.shape[0])
            return right[:upper], left[upper:]
        return right, left

    def fire(self, right, left):
        last = len(self.ahead) == self.n // 2 - 1
        self.latest = send(right, self.forward), send(left, self.backward)
        if not last:
            self.behind.insert(0, self.latest[0])
            self.ahead.append(self.latest[1])

    def parts(self):
        return [self.block] + self.ahead + list(self.latest) + self.behind


class Reduce:
    def __init__(self, chunk, n, pieces=None):
        self.forward, self.backward = ring_routes(n)
        self.chunk, self.n, self.step = chunk, n, n // 2
        if pieces is None:
            first = chunk(n // 2).astype(BF16)
            upper, _ = halves(first.shape[0])
            pieces = first[:upper], first[upper:]
        self.right, self.left = pieces
        self.upper = self.right.shape[0]

    def load(self):
        return self.right, self.left

    def fire(self, right, left):
        self.latest = send(right, self.forward), send(left, self.backward)
        self.step -= 1

    def join(self):
        right, left = (part.astype(F32) for part in self.latest)
        if self.step == 0:
            return self.chunk(0).astype(F32) + right + left
        own_right = self.chunk(self.step).astype(F32)
        own_left = self.chunk(self.n - self.step).astype(F32)
        cut = self.upper
        if self.step == self.n // 2 - 1:
            right = jnp.concatenate([own_right[:cut] + right, own_right[cut:]], axis=0)
            left = jnp.concatenate([own_left[:cut], own_left[cut:] + left], axis=0)
        else:
            right, left = own_right + right, own_left + left
        self.right, self.left = right.astype(BF16), left.astype(BF16)


def cut_in_two(grads_ref, right_ref, left_ref):
    upper = right_ref.shape[0]
    right_ref[...] = grads_ref[:upper]
    left_ref[...] = grads_ref[upper:]


def run_cut(grads, rows, block):
    shapes = [(half, SEG) for half in halves(rows)]
    return pl.pallas_call(
        cut_in_two,
        grid=(1,),
        in_specs=[pl.BlockSpec((rows, SEG), lambda i: (0, block))],
        out_specs=[pl.BlockSpec(shape, lambda i: (0, 0)) for shape in shapes],
        out_shape=[jax.ShapeDtypeStruct(shape, BF16) for shape in shapes],
        cost_estimate=busy(1, 1),
        name="cut_in_two",
    )(grads)


def barrier(value, *earlier):
    return lax.optimization_barrier((value, earlier))[0]


def next_hop(rings, inputs, *earlier):
    loads, inputs = barrier(([ring.load() for ring in rings], inputs), *earlier)
    for ring, load in zip(rings, loads):
        ring.fire(*load)
    return inputs


def arrivals(*rings):
    return sum((ring.latest for ring in rings), ())


def ctx_route(m, flip):
    return [(i, i ^ flip) for i in range(m)]


def far_share(block, m):
    return lax.ppermute(block, "ctx", ctx_route(m, 2))


def near_share(block, other, m):
    near = lax.ppermute(block, "ctx", ctx_route(m, 1))
    far = lax.ppermute(other, "ctx", ctx_route(m, 1))
    return [block, near, other, far]


def ctx_share(block, m):
    return near_share(block, far_share(block, m), m)


def gather_small(conv0, conv1, heads0, heads1, gate_ref, gain_ref, out_ref):
    out_ref[...] = jnp.zeros_like(out_ref)
    lines = [(conv0, k, conv1) for k in range(KW + 1)]
    lines += [(gate_ref, 0, None), (gate_ref, 1, None), (gain_ref, 0, None)]
    at = 0
    for ref, row, other in lines:
        for start in range(0, ref.shape[1], SEG):
            line = ref[row : row + 1, start : start + SEG]
            if other is not None:
                line = line + other[row : row + 1, start : start + SEG]
            out_ref[at : at + 1, :] = line
            at += 1
    at = out_ref.shape[0] - heads0.shape[0]
    out_ref[at:, :] = heads0[...] + heads1[...]


def run_gather_small(conv_grads, head_grads, gate_cols, d_gain):
    arrays = [*conv_grads, *head_grads, gate_cols, d_gain]
    lines = (KW + 1) * conv_grads[0].shape[1] + 2 * gate_cols.shape[1] + d_gain.shape[1]
    rows = -(-lines // SEG // 8) * 8 + head_grads[0].shape[0]
    return pl.pallas_call(
        gather_small,
        grid=(1,),
        in_specs=[pl.BlockSpec(v.shape, lambda i: (0, 0)) for v in arrays],
        out_specs=pl.BlockSpec((rows, SEG), lambda i: (0, 0)),
        out_shape=jax.ShapeDtypeStruct((rows, SEG), F32),
        cost_estimate=busy(1, 1),
        name="gather_small",
    )(*arrays)


class CtxReduce:
    def __init__(self, kept, given, m):
        self.m, place = m, lax.axis_index("ctx")
        self.core, self.across = place % 2, place // 2
        self.kept = kept
        self.near = lax.ppermute(given, "ctx", ctx_route(m, 1))

    def middle(self):
        self.both = self.kept.astype(F32) + self.near.astype(F32)
        self.sent = lax.dynamic_index_in_dim(self.both, 1 - self.across, 0, False).astype(BF16)

    def send_far(self):
        self.far = lax.ppermute(self.sent, "ctx", ctx_route(self.m, 2))

    def total(self):
        return lax.dynamic_index_in_dim(self.both, self.across, 0, False) + self.far.astype(F32)


def by_core(share, m):
    core = lax.axis_index("ctx") % 2
    split = share.reshape((m // 2, 2) + share.shape[1:])
    return (
        lax.dynamic_index_in_dim(split, core, 1, False),
        lax.dynamic_index_in_dim(split, 1 - core, 1, False),
    )


def ctx_sum(values, m):
    near, across, far = (lax.ppermute(values, "ctx", ctx_route(m, flip)) for flip in (1, 2, 3))
    return (values + near) + (across + far)


def nt(a, b):
    return lax.dot_general(a, b, (((1,), (1,)), ((), ())), preferred_element_type=F32)


def nn(a, b):
    return lax.dot_general(a, b, (((1,), (0,)), ((), ())), preferred_element_type=F32)


def tn(a, b):
    return lax.dot_general(a, b, (((0,), (0,)), ((), ())), preferred_element_type=F32)


def lanes(shape):
    return lax.broadcasted_iota(jnp.int32, shape, len(shape) - 1)


def busy(us, megabytes):
    return pl.CostEstimate(
        flops=int(us * 1e9), transcendentals=0, bytes_accessed=int(megabytes * 1e6)
    )


def softplus(v):
    return jnp.maximum(v, 0.0) + jnp.log1p(jnp.exp(-jnp.abs(v)))


def sigmoid(v):
    return 1.0 / (1.0 + jnp.exp(-v))


def ones_where(keep):
    row = lax.broadcasted_iota(jnp.int32, (GROUP, GROUP), 0)
    col = lax.broadcasted_iota(jnp.int32, (GROUP, GROUP), 1)
    return keep(row, col)


def exact(a, b):
    return lax.dot_general(
        a, b, (((1,), (0,)), ((), ())), preferred_element_type=F32, precision=lax.Precision.HIGHEST
    )


def tiles(width):
    return [slice(at, at + PAIR) for at in range(0, width, PAIR)]


def conv_tile(extended, taps_ref, cols):
    total = taps_ref[KW : KW + 1, cols]
    for k in range(KW):
        at = HALO - KW + 1 + k
        total = total + taps_ref[k : k + 1, cols] * extended[at : at + GROUP]
    return total


def by_segments(weights):
    n = D // SEG
    places = list(range(n // 2)) + [n // 2] * 2 + list(range(n // 2 + 1, n))
    at = [0] * len(places)
    at[n // 2 + 1] = weights[n // 2].shape[0]
    return list(zip(places, at, weights))


def project_into(out_ref, normed_ref, weights, total):
    whole = None
    for o, at, w in by_segments(weights):
        part = nt(normed_ref[:, o * SEG : (o + 1) * SEG], w[...])
        if o == D // SEG // 2:
            total[:, at : at + w.shape[0]] = part
        else:
            whole = part if whole is None else whole + part
    out_ref[...] = (whole + total[...]).astype(BF16)


def pack(
    place_ref, columns_ref, out_ref, small_ref, x_ref, z_ref, o_ref, steps, rows, sems,
):
    place = place_ref[0]
    pairs, m = z_ref.shape[0] // PAIR, out_ref.shape[0] // PAIR
    core = pairs * PAIR + 2 * STATE
    copies = [
        (columns_ref.at[pl.ds(DI + CONV, HEADS)], steps),
        (columns_ref.at[pl.ds(2 * DI, 2 * STATE)], x_ref.at[pl.ds(pairs * PAIR, 2 * STATE)]),
        (out_ref.at[pl.ds(pl.multiple_of(place * PAIR, PAIR), PAIR)], o_ref),
    ]
    for g in range(pairs):
        here = pl.ds(g * PAIR, PAIR)
        for start, ref in ((DI, x_ref), (0, z_ref)):
            at = pl.multiple_of(start + (g * m + place) * PAIR, PAIR)
            copies.append((columns_ref.at[pl.ds(at, PAIR)], ref.at[here]))
    copies = [pltpu.make_async_copy(*pair, sems.at[k]) for k, pair in enumerate(copies)]
    for copy in copies:
        copy.start()
    rows[...] = jnp.zeros_like(rows)
    rows[SMALL : SMALL + small_ref.shape[0], :] = small_ref[...].astype(F32)
    copies[0].wait()
    want = lax.broadcasted_iota(jnp.int32, (2 * pairs, HEADS), 0)
    have = lax.broadcasted_iota(jnp.int32, (2 * pairs, HEADS), 1)
    head = (want % pairs) * 2 * m + 2 * place + want // pairs
    rows[: 2 * pairs, :] = nn((have == head).astype(BF16), steps[...])
    x_ref[core : core + ENDS, :] = rows[...].astype(BF16)
    for copy in copies[1:]:
        copy.wait()


def run_pack(place, columns, w_out, small, pairs):
    rows = columns.shape[1]
    core = pairs * PAIR + 2 * STATE
    anywhere = pl.BlockSpec(memory_space=pl.ANY)
    shapes = [(core + ENDS, rows), (pairs * PAIR, rows), (PAIR, D)]
    return pl.pallas_call(
        pack,
        grid_spec=pltpu.PrefetchScalarGridSpec(
            num_scalar_prefetch=1,
            grid=(1,),
            in_specs=[anywhere, anywhere, pl.BlockSpec(small.shape, lambda i, t: (0, 0))],
            out_specs=[pl.BlockSpec(shape, lambda i, t: (0, 0)) for shape in shapes],
            scratch_shapes=[
                pltpu.VMEM((HEADS, rows), BF16),
                pltpu.VMEM((ENDS, rows), F32),
                pltpu.SemaphoreType.DMA((2 * pairs + 3,)),
            ],
        ),
        out_shape=[jax.ShapeDtypeStruct(shape, BF16) for shape in shapes],
        compiler_params=pltpu.CompilerParams(vmem_limit_bytes=VMEM_LIMIT),
        name="pack",
    )(place, columns, w_out, small)


def collect(members_ref, *refs):
    out_ref = refs[-1]
    for o, ref in enumerate(refs[:-1]):
        out_ref[members_ref[o]] = ref[...].astype(F32)


def run_collect(members, parts):
    n = len(parts) - 1
    lasts = parts[: n // 2] + parts[n // 2 + 1 :]
    at = lambda part: (part.shape[0] - ENDS + SMALL) // 32
    return pl.pallas_call(
        collect,
        grid_spec=pltpu.PrefetchScalarGridSpec(
            num_scalar_prefetch=1,
            grid=(1,),
            in_specs=[pl.BlockSpec((32, SEG), lambda i, t, k=at(p): (k, 0)) for p in lasts],
            out_specs=pl.BlockSpec((n, 32, SEG), lambda i, t: (0, 0, 0)),
        ),
        out_shape=jax.ShapeDtypeStruct((n, 32, SEG), F32),
        compiler_params=pltpu.CompilerParams(vmem_limit_bytes=VMEM_LIMIT),
        cost_estimate=busy(1, 1),
        name="collect",
    )(members, *lasts)


def front(members_ref, tokens_ref, *refs):
    weights, (normed_ref, proj_ref, total) = refs[:-3], refs[-3:]
    tokens = tokens_ref[...].astype(F32)
    inv = lax.rsqrt(jnp.mean(tokens * tokens, axis=-1, keepdims=True) + EPS)
    for o in range(D // SEG):
        at = pl.multiple_of(members_ref[o] * SEG, SEG)
        cols = slice(o * SEG, (o + 1) * SEG)
        last = weights[o if o < D // SEG // 2 else o + 1]
        row = last.shape[0] - ENDS + SMALL
        gain = last[row : row + 16, :].astype(F32)[0:1]
        part = tokens_ref[:, pl.ds(at, SEG)].astype(F32) * inv * gain
        normed_ref[:, cols] = part.astype(BF16)
    project_into(proj_ref, normed_ref, weights, total)


def resident(array, grid_args=1):
    zeros = (0,) * array.ndim
    maps = {1: lambda i: zeros, 2: lambda i, t: zeros, 3: lambda i, t, p: zeros}
    return pl.BlockSpec(array.shape, maps[grid_args], pipeline_mode=pl.Buffered(1))


def run_front(members, tokens, weights):
    length, cols = tokens.shape[0], weights[0].shape[0]
    return pl.pallas_call(
        front,
        grid_spec=pltpu.PrefetchScalarGridSpec(
            num_scalar_prefetch=1,
            grid=(length // GROUP,),
            in_specs=[
                pl.BlockSpec((GROUP, D), lambda i, t: (i, 0)),
            ]
            + [resident(w, 2) for w in weights],
            out_specs=[
                pl.BlockSpec((GROUP, D), lambda i, t: (i, 0)),
                pl.BlockSpec((GROUP, cols), lambda i, t: (i, 0)),
            ],
            scratch_shapes=[pltpu.VMEM((GROUP, cols), F32)],
        ),
        out_shape=[
            jax.ShapeDtypeStruct((length, D), BF16),
            jax.ShapeDtypeStruct((length, cols), BF16),
        ],
        compiler_params=pltpu.CompilerParams(vmem_limit_bytes=VMEM_LIMIT),
        cost_estimate=busy(12, 18),
        name="front",
    )(members, tokens, *weights)


def project(normed_ref, *refs):
    project_into(refs[-2], normed_ref, refs[:-2], refs[-1])


def run_project(normed, weights):
    length, cols = normed.shape[0], weights[0].shape[0]
    return pl.pallas_call(
        project,
        grid=(length // GROUP,),
        in_specs=[pl.BlockSpec((GROUP, D), lambda i: (i, 0))] + [resident(w) for w in weights],
        out_specs=pl.BlockSpec((GROUP, cols), lambda i: (i, 0)),
        out_shape=jax.ShapeDtypeStruct((length, cols), BF16),
        scratch_shapes=[pltpu.VMEM((GROUP, cols), F32)],
        compiler_params=pltpu.CompilerParams(vmem_limit_bytes=VMEM_LIMIT),
        cost_estimate=busy(8, 10),
        name="project",
    )(normed, *weights)


def spread_rows(ref, index, rows):
    count = rows.shape[0]
    ref[pl.ds(index, count), :] = rows[:, :128]
    ref[pl.ds(ref.shape[0] // 2 + index, count), :] = rows[:, 128:]


def all_rows(stack):
    half = stack.shape[0] // 2
    return jnp.concatenate([stack[:half], stack[half:]], axis=1)


def pair_rows(ref, g, pairs):
    half = 8 * pairs
    return jnp.concatenate(
        [ref[pl.ds(g, 8, stride=pairs), :], ref[pl.ds(half + g, 8, stride=pairs), :]], axis=1
    )


def high_low(v):
    high = v.astype(BF16)
    return high, (v - high.astype(F32)).astype(BF16)


def tri_units(back):
    units = []
    for r in range(GROUP // 64):
        for t in range(GROUP // 128):
            if (t >= r // 2) if back else (t <= r // 2):
                units.append((slice(64 * r, 64 * r + 64), slice(128 * t, 128 * t + 128), t == r // 2))
    return units


def diagonal(keep):
    row = lax.broadcasted_iota(jnp.int32, (128, 128), 0)
    col = lax.broadcasted_iota(jnp.int32, (128, 128), 1)
    return jnp.where(keep(row, col), 0.0, -1e30)


def mix_forward(
    proj_ref, taps_ref, heads_ref, skip_ref, act_ref, table_ref, y_ref, start_ref,
    state, halo, gram, bias, scores,
):
    pairs = state.shape[0]
    heads, width = 2 * pairs, pairs * PAIR
    core = width + 2 * STATE

    @pl.when(pl.program_id(0) == 0)
    def _():
        state[...] = jnp.zeros_like(state)
        halo[...] = jnp.zeros_like(halo)
        scores[...] = jnp.zeros_like(scores)
        bias[...] = diagonal(lambda row, col: row >= col)

    def activate(cols):
        current = proj_ref[:, cols].astype(F32)
        conv = conv_tile(jnp.concatenate([halo[:, cols], current], axis=0), taps_ref, cols)
        halo[:, cols] = current[GROUP - HALO :]
        act = (conv * sigmoid(conv)).astype(BF16)
        act_ref[:, cols] = act
        return act

    bs = activate(slice(width, width + STATE))
    cs = activate(slice(width + STATE, core))
    raw = proj_ref[:, core : core + ENDS].astype(F32).T[:heads]
    dt = softplus(raw + heads_ref[:heads, 0:1])
    upto = ones_where(lambda row, col: row <= col).astype(F32)
    cum = exact(dt * heads_ref[heads:, 0:1], upto)
    last = cum[:, GROUP - 1 :]
    table = jnp.concatenate([cum, dt, jnp.exp(last - cum) * dt, jnp.exp(cum)], axis=0)
    spread_rows(table_ref.at[0], 0, table)
    gram[...] = nt(cs, bs)
    bs_t = bs.astype(F32).T

    def one(g, unused):
        cols = pl.ds(pl.multiple_of(g * PAIR, PAIR), PAIR)
        rows = pair_rows(table_ref.at[0], g, pairs)
        turned = rows.T
        x = activate(cols)
        first = lanes(x.shape) < HEADDIM
        start = state[g]
        start_ref[0, g] = start
        inner = nn(cs, start.astype(BF16))
        parts, locals_ = [], []
        for e in range(2):
            for at, to, on in tri_units(False):
                differ = turned[at, e : e + 1] - rows[e : e + 1, to]
                if on:
                    differ = differ + bias[at.start % 128 : at.start % 128 + 64, :]
                decay = jnp.exp(differ)
                scores[e, at, to] = (gram[at, to] * decay * rows[2 + e : 3 + e, to]).astype(BF16)
            parts.append(nn(scores[e], x))
            locals_.append(nn((bs_t * rows[4 + e : 5 + e, :]).astype(BF16), x))
        grow = jnp.where(first, turned[:, 6:7], turned[:, 7:8])
        y_ref[:, cols] = (
            jnp.where(first, parts[0], parts[1]) + grow * inner + skip_ref[:, cols] * x.astype(F32)
        )
        shrink = jnp.where(first[:1], rows[6:7, GROUP - 1 :], rows[7:8, GROUP - 1 :])
        state[g] = shrink * start + jnp.where(first[:STATE], locals_[0], locals_[1])
        return unused

    lax.fori_loop(0, pairs, one, 0, unroll=2)


def run_mix_forward(proj, taps, heads_in, skip, pairs):
    length = proj.shape[0]
    blocks, width = length // GROUP, pairs * PAIR
    core = width + 2 * STATE
    whole = lambda i: (0, 0)
    return pl.pallas_call(
        mix_forward,
        grid=(blocks,),
        in_specs=[
            pl.BlockSpec((GROUP, proj.shape[1]), lambda i: (i, 0)),
            pl.BlockSpec(taps.shape, whole),
            pl.BlockSpec(heads_in.shape, whole),
            pl.BlockSpec(skip.shape, whole),
        ],
        out_specs=[
            pl.BlockSpec((GROUP, core), lambda i: (i, 0)),
            pl.BlockSpec((1, 16 * pairs, 128), lambda i: (i, 0, 0)),
            pl.BlockSpec((GROUP, width), lambda i: (i, 0)),
            pl.BlockSpec((1, pairs, STATE, PAIR), lambda i: (i, 0, 0, 0)),
        ],
        out_shape=[
            jax.ShapeDtypeStruct((length, core), BF16),
            jax.ShapeDtypeStruct((blocks, 16 * pairs, 128), F32),
            jax.ShapeDtypeStruct((length, width), F32),
            jax.ShapeDtypeStruct((blocks, pairs, STATE, PAIR), F32),
        ],
        scratch_shapes=[
            pltpu.VMEM((pairs, STATE, PAIR), F32),
            pltpu.VMEM((HALO, core), F32),
            pltpu.VMEM((GROUP, GROUP), F32),
            pltpu.VMEM((128, 128), F32),
            pltpu.VMEM((2, GROUP, GROUP), BF16),
        ],
        compiler_params=pltpu.CompilerParams(vmem_limit_bytes=VMEM_LIMIT),
        cost_estimate=busy(18, 15),
        name="mix_forward",
    )(proj, taps, heads_in, skip)


def mix_backward(
    top, follows, act_ref, proj_ref, prev_ref, taps_ref, heads_ref, skip_ref, table_ref, start_ref, dy_ref,
    carry_in, halo_in, held_ref, dx_ref, grads_ref, dheads_ref, carried, halo,
    gram, dgram, bias, d_scores, scores, db, dc, found, ends,
):
    pairs = carried.shape[0]
    heads, width = 2 * pairs, pairs * PAIR
    core = width + 2 * STATE
    step = pl.program_id(0)

    @pl.when(step == 0)
    def _():
        carried[...] = carry_in[...] if follows else jnp.zeros_like(carried)
        halo[...] = halo_in[...] if follows else jnp.zeros_like(halo)
        grads_ref[...] = jnp.zeros_like(grads_ref)
        dheads_ref[...] = jnp.zeros_like(dheads_ref)
        scores[...] = jnp.zeros_like(scores)
        bias[...] = diagonal(lambda row, col: row <= col)

    has_prev = jnp.where(top - step > 0, 1.0, 0.0)
    bs, cs = act_ref[:, width : width + STATE], act_ref[:, width + STATE : core]
    bs_float = bs.astype(F32)
    cs_t = cs.astype(F32).T.astype(BF16)
    gram[...] = nt(bs, cs)
    for ref in (dgram, db, dc):
        ref[...] = jnp.zeros_like(ref)

    def conv_back(d_act, cols):
        before = prev_ref[:, cols].astype(F32)[prev_ref.shape[0] - HALO :] * has_prev
        extended = jnp.concatenate([before, proj_ref[:, cols].astype(F32)], axis=0)
        conv = conv_tile(extended, taps_ref, cols)
        sig = sigmoid(conv)
        d_conv = d_act * (sig * (1.0 + conv * (1.0 - sig)))
        onward = jnp.concatenate([d_conv, halo[:, cols]], axis=0)
        d_in = taps_ref[KW - 1 : KW, cols] * d_conv
        for k in range(KW - 1):
            at = KW - 1 - k
            d_in = d_in + taps_ref[k : k + 1, cols] * onward[at : at + GROUP]
        dx_ref[:, cols] = d_in.astype(BF16)
        sums = []
        for k in range(KW):
            at = HALO - KW + 1 + k
            sums.append(jnp.sum(d_conv * extended[at : at + GROUP], axis=0, keepdims=True))
        sums.append(jnp.sum(d_conv, axis=0, keepdims=True))
        sums.append(jnp.zeros((8 - KW - 1, sums[0].shape[1]), F32))
        grads_ref[:, cols] += jnp.concatenate(sums, axis=0)
        halo[:, cols] = d_conv[:HALO]

    def one(g, unused):
        cols = pl.ds(pl.multiple_of(g * PAIR, PAIR), PAIR)
        rows = pair_rows(table_ref.at[0], g, pairs)
        turned = rows.T
        x, dy = act_ref[:, cols], dy_ref[:, cols]
        first = lanes(x.shape) < HEADDIM
        dy_float = dy.astype(F32)
        start, grad = start_ref[0, g], carried[g]
        start_low, grad_low = start.astype(BF16), grad.astype(BF16)
        inner = nn(cs, start_low)
        grow = jnp.where(first, turned[:, 6:7], turned[:, 7:8])
        d_inner = (dy_float * grow).astype(BF16)
        dc[...] += nt(d_inner, start_low)
        touched = dy_float * inner
        held = jnp.sum(grad * start, axis=0, keepdims=True)
        zero = jnp.zeros_like(x)
        reach = nn(bs, grad_low)
        sent = x.astype(F32) * jnp.where(first, turned[:, 4:5], turned[:, 5:6])
        for half in high_low(sent):
            db[...] += nt(half, grad_low)
        parts, sums_j, linked = [], [], []
        for e in range(2):
            own = first if e == 0 else jnp.logical_not(first)
            d_scores[e] = nt(jnp.where(own, x, zero), dy)
            linked_i, linked_j = {}, {}
            for at, to, on in tri_units(True):
                dt_col = turned[at, 2 + e : 3 + e]
                differ = rows[e : e + 1, to] - turned[at, e : e + 1]
                if on:
                    differ = differ + bias[at.start % 128 : at.start % 128 + 64, :]
                decay = jnp.exp(differ)
                grown = gram[at, to] * decay
                d_score = d_scores[e, at, to]
                score = grown * dt_col
                scores[e, at, to] = score.astype(BF16)
                dgram[at, to] += d_score * decay * dt_col
                along_i = d_score * grown
                along_j = jnp.sum(d_score * score, axis=0, keepdims=True)
                key_i, key_j = at.start, to.start
                linked_i[key_i] = along_i if key_i not in linked_i else linked_i[key_i] + along_i
                linked_j[key_j] = along_j if key_j not in linked_j else linked_j[key_j] + along_j
            sums_j.append(jnp.concatenate([linked_j[k] for k in sorted(linked_j)], axis=1))
            linked.append(jnp.concatenate([linked_i[k] for k in sorted(linked_i)], axis=0))
            tail_col = turned[:, 4 + e : 5 + e]
            parts.append(nn(scores[e], dy) + nn((bs_float * tail_col).astype(BF16), grad_low))
        pick = lax.broadcasted_iota(jnp.int32, (8, 2 * PAIR), 0)
        lane = lanes((8, 2 * PAIR))
        by_head = (pick == lane // HEADDIM).astype(BF16)
        by_pair = (pick == 4 + lane // PAIR).astype(BF16)
        kept = jnp.zeros((8, GROUP), F32)
        for sums, select in (
            ((x.astype(F32) * reach, touched), by_head),
            (linked, by_pair),
        ):
            for half in high_low(jnp.concatenate(sums, axis=1)):
                kept = kept + nt(select, half)
        kept = jnp.concatenate([kept[:6]] + sums_j, axis=0)
        found[pl.ds(g, 8, stride=pairs), :] = kept[:, :128]
        found[pl.ds(8 * pairs + g, 8, stride=pairs), :] = kept[:, 128:]
        ends[pl.ds(g, 2, stride=pairs), :] = jnp.concatenate(
            [jnp.where(first[:1], held, 0.0), jnp.where(first[:1], 0.0, held)], axis=0
        )
        conv_back(jnp.where(first, parts[0], parts[1]) + skip_ref[:, cols] * dy_float, cols)
        shrink = jnp.where(first[:1], rows[6:7, GROUP - 1 :], rows[7:8, GROUP - 1 :])
        carried[g] = shrink * grad + nn(cs_t, d_inner)
        return unused

    lax.fori_loop(0, pairs, one, 0, unroll=2)
    low = dgram[...].astype(BF16)
    conv_back(db[...] + nn(low, cs), slice(width, width + STATE))
    conv_back(dc[...] + tn(low, bs), slice(width + STATE, core))

    rows, sums = all_rows(table_ref[0]), all_rows(found[...])
    d_tail, touched, sum_i, sum_j = (sums[k * heads : (k + 1) * heads] for k in range(4))
    cum, dt, tail, growth = (rows[k * heads : (k + 1) * heads] for k in range(4))
    a_neg = heads_ref[heads:, 0:1]
    tail_log = d_tail * tail
    d_last = jnp.sum(tail_log, axis=1, keepdims=True)
    d_last = d_last + jnp.sum(ends[...], axis=1, keepdims=True) * growth[:, GROUP - 1 :]
    d_cum = touched * growth - tail_log + sum_j - dt * sum_i
    d_cum = d_cum + jnp.where(lanes(d_cum.shape) == GROUP - 1, d_last, 0.0)
    d_rate = exact(d_cum, ones_where(lambda row, col: row >= col).astype(F32))
    raw = proj_ref[:, core : core + ENDS].astype(F32).T[:heads]
    d_step = d_tail * jnp.exp(cum[:, GROUP - 1 :] - cum) + sum_i
    d_dt = (d_step + d_rate * a_neg) * sigmoid(raw + heads_ref[:heads, 0:1])
    dheads_ref[:heads, :] += d_dt
    dheads_ref[heads:, :] += d_rate * dt
    filled = jnp.concatenate([d_dt, jnp.zeros((ENDS - heads, GROUP), F32)], axis=0)
    dx_ref[:, core : core + ENDS] = filled.T.astype(BF16)


def run_mix_backward(span, top, act, proj, taps, heads_in, skip, table, starts, dy, before):
    pairs = starts.shape[1]
    follows = before is not None
    held, carry, halo = before if follows else (dy, skip[:, :128], skip[:, :128])
    heads, width = 2 * pairs, pairs * PAIR
    core = width + 2 * STATE
    whole = lambda i: (0, 0)
    block = lambda i: (top - i, 0)
    above = GROUP // 16
    return pl.pallas_call(
        lambda *refs: mix_backward(top, follows, *refs),
        grid=(span,),
        in_specs=[
            pl.BlockSpec((GROUP, core), block),
            pl.BlockSpec((GROUP, proj.shape[1]), block),
            pl.BlockSpec((16, proj.shape[1]), lambda i: (jnp.maximum((top - i) * above - 1, 0), 0)),
            pl.BlockSpec(taps.shape, whole),
            pl.BlockSpec(heads_in.shape, whole),
            pl.BlockSpec(skip.shape, whole),
            pl.BlockSpec((1, 16 * pairs, 128), lambda i: (top - i, 0, 0)),
            pl.BlockSpec((1, pairs, STATE, PAIR), lambda i: (top - i, 0, 0, 0)),
            pl.BlockSpec((GROUP, width), block),
            pl.BlockSpec(carry.shape, lambda i: (0,) * carry.ndim),
            pl.BlockSpec(halo.shape, whole),
            pl.BlockSpec(memory_space=pl.ANY),
        ],
        out_specs=[
            pl.BlockSpec((GROUP, proj.shape[1]), block),
            pl.BlockSpec((8, core), whole),
            pl.BlockSpec((2 * heads, GROUP), whole),
            pl.BlockSpec((pairs, STATE, PAIR), lambda i: (0, 0, 0)),
            pl.BlockSpec((HALO, core), whole),
        ],
        out_shape=[
            jax.ShapeDtypeStruct(proj.shape, BF16),
            jax.ShapeDtypeStruct((8, core), F32),
            jax.ShapeDtypeStruct((2 * heads, GROUP), F32),
            jax.ShapeDtypeStruct((pairs, STATE, PAIR), F32),
            jax.ShapeDtypeStruct((HALO, core), F32),
        ],
        scratch_shapes=[
            pltpu.VMEM((GROUP, GROUP), F32),
            pltpu.VMEM((GROUP, GROUP), F32),
            pltpu.VMEM((128, 128), F32),
            pltpu.VMEM((2, GROUP, GROUP), F32),
            pltpu.VMEM((2, GROUP, GROUP), BF16),
            pltpu.VMEM((GROUP, STATE), F32),
            pltpu.VMEM((GROUP, STATE), F32),
            pltpu.VMEM((8 * heads, 128), F32),
            pltpu.VMEM((heads, PAIR), F32),
        ],
        compiler_params=pltpu.CompilerParams(vmem_limit_bytes=VMEM_LIMIT),
        input_output_aliases={11: 0} if follows else {},
        cost_estimate=busy(12 * span, 5 * span),
        name="mix_backward",
    )(act, proj, proj, taps, heads_in, skip, table, starts, dy, carry, halo, held)


def gate_sums(members_ref, seed_ref, z_ref, y_ref, gain_ref, *refs):
    parts, (w_ref, scaled_ref, sums_ref, squares, along) = refs[:-5], refs[-5:]
    step, n = pl.program_id(0), len(refs[:-5]) - 1

    @pl.when(step == 0)
    def _():
        squares[...] = jnp.zeros_like(squares)
        along[...] = jnp.zeros_like(along)
        places = list(range(n // 2)) + [n // 2] * 2 + list(range(n // 2 + 1, n))
        for k, (o, part) in enumerate(zip(places, parts)):
            at = pl.multiple_of(members_ref[o] * PAIR, PAIR)
            if k == n // 2 + 1:
                at = at + PAIR - part.shape[0]
            w_ref[pl.ds(at, part.shape[0]), :] = part[...]

    tile = z_ref.shape[1]
    scaled = nt(seed_ref[...], w_ref[pl.ds(pl.multiple_of(step * tile, tile), tile), :])
    scaled_ref[...] = scaled
    z = z_ref[...].astype(F32)
    gated = y_ref[...] * (z * sigmoid(z))
    square = gated * gated
    lean = scaled * gain_ref[...] * gated
    for cols in tiles(square.shape[1]):
        squares[...] += square[:, cols]
        along[...] += lean[:, cols]

    @pl.when(step == pl.num_programs(0) - 1)
    def _():
        spot = lanes(squares.shape)
        both = jnp.where(
            spot == 0,
            jnp.sum(squares[...], axis=1, keepdims=True),
            jnp.where(spot == 1, jnp.sum(along[...], axis=1, keepdims=True), 0.0),
        )
        sums_ref[...] = both.T[:8]


def run_gate_sums(members, seed, parts, z, y, gain):
    length, width = y.shape
    tile = 2 * PAIR
    col = pl.BlockSpec((length, tile), lambda i, t: (0, i))
    return pl.pallas_call(
        gate_sums,
        grid_spec=pltpu.PrefetchScalarGridSpec(
            num_scalar_prefetch=1,
            grid=(width // tile,),
            in_specs=[resident(seed, 2), col, col, pl.BlockSpec((1, tile), lambda i, t: (0, i))]
            + [resident(part, 2) for part in parts],
            out_specs=[
                pl.BlockSpec((width, D), lambda i, t: (0, 0)),
                col,
                pl.BlockSpec((8, length), lambda i, t: (0, 0)),
            ],
            scratch_shapes=[pltpu.VMEM((length, PAIR), F32)] * 2,
        ),
        out_shape=[
            jax.ShapeDtypeStruct((width, D), BF16),
            jax.ShapeDtypeStruct(y.shape, F32),
            jax.ShapeDtypeStruct((8, length), F32),
        ],
        compiler_params=pltpu.CompilerParams(vmem_limit_bytes=VMEM_LIMIT),
        cost_estimate=busy(11, 20),
        name="gate_sums",
    )(members, seed, z, y, gain, *parts)


def gate_back(sums_ref, scaled_ref, z_ref, y_ref, x_ref, gain_ref, mixed_ref, dy_ref, dz_ref, cols_ref, turned):
    @pl.when(pl.program_id(0) == 0)
    def _():
        inv = lax.rsqrt(sums_ref[0:1, :] / DI + EPS)
        slope = inv * inv * inv * (sums_ref[1:2, :] / DI)
        rest = jnp.zeros((PAIR - 2, sums_ref.shape[1]), F32)
        both = jnp.concatenate([inv, slope, rest], axis=0).T
        turned[0] = jnp.broadcast_to(both[:, 0:1], turned.shape[1:])
        turned[1] = jnp.broadcast_to(both[:, 1:2], turned.shape[1:])

    inv, slope = turned[0], turned[1]
    z, y, scaled, gain = z_ref[...].astype(F32), y_ref[...], scaled_ref[...], gain_ref[...]
    sig = sigmoid(z)
    silu = z * sig
    gated = y * silu
    normal = gated * inv
    mixed_ref[...] = (normal * gain).astype(BF16)
    d_gated = scaled * gain * inv - gated * slope
    dy = (d_gated * silu).astype(BF16)
    dy_ref[...] = dy
    dz_ref[...] = (d_gated * y * (sig * (1.0 + z * (1.0 - sig)))).astype(BF16)
    cols_ref[0:1, :] = jnp.sum(scaled * normal, axis=0, keepdims=True)
    cols_ref[1:2, :] = jnp.sum(dy.astype(F32) * x_ref[...].astype(F32), axis=0, keepdims=True)
    cols_ref[2:, :] = jnp.zeros_like(cols_ref[2:, :])


def run_gate_back(sums, scaled, z, y, x, gain):
    length, width = y.shape
    tile = 2 * PAIR
    col = pl.BlockSpec((length, tile), lambda i: (0, i))
    low = jax.ShapeDtypeStruct(y.shape, BF16)
    return pl.pallas_call(
        gate_back,
        grid=(width // tile,),
        in_specs=[
            pl.BlockSpec(sums.shape, lambda i: (0, 0)),
            col,
            col,
            col,
            col,
            pl.BlockSpec((1, tile), lambda i: (0, i)),
        ],
        out_specs=[col, col, col, pl.BlockSpec((8, tile), lambda i: (0, i))],
        out_shape=[low, low, low, jax.ShapeDtypeStruct((8, width), F32)],
        scratch_shapes=[pltpu.VMEM((2, length, 2 * PAIR), F32)],
        compiler_params=pltpu.CompilerParams(vmem_limit_bytes=VMEM_LIMIT),
        cost_estimate=busy(11, 20),
        name="gate_back",
    )(sums, scaled, z, y, x, gain)


def keep_or_give(place_ref, value, keep_ref, give_ref):
    mine = place_ref[0] % 2 == pl.program_id(0) % 2

    @pl.when(mine)
    def _():
        keep_ref[0] = value

    @pl.when(jnp.logical_not(mine))
    def _():
        give_ref[0] = value


def back_norm(members_ref, place_ref, tokens_ref, dz_ref, dx_ref, *refs):
    parts, (keep_ref, give_ref, gain_ref, dn_ref) = refs[:-4], refs[-4:]
    count = len(parts) // 2

    @pl.when(pl.program_id(0) == 0)
    def _():
        gain_ref[...] = jnp.zeros_like(gain_ref)

    tokens = tokens_ref[...].astype(F32)
    inv = lax.rsqrt(jnp.mean(tokens * tokens, axis=-1, keepdims=True) + EPS)
    sums = [None] * (D // SEG)
    for source, weights in ((dz_ref, parts[:count]), (dx_ref, parts[count:])):
        for o, at, w in by_segments(weights):
            part = nn(source[:, at : at + w.shape[0]], w[...])
            sums[o] = part if sums[o] is None else sums[o] + part
    for o, d_normed in enumerate(sums):
        at = pl.multiple_of(members_ref[o] * SEG, SEG)
        dn_ref[:, pl.ds(at, SEG)] = d_normed.astype(BF16)
        scaled = tokens_ref[:, pl.ds(at, SEG)].astype(F32) * inv
        gain_ref[0:1, pl.ds(at, SEG)] += jnp.sum(d_normed * scaled, axis=0, keepdims=True)
    keep_or_give(place_ref, dn_ref[...], keep_ref, give_ref)


def run_back_norm(members, place, tokens, dz, dx, weights_z, weights_x):
    length = tokens.shape[0]
    row = lambda i, t, p: (i, 0)
    half = pl.BlockSpec((1, GROUP, D), lambda i, t, p: (i // 2, 0, 0))
    halves_shape = jax.ShapeDtypeStruct((length // GROUP // 2, GROUP, D), BF16)
    return pl.pallas_call(
        back_norm,
        grid_spec=pltpu.PrefetchScalarGridSpec(
            num_scalar_prefetch=2,
            grid=(length // GROUP,),
            in_specs=[
                pl.BlockSpec((GROUP, D), row),
                pl.BlockSpec((GROUP, dz.shape[1]), row),
                pl.BlockSpec((GROUP, dx.shape[1]), row),
            ]
            + [resident(w, 3) for w in weights_z + weights_x],
            out_specs=[half, half, pl.BlockSpec((8, D), lambda i, t, p: (0, 0))],
            scratch_shapes=[pltpu.VMEM((GROUP, D), BF16)],
        ),
        out_shape=[halves_shape, halves_shape, jax.ShapeDtypeStruct((8, D), F32)],
        compiler_params=pltpu.CompilerParams(vmem_limit_bytes=VMEM_LIMIT),
        cost_estimate=busy(18, 24),
        name="back_norm",
    )(members, place, tokens, dz, dx, *weights_z, *weights_x)


def assemble_o(place_ref, o0, o1, o2, o3, out_ref):
    for k, ref in enumerate((o0, o1, o2, o3)):

        @pl.when(pl.program_id(0) == k)
        def _():
            out_ref[...] = ref[...].astype(F32)


def run_assemble_o(place, shares):
    m, (rows, cols) = len(shares), shares[0].shape
    return pl.pallas_call(
        assemble_o,
        grid_spec=pltpu.PrefetchScalarGridSpec(
            num_scalar_prefetch=1,
            grid=(m,),
            in_specs=[resident(share, 2) for share in shares],
            out_specs=pl.BlockSpec((rows, cols), lambda i, t: (t[0] ^ i, 0)),
        ),
        out_shape=jax.ShapeDtypeStruct((m * rows, cols), F32),
        compiler_params=pltpu.CompilerParams(vmem_limit_bytes=VMEM_LIMIT),
        cost_estimate=busy(3, 3),
        name="assemble_o",
    )(place, *shares)


def put_pairs(place_ref, refs, out_ref, g):
    m = len(refs)
    for k, ref in enumerate(refs):
        to = pl.multiple_of((place_ref[0] ^ k) * PAIR, PAIR)
        out_ref[pl.ds(to, PAIR), :] = ref[pl.ds(pl.multiple_of(g * PAIR, PAIR), PAIR), :].astype(F32)


def assemble_z(place_ref, z0, z1, z2, z3, out_ref):
    put_pairs(place_ref, (z0, z1, z2, z3), out_ref, pl.program_id(0))


def assemble_a(place_ref, held_ref, a0, a1, a2, a3, out_ref):
    put_pairs(place_ref, (a0, a1, a2, a3), out_ref, pl.program_id(0))


def assemble_b(place_ref, order_ref, held_ref, b0, b1, b2, b3, out_ref):
    step, last = pl.program_id(0), pl.num_programs(0) - 1
    refs = (b0, b1, b2, b3)
    width = last * PAIR
    core = width + 2 * STATE

    @pl.when(step < last)
    def _():
        put_pairs(place_ref, refs, out_ref, step)

    @pl.when(step == last)
    def _():
        total = jnp.zeros((2 * STATE, out_ref.shape[1]), F32)
        steps = jnp.zeros((HEADS, out_ref.shape[1]), F32)
        for k, x in enumerate(refs):
            total = total + x[width:core].astype(F32)
            steps = steps + nn(order_ref[place_ref[0] ^ k], x[core : core + TAIL])
        out_ref[: 2 * STATE] = total
        out_ref[2 * STATE : 2 * STATE + HEADS] = steps


def run_assemble_z(place, shares, columns):
    m, rows = len(shares), shares[0].shape[1]
    tile = m * PAIR
    return pl.pallas_call(
        assemble_z,
        grid_spec=pltpu.PrefetchScalarGridSpec(
            num_scalar_prefetch=1,
            grid=(DI // tile,),
            in_specs=[resident(s, 2) for s in shares],
            out_specs=pl.BlockSpec((tile, rows), lambda i, t: (i, 0)),
        ),
        out_shape=jax.ShapeDtypeStruct((columns, rows), F32),
        compiler_params=pltpu.CompilerParams(vmem_limit_bytes=VMEM_LIMIT),
        cost_estimate=busy(4, 6),
        name="assemble_z",
    )(place, *shares)


def run_assemble_b(place, order, held, shares, count):
    m, rows = len(shares), shares[0].shape[1]
    tile = m * PAIR
    first = 2 * (DI // tile) - count
    return pl.pallas_call(
        assemble_b,
        grid_spec=pltpu.PrefetchScalarGridSpec(
            num_scalar_prefetch=1,
            grid=(count + 1,),
            in_specs=[resident(order, 2), pl.BlockSpec(memory_space=pl.ANY)]
            + [resident(s, 2) for s in shares],
            out_specs=pl.BlockSpec((tile, rows), lambda i, t: (i + first, 0)),
        ),
        out_shape=jax.ShapeDtypeStruct(held.shape, F32),
        input_output_aliases={2: 0},
        compiler_params=pltpu.CompilerParams(vmem_limit_bytes=VMEM_LIMIT),
        cost_estimate=busy(3, 2),
        name="assemble_b",
    )(place, order, held, *shares)


def run_assemble_a(place, held, shares):
    m, rows = len(shares), shares[0].shape[1]
    tile = m * PAIR
    return pl.pallas_call(
        assemble_a,
        grid_spec=pltpu.PrefetchScalarGridSpec(
            num_scalar_prefetch=1,
            grid=(shares[0].shape[0] // PAIR,),
            in_specs=[pl.BlockSpec(memory_space=pl.ANY)] + [resident(s, 2) for s in shares],
            out_specs=pl.BlockSpec((tile, rows), lambda i, t: (i + DI // tile, 0)),
        ),
        out_shape=jax.ShapeDtypeStruct(held.shape, F32),
        input_output_aliases={1: 0},
        compiler_params=pltpu.CompilerParams(vmem_limit_bytes=VMEM_LIMIT),
        cost_estimate=busy(4, 5),
        name="assemble_a",
    )(place, held, *shares)


def body(
    tokens, norm_gain, w_in, conv_w, conv_b, dt_bias, a_log, d_skip, gate_gain, w_out, cotangent
):
    n, m = lax.axis_size("fsdp"), lax.axis_size("ctx")
    place = lax.axis_index("ctx")
    piece = tokens.shape[1]
    length = piece * m
    blocks = length // GROUP
    pairs = DI // PAIR // m
    width = pairs * PAIR
    heads = 2 * pairs
    rows = w_in.shape[0]
    core_cols = width + 2 * STATE
    head_cols = core_cols + heads
    ring = rows == SEG and (DI // PAIR) // n == m

    def of_pairs(array, axis):
        shape = array.shape
        each = shape[axis] // (pairs * m)
        split = array.reshape(shape[:axis] + (pairs, m, each) + shape[axis + 1 :])
        mine = lax.dynamic_index_in_dim(split, place, axis + 1, False)
        return mine.reshape(shape[:axis] + (pairs * each,) + shape[axis + 1 :])

    def of_heads(array):
        mine = of_pairs(array, 0)
        split = mine.reshape((pairs, 2) + mine.shape[1:]).swapaxes(0, 1)
        return split.reshape(mine.shape)

    all_tokens = lax.all_gather(tokens[0], "ctx", axis=0, tiled=True)
    seed = lax.all_gather(cotangent[0], "ctx", axis=0, tiled=True)


    columns = w_in.T
    total_cols = core_cols + ENDS
    cut = halves(total_cols)[0]
    place_ref = place.reshape(1).astype(jnp.int32)
    smalls = [norm_gain[None], gate_gain[None], conv_b[None], conv_w]
    small_rows = [-(-v.shape[1] // SEG) for v in smalls]

    def split(whole):
        upper, _ = halves(whole.shape[0])
        parts = [whole[:, o * SEG : (o + 1) * SEG] for o in range(D // SEG)]
        middle = parts[len(parts) // 2]
        return parts[: len(parts) // 2] + [middle[:upper], middle[upper:]] + parts[len(parts) // 2 + 1 :]

    if ring:
        me = ring_place(lax.axis_index("fsdp"), n)
        members = ring_member(me + jnp.arange(n), n).astype(jnp.int32)
        padded = [jnp.pad(v, ((0, 0), (0, k * SEG - v.shape[1]))) for v, k in zip(smalls, small_rows)]
        small = jnp.concatenate([v.reshape(-1) for v in padded]).reshape(-1, SEG)
        block_x, block_z, block_o = run_pack(place_ref, columns, w_out, small, pairs)
        ring_x, ring_z, ring_o = Gather(block_x, n), Gather(block_z, n), Gather(block_o, n)
        next_hop([ring_x], ())
        dt_bias, a_log, d_skip = next_hop([ring_x], (dt_bias, a_log, d_skip))
        for _ in range(n // 2 - 4):
            next_hop([ring_x], ())
        next_hop([ring_x, ring_z], ())
        next_hop([ring_x], (), *arrivals(ring_z))
        parts_x = ring_x.parts()
        all_tokens, members_late, parts_late = next_hop(
            [ring_z, ring_o], (all_tokens, members, parts_x), *arrivals(ring_x)
        )
    else:
        members = jnp.arange(D // SEG, dtype=jnp.int32)
        block_x = jnp.concatenate(
            [
                of_pairs(columns[DI : 2 * DI], 0),
                columns[2 * DI : 2 * DI + 2 * STATE],
                of_heads(columns[DI + CONV :]),
                jnp.zeros((ENDS - heads, rows), BF16),
            ],
            axis=0,
        )
        whole_x = lax.all_gather(block_x, "fsdp", axis=1, tiled=True)
        norm_whole = lax.all_gather(norm_gain[None], "fsdp", axis=1, tiled=True)
        at = core_cols + SMALL
        whole_x = jnp.concatenate([whole_x[:at], norm_whole, whole_x[at + 1 :]], axis=0)
        parts_x, parts_z = split(whole_x), split(lax.all_gather(of_pairs(columns[:DI], 0), "fsdp", axis=1, tiled=True))
        w_o = of_pairs(lax.all_gather(w_out, "fsdp", axis=0, tiled=True), 0)
        parts_o = [w_o[o * PAIR : (o + 1) * PAIR] for o in range(pairs)]
        middle, upper = parts_o[pairs // 2], halves(PAIR)[0]
        parts_o = parts_o[: pairs // 2] + [middle[:upper], middle[upper:]] + parts_o[pairs // 2 + 1 :]

    if ring:
        kept = run_collect(members_late, parts_late)
        spans, at = [], 0
        for v, each in zip(smalls, small_rows):
            here = kept[:, at : at + v.shape[0] * each].reshape(n, v.shape[0], each * SEG)
            spans.append(here[:, :, : v.shape[1]].transpose(1, 0, 2).reshape(v.shape[0], -1))
            at += v.shape[0] * each
        norm_full, gate_full, bias_full, taps_full = spans
    else:
        norm_full, gate_full, bias_full, taps_full = (
            lax.all_gather(v, "fsdp", axis=1, tiled=True).astype(F32) for v in smalls
        )
    gate_full = of_pairs(gate_full, 1)
    taps_full = jnp.concatenate([taps_full, bias_full], axis=0)
    taps = jnp.concatenate([of_pairs(taps_full[:, :DI], 1), taps_full[:, DI:]], axis=1)
    taps = jnp.pad(taps, ((0, 8 - KW - 1), (0, 0)))

    dt_bias_own, a_log_own = of_heads(dt_bias), of_heads(a_log)
    skip_own = of_pairs(d_skip, 0)
    a_neg = -jnp.exp(a_log_own)
    heads_in = jnp.broadcast_to(jnp.concatenate([dt_bias_own, a_neg])[:, None], (2 * heads, 128))
    skip_row = jnp.repeat(skip_own, HEADDIM)[None, :]

    normed, proj_x = run_front(members, all_tokens, parts_x)
    if ring:
        proj_x = next_hop([ring_z, ring_o], proj_x, *arrivals(ring_z, ring_o))
    act, table, ssd, starts = run_mix_forward(proj_x, taps, heads_in, skip_row, pairs)
    normed_z = normed
    if ring:
        for _ in range(n // 2 - 3):
            next_hop([ring_z, ring_o], (), ssd, *arrivals(ring_z, ring_o))
        normed_z = next_hop([ring_o], normed, *arrivals(ring_z))
        parts_z, parts_o = ring_z.parts(), ring_o.parts()
    proj_z = run_project(normed_z, parts_z)

    w_o, scaled, sums = run_gate_sums(members, seed, parts_o, proj_z, ssd, gate_full)
    sums = ctx_sum(sums, m)
    mixed, dy, d_z, gate_cols = run_gate_back(sums, scaled, proj_z, ssd, act, gate_full)

    grads_o = tn(mixed, seed).astype(BF16)
    conv_grads, head_grads, top, before = [], [], blocks - 1, None
    d_z_late, mixed_late = d_z, mixed
    if ring:
        sum_o = Reduce(lambda o: lax.dynamic_slice_in_dim(grads_o, members[o] * PAIR, PAIR, 0), n)
        d_z_late, mixed_late = next_hop([sum_o], (d_z, mixed))
    grads_z = tn(d_z_late, normed).astype(BF16)
    branch = nn(mixed_late, w_o).astype(BF16)
    if ring:
        sum_z = Reduce(lambda o: grads_z[:, o * SEG : (o + 1) * SEG], n)
    for at in range(2):
        if ring:
            sum_o.join()
            if at > 0:
                sum_z.join()
                branch_own.middle()
                dy, before, branch_own.sent = next_hop(
                    [sum_o, sum_z], (dy, before, branch_own.sent)
                )
                branch_own.send_far()
            else:
                dy, branch = next_hop([sum_o, sum_z], (dy, branch))
                branch_own = CtxReduce(*by_core(branch.reshape(m, piece, D), m), m)
        span = blocks // 2
        d_x, conv_part, head_part, *before = run_mix_backward(
            span, top, act, proj_x, taps, heads_in, skip_row, table, starts, dy, before
        )
        before = (d_x, *before)
        conv_grads.append(conv_part)
        head_grads.append(head_part)
        top -= span
    normed_late = normed
    if ring:
        sum_o.join()
        sum_z.join()
        d_x, normed_late, branch_own.far = next_hop(
            [sum_o, sum_z], (d_x, normed, branch_own.far)
        )
    else:
        branch_own = CtxReduce(*by_core(branch.reshape(m, piece, D), m), m)
        branch_own.middle()
        branch_own.send_far()
    grads_x = tn(d_x, normed_late).astype(BF16)
    kept, given, d_gain = run_back_norm(
        members, place_ref, all_tokens, d_z, after(d_x, grads_x), parts_z, parts_x
    )
    small = run_gather_small(conv_grads, head_grads, gate_cols, d_gain)
    if ring:
        used = core_cols + TAIL
        sum_x = Reduce(
            lambda o: grads_x[:used, o * SEG : (o + 1) * SEG], n, run_cut(grads_x, used, n // 2)
        )
        part_o = sum_o.join().astype(BF16)
        sum_z.join()
        kept, given, small, part_o, branch_own.far = next_hop(
            [sum_x, sum_z], (kept, given, small, part_o, branch_own.far)
        )
    flip = 1
    steps = []
    while flip < n:
        steps.append(flip)
        flip *= 2

    def small_step(small):
        if steps:
            small = small + lax.ppermute(small, "fsdp", ctx_route(n, steps.pop()))
        return small

    d_own = CtxReduce(kept, given, m)
    d_own.middle()
    d_own.send_far()
    small = small_step(small)
    if ring:
        sum_x.join()
        part_z = sum_z.join().astype(BF16)
        d_own.far, small, part_o, part_z, branch_own.far = next_hop(
            [sum_x], (d_own.far, small, part_o, part_z, branch_own.far)
        )
        other_o = far_share(part_o, m)
    small = small_step(small)
    output = (tokens[0].astype(F32) + branch_own.total()).astype(BF16)[None]
    if ring:
        sum_x.join()
        small, other_o, part_z, d_own.far = next_hop(
            [sum_x], (small, other_o, part_z, d_own.far), output
        )
        shares_o, other_z = near_share(part_o, other_o, m), far_share(part_z, m)
        grad_w_out = run_assemble_o(place_ref, shares_o)
    small = small_step(small)
    own = tokens[0].astype(F32)
    inv = lax.rsqrt(jnp.mean(own * own, axis=-1, keepdims=True) + EPS)
    d_direct = d_own.total() * norm_full
    along = jnp.mean(d_direct * own, axis=-1, keepdims=True)
    grad_tokens = (cotangent[0].astype(F32) + d_direct * inv - own * (inv * inv * inv * along))[None]
    if ring:
        for at in range(n // 2 - 3):
            sum_x.join()
            small, part_z, other_z = next_hop(
                [sum_x], (small, part_z, other_z), grad_tokens, grad_w_out
            )
        shares_z = near_share(part_z, other_z, m)
        held = run_assemble_z(place_ref, shares_z, w_in.shape[1])
    while steps:
        small = small_step(small)
    smalls_of = ctx_share(small, m)
    if ring:
        part_x = sum_x.join().astype(BF16)
        part_a, part_b = part_x[:cut], part_x[cut:]
        part_a, part_b, smalls_of = barrier((part_a, part_b, smalls_of))
    by_place = jnp.zeros((m,) + small.shape, F32)
    for k in range(m):
        by_place = lax.dynamic_update_slice(by_place, smalls_of[k][None], (place ^ k, 0, 0))

    mine = lax.axis_index("fsdp")
    lines = [core_cols] * (KW + 1) + [width, width, D]
    found, at = [], 0
    for count in lines:
        found.append(by_place[:, at : at + count // SEG].reshape(m, 1, count))
        at += count // SEG
    conv_lines = jnp.concatenate(found[: KW + 1], axis=1)

    def interleaved(lines):
        return lines.reshape(m, -1, pairs, PAIR).transpose(1, 2, 0, 3).reshape(-1, DI)

    whole = jnp.concatenate(
        [interleaved(conv_lines[:, :, :width]), jnp.sum(conv_lines[:, :, width:], axis=0)], axis=1
    )
    each = conv_b.shape[0]
    grad_conv = lax.dynamic_slice_in_dim(whole, mine * each, each, 1)
    each = gate_gain.shape[0]
    grad_gate_gain = lax.dynamic_slice_in_dim(interleaved(found[KW + 1]), mine * each, each, 1)[0]
    grad_gain = lax.dynamic_slice_in_dim(jnp.sum(found[KW + 3], axis=0)[0], mine * rows, rows, 0)
    skips = jnp.sum(found[KW + 2].reshape(m, pairs, 2, HEADDIM), axis=3).reshape(m, 1, pairs, 2)
    of_steps = jnp.sum(by_place[:, by_place.shape[1] - 2 * heads :], axis=2)
    of_steps = of_steps.reshape(m, 2, 2, pairs).transpose(0, 1, 3, 2)
    per_head = jnp.concatenate([of_steps, skips], axis=1).transpose(1, 2, 0, 3).reshape(3, HEADS)
    grad_a_log = per_head[1] * -jnp.exp(a_log)
    if not ring:
        part_z = lax.psum_scatter(grads_z.astype(F32), "fsdp", scatter_dimension=1, tiled=True)
        part_x = lax.psum_scatter(grads_x.astype(F32), "fsdp", scatter_dimension=1, tiled=True)
        whole_o = jnp.zeros((pairs, m, PAIR, D), F32)
        whole_o = lax.dynamic_update_index_in_dim(
            whole_o, grads_o.astype(F32).reshape(pairs, PAIR, D), place, 1
        )
        grad_w_out = lax.psum_scatter(whole_o.reshape(DI, D), "fsdp", scatter_dimension=0, tiled=True)
        grad_w_out = lax.psum(grad_w_out, "ctx")
        held = run_assemble_z(place_ref, ctx_share(part_z.astype(BF16), m), w_in.shape[1])
        part_x = part_x.astype(BF16)
        part_a, part_b = part_x[:cut], part_x[cut : core_cols + TAIL]
    other_b, other_a = far_share(part_b, m), far_share(part_a, m)
    order = np.zeros((m, HEADS, TAIL), np.float32)
    for member in range(m):
        for h in range(heads):
            order[member, (h % pairs) * 2 * m + 2 * member + h // pairs, h] = 1.0
    shares_b = near_share(part_b, other_b, m)
    held = run_assemble_b(place_ref, jnp.asarray(order, BF16), held, shares_b, pairs - cut // PAIR)
    shares_a = near_share(part_a, other_a, m)
    grad_w_in = run_assemble_a(place_ref, held, shares_a)
    return (
        output,
        grad_tokens,
        grad_gain,
        grad_w_in.T,
        grad_conv[:KW],
        grad_conv[KW],
        per_head[0],
        grad_a_log,
        per_head[2],
        grad_gate_gain,
        grad_w_out,
    )


def solution(mesh):
    in_specs = (
        P("fsdp", "ctx", None),
        P("fsdp"),
        P("fsdp", None),
        P(None, "fsdp"),
        P("fsdp"),
        P(),
        P(),
        P(),
        P("fsdp"),
        P("fsdp", None),
        P("fsdp", "ctx", None),
    )
    out_specs = (
        P("fsdp", "ctx", None),
        P("fsdp", "ctx", None),
        P("fsdp"),
        P("fsdp", None),
        P(None, "fsdp"),
        P("fsdp"),
        P(),
        P(),
        P(),
        P("fsdp"),
        P("fsdp", None),
    )
    return jax.shard_map(body, mesh=mesh, in_specs=in_specs, out_specs=out_specs, check_vma=False)
```

```python
import jax
import jax.numpy as jnp
import numpy as np
from jax import lax
from jax.experimental import pallas as pl
from jax.experimental.pallas import tpu as pltpu
from jax.sharding import PartitionSpec as P

D = 2048
HEADS = 64
HEADDIM = 64
STATE = 128
KW = 4
GROUP = 256
DI = HEADS * HEADDIM
CONV = DI + 2 * STATE
PAIR = 2 * HEADDIM
EPS = 1e-05
SEG = 256
HALO = 8
SMALL = 32
TAIL = 32
ENDS = 64
VMEM_LIMIT = 56 * 1024 * 1024
F32 = jnp.float32
BF16 = jnp.bfloat16


def ring_place(index, n):
    return jnp.where(index % 2 == 0, index // 2, n - 1 - index // 2)


def ring_member(place, n):
    place = place % n
    return jnp.where(place < n // 2, 2 * place, 2 * (n - 1 - place) + 1)


def ring_routes(n):
    order = [2 * p if p < n // 2 else 2 * (n - 1 - p) + 1 for p in range(n)]
    forward = [(order[p], order[(p + 1) % n]) for p in range(n)]
    return forward, [(b, a) for a, b in forward]


def send(block, route):
    return lax.ppermute(block, "fsdp", route)


def after(value, *earlier):
    return lax.optimization_barrier((value, *earlier))[0]


def halves(rows):
    upper = -(-rows // 256) * 128 if rows >= 512 else rows // 2
    return upper, rows - upper


class Gather:
    def __init__(self, block, n):
        self.forward, self.backward = ring_routes(n)
        self.block, self.n = block, n
        self.latest = (block, block)
        self.ahead, self.behind = [], []

    def load(self):
        right, left = self.latest
        if len(self.ahead) == self.n // 2 - 1:
            upper, _ = halves(self.block.shape[0])
            return right[:upper], left[upper:]
        return right, left

    def fire(self, right, left):
        last = len(self.ahead) == self.n // 2 - 1
        self.latest = send(right, self.forward), send(left, self.backward)
        if not last:
            self.behind.insert(0, self.latest[0])
            self.ahead.append(self.latest[1])

    def parts(self):
        return [self.block] + self.ahead + list(self.latest) + self.behind


class Reduce:
    def __init__(self, chunk, n, pieces=None):
        self.forward, self.backward = ring_routes(n)
        self.chunk, self.n, self.step = chunk, n, n // 2
        if pieces is None:
            first = chunk(n // 2).astype(BF16)
            upper, _ = halves(first.shape[0])
            pieces = first[:upper], first[upper:]
        self.right, self.left = pieces
        self.upper = self.right.shape[0]

    def load(self):
        return self.right, self.left

    def fire(self, right, left):
        self.latest = send(right, self.forward), send(left, self.backward)
        self.step -= 1

    def join(self):
        right, left = (part.astype(F32) for part in self.latest)
        if self.step == 0:
            return self.chunk(0).astype(F32) + right + left
        own_right = self.chunk(self.step).astype(F32)
        own_left = self.chunk(self.n - self.step).astype(F32)
        cut = self.upper
        if self.step == self.n // 2 - 1:
            right = jnp.concatenate([own_right[:cut] + right, own_right[cut:]], axis=0)
            left = jnp.concatenate([own_left[:cut], own_left[cut:] + left], axis=0)
        else:
            right, left = own_right + right, own_left + left
        self.right, self.left = right.astype(BF16), left.astype(BF16)


def cut_in_two(grads_ref, right_ref, left_ref):
    upper = right_ref.shape[0]
    right_ref[...] = grads_ref[:upper]
    left_ref[...] = grads_ref[upper:]


def run_cut(grads, rows, block):
    shapes = [(half, SEG) for half in halves(rows)]
    return pl.pallas_call(
        cut_in_two,
        grid=(1,),
        in_specs=[pl.BlockSpec((rows, SEG), lambda i: (0, block))],
        out_specs=[pl.BlockSpec(shape, lambda i: (0, 0)) for shape in shapes],
        out_shape=[jax.ShapeDtypeStruct(shape, BF16) for shape in shapes],
        cost_estimate=busy(1, 1),
        name="cut_in_two",
    )(grads)


def barrier(value, *earlier):
    return lax.optimization_barrier((value, earlier))[0]


def next_hop(rings, inputs, *earlier):
    loads, inputs = barrier(([ring.load() for ring in rings], inputs), *earlier)
    for ring, load in zip(rings, loads):
        ring.fire(*load)
    return inputs


def arrivals(*rings):
    return sum((ring.latest for ring in rings), ())


def ctx_route(m, flip):
    return [(i, i ^ flip) for i in range(m)]


def far_share(block, m):
    return lax.ppermute(block, "ctx", ctx_route(m, 2))


def near_share(block, other, m):
    near = lax.ppermute(block, "ctx", ctx_route(m, 1))
    far = lax.ppermute(other, "ctx", ctx_route(m, 1))
    return [block, near, other, far]


def ctx_share(block, m):
    return near_share(block, far_share(block, m), m)


def gather_small(conv0, conv1, heads0, heads1, gate_ref, gain_ref, out_ref):
    out_ref[...] = jnp.zeros_like(out_ref)
    lines = [(conv0, k, conv1) for k in range(KW + 1)]
    lines += [(gate_ref, 0, None), (gate_ref, 1, None), (gain_ref, 0, None)]
    at = 0
    for ref, row, other in lines:
        for start in range(0, ref.shape[1], SEG):
            line = ref[row : row + 1, start : start + SEG]
            if other is not None:
                line = line + other[row : row + 1, start : start + SEG]
            out_ref[at : at + 1, :] = line
            at += 1
    at = out_ref.shape[0] - heads0.shape[0]
    out_ref[at:, :] = heads0[...] + heads1[...]


def run_gather_small(conv_grads, head_grads, gate_cols, d_gain):
    arrays = [*conv_grads, *head_grads, gate_cols, d_gain]
    lines = (KW + 1) * conv_grads[0].shape[1] + 2 * gate_cols.shape[1] + d_gain.shape[1]
    rows = -(-lines // SEG // 8) * 8 + head_grads[0].shape[0]
    return pl.pallas_call(
        gather_small,
        grid=(1,),
        in_specs=[pl.BlockSpec(v.shape, lambda i: (0, 0)) for v in arrays],
        out_specs=pl.BlockSpec((rows, SEG), lambda i: (0, 0)),
        out_shape=jax.ShapeDtypeStruct((rows, SEG), F32),
        cost_estimate=busy(1, 1),
        name="gather_small",
    )(*arrays)


class CtxReduce:
    def __init__(self, kept, given, m):
        self.m, place = m, lax.axis_index("ctx")
        self.core, self.across = place % 2, place // 2
        self.kept = kept
        self.near = lax.ppermute(given, "ctx", ctx_route(m, 1))

    def middle(self):
        self.both = self.kept.astype(F32) + self.near.astype(F32)
        self.sent = lax.dynamic_index_in_dim(self.both, 1 - self.across, 0, False).astype(BF16)

    def send_far(self):
        self.far = lax.ppermute(self.sent, "ctx", ctx_route(self.m, 2))

    def total(self):
        return lax.dynamic_index_in_dim(self.both, self.across, 0, False) + self.far.astype(F32)


def by_core(share, m):
    core = lax.axis_index("ctx") % 2
    split = share.reshape((m // 2, 2) + share.shape[1:])
    return (
        lax.dynamic_index_in_dim(split, core, 1, False),
        lax.dynamic_index_in_dim(split, 1 - core, 1, False),
    )


def ctx_sum(values, m):
    near, across, far = (lax.ppermute(values, "ctx", ctx_route(m, flip)) for flip in (1, 2, 3))
    return (values + near) + (across + far)


def nt(a, b):
    return lax.dot_general(a, b, (((1,), (1,)), ((), ())), preferred_element_type=F32)


def nn(a, b):
    return lax.dot_general(a, b, (((1,), (0,)), ((), ())), preferred_element_type=F32)


def tn(a, b):
    return lax.dot_general(a, b, (((0,), (0,)), ((), ())), preferred_element_type=F32)


def lanes(shape):
    return lax.broadcasted_iota(jnp.int32, shape, len(shape) - 1)


def busy(us, megabytes):
    return pl.CostEstimate(
        flops=int(us * 1e9), transcendentals=0, bytes_accessed=int(megabytes * 1e6)
    )


def softplus(v):
    return jnp.maximum(v, 0.0) + jnp.log1p(jnp.exp(-jnp.abs(v)))


def sigmoid(v):
    return 1.0 / (1.0 + jnp.exp(-v))


def ones_where(keep):
    row = lax.broadcasted_iota(jnp.int32, (GROUP, GROUP), 0)
    col = lax.broadcasted_iota(jnp.int32, (GROUP, GROUP), 1)
    return keep(row, col)


def exact(a, b):
    return lax.dot_general(
        a, b, (((1,), (0,)), ((), ())), preferred_element_type=F32, precision=lax.Precision.HIGHEST
    )


def tiles(width):
    return [slice(at, at + PAIR) for at in range(0, width, PAIR)]


def conv_tile(extended, taps_ref, cols):
    total = taps_ref[KW : KW + 1, cols]
    for k in range(KW):
        at = HALO - KW + 1 + k
        total = total + taps_ref[k : k + 1, cols] * extended[at : at + GROUP]
    return total


def by_segments(weights):
    n = D // SEG
    places = list(range(n // 2)) + [n // 2] * 2 + list(range(n // 2 + 1, n))
    at = [0] * len(places)
    at[n // 2 + 1] = weights[n // 2].shape[0]
    return list(zip(places, at, weights))


def project_into(out_ref, normed_ref, weights, total):
    whole = None
    for o, at, w in by_segments(weights):
        part = nt(normed_ref[:, o * SEG : (o + 1) * SEG], w[...])
        if o == D // SEG // 2:
            total[:, at : at + w.shape[0]] = part
        else:
            whole = part if whole is None else whole + part
    out_ref[...] = (whole + total[...]).astype(BF16)


def pack(
    place_ref, columns_ref, out_ref, small_ref, x_ref, z_ref, o_ref, steps, rows, sems,
):
    place = place_ref[0]
    pairs, m = z_ref.shape[0] // PAIR, out_ref.shape[0] // PAIR
    core = pairs * PAIR + 2 * STATE
    copies = [
        (columns_ref.at[pl.ds(DI + CONV, HEADS)], steps),
        (columns_ref.at[pl.ds(2 * DI, 2 * STATE)], x_ref.at[pl.ds(pairs * PAIR, 2 * STATE)]),
        (out_ref.at[pl.ds(pl.multiple_of(place * PAIR, PAIR), PAIR)], o_ref),
    ]
    for g in range(pairs):
        here = pl.ds(g * PAIR, PAIR)
        for start, ref in ((DI, x_ref), (0, z_ref)):
            at = pl.multiple_of(start + (g * m + place) * PAIR, PAIR)
            copies.append((columns_ref.at[pl.ds(at, PAIR)], ref.at[here]))
    copies = [pltpu.make_async_copy(*pair, sems.at[k]) for k, pair in enumerate(copies)]
    for copy in copies:
        copy.start()
    rows[...] = jnp.zeros_like(rows)
    rows[SMALL : SMALL + small_ref.shape[0], :] = small_ref[...].astype(F32)
    copies[0].wait()
    want = lax.broadcasted_iota(jnp.int32, (2 * pairs, HEADS), 0)
    have = lax.broadcasted_iota(jnp.int32, (2 * pairs, HEADS), 1)
    head = (want % pairs) * 2 * m + 2 * place + want // pairs
    rows[: 2 * pairs, :] = nn((have == head).astype(BF16), steps[...])
    x_ref[core : core + ENDS, :] = rows[...].astype(BF16)
    for copy in copies[1:]:
        copy.wait()


def run_pack(place, columns, w_out, small, pairs):
    rows = columns.shape[1]
    core = pairs * PAIR + 2 * STATE
    anywhere = pl.BlockSpec(memory_space=pl.ANY)
    shapes = [(core + ENDS, rows), (pairs * PAIR, rows), (PAIR, D)]
    return pl.pallas_call(
        pack,
        grid_spec=pltpu.PrefetchScalarGridSpec(
            num_scalar_prefetch=1,
            grid=(1,),
            in_specs=[anywhere, anywhere, pl.BlockSpec(small.shape, lambda i, t: (0, 0))],
            out_specs=[pl.BlockSpec(shape, lambda i, t: (0, 0)) for shape in shapes],
            scratch_shapes=[
                pltpu.VMEM((HEADS, rows), BF16),
                pltpu.VMEM((ENDS, rows), F32),
                pltpu.SemaphoreType.DMA((2 * pairs + 3,)),
            ],
        ),
        out_shape=[jax.ShapeDtypeStruct(shape, BF16) for shape in shapes],
        compiler_params=pltpu.CompilerParams(vmem_limit_bytes=VMEM_LIMIT),
        name="pack",
    )(place, columns, w_out, small)


def collect(members_ref, *refs):
    out_ref = refs[-1]
    for o, ref in enumerate(refs[:-1]):
        out_ref[members_ref[o]] = ref[...].astype(F32)


def run_collect(members, parts):
    n = len(parts) - 1
    lasts = parts[: n // 2] + parts[n // 2 + 1 :]
    at = lambda part: (part.shape[0] - ENDS + SMALL) // 32
    return pl.pallas_call(
        collect,
        grid_spec=pltpu.PrefetchScalarGridSpec(
            num_scalar_prefetch=1,
            grid=(1,),
            in_specs=[pl.BlockSpec((32, SEG), lambda i, t, k=at(p): (k, 0)) for p in lasts],
            out_specs=pl.BlockSpec((n, 32, SEG), lambda i, t: (0, 0, 0)),
        ),
        out_shape=jax.ShapeDtypeStruct((n, 32, SEG), F32),
        compiler_params=pltpu.CompilerParams(vmem_limit_bytes=VMEM_LIMIT),
        cost_estimate=busy(1, 1),
        name="collect",
    )(members, *lasts)


def front(members_ref, tokens_ref, *refs):
    weights, (normed_ref, proj_ref, total) = refs[:-3], refs[-3:]
    tokens = tokens_ref[...].astype(F32)
    inv = lax.rsqrt(jnp.mean(tokens * tokens, axis=-1, keepdims=True) + EPS)
    for o in range(D // SEG):
        at = pl.multiple_of(members_ref[o] * SEG, SEG)
        cols = slice(o * SEG, (o + 1) * SEG)
        last = weights[o if o < D // SEG // 2 else o + 1]
        row = last.shape[0] - ENDS + SMALL
        gain = last[row : row + 16, :].astype(F32)[0:1]
        part = tokens_ref[:, pl.ds(at, SEG)].astype(F32) * inv * gain
        normed_ref[:, cols] = part.astype(BF16)
    project_into(proj_ref, normed_ref, weights, total)


def resident(array, grid_args=1):
    zeros = (0,) * array.ndim
    maps = {1: lambda i: zeros, 2: lambda i, t: zeros, 3: lambda i, t, p: zeros}
    return pl.BlockSpec(array.shape, maps[grid_args], pipeline_mode=pl.Buffered(1))


def run_front(members, tokens, weights):
    length, cols = tokens.shape[0], weights[0].shape[0]
    return pl.pallas_call(
        front,
        grid_spec=pltpu.PrefetchScalarGridSpec(
            num_scalar_prefetch=1,
            grid=(length // GROUP,),
            in_specs=[
                pl.BlockSpec((GROUP, D), lambda i, t: (i, 0)),
            ]
            + [resident(w, 2) for w in weights],
            out_specs=[
                pl.BlockSpec((GROUP, D), lambda i, t: (i, 0)),
                pl.BlockSpec((GROUP, cols), lambda i, t: (i, 0)),
            ],
            scratch_shapes=[pltpu.VMEM((GROUP, cols), F32)],
        ),
        out_shape=[
            jax.ShapeDtypeStruct((length, D), BF16),
            jax.ShapeDtypeStruct((length, cols), BF16),
        ],
        compiler_params=pltpu.CompilerParams(vmem_limit_bytes=VMEM_LIMIT),
        cost_estimate=busy(12, 18),
        name="front",
    )(members, tokens, *weights)


def project(normed_ref, *refs):
    project_into(refs[-2], normed_ref, refs[:-2], refs[-1])


def run_project(normed, weights):
    length, cols = normed.shape[0], weights[0].shape[0]
    return pl.pallas_call(
        project,
        grid=(length // GROUP,),
        in_specs=[pl.BlockSpec((GROUP, D), lambda i: (i, 0))] + [resident(w) for w in weights],
        out_specs=pl.BlockSpec((GROUP, cols), lambda i: (i, 0)),
        out_shape=jax.ShapeDtypeStruct((length, cols), BF16),
        scratch_shapes=[pltpu.VMEM((GROUP, cols), F32)],
        compiler_params=pltpu.CompilerParams(vmem_limit_bytes=VMEM_LIMIT),
        cost_estimate=busy(8, 10),
        name="project",
    )(normed, *weights)


def spread_rows(ref, index, rows):
    count = rows.shape[0]
    ref[pl.ds(index, count), :] = rows[:, :128]
    ref[pl.ds(ref.shape[0] // 2 + index, count), :] = rows[:, 128:]


def all_rows(stack):
    half = stack.shape[0] // 2
    return jnp.concatenate([stack[:half], stack[half:]], axis=1)


def pair_rows(ref, g, pairs):
    half = 8 * pairs
    return jnp.concatenate(
        [ref[pl.ds(g, 8, stride=pairs), :], ref[pl.ds(half + g, 8, stride=pairs), :]], axis=1
    )


def high_low(v):
    high = v.astype(BF16)
    return high, (v - high.astype(F32)).astype(BF16)


def tri_units(back):
    units = []
    for r in range(GROUP // 64):
        for t in range(GROUP // 128):
            if (t >= r // 2) if back else (t <= r // 2):
                units.append((slice(64 * r, 64 * r + 64), slice(128 * t, 128 * t + 128), t == r // 2))
    return units


def diagonal(keep):
    row = lax.broadcasted_iota(jnp.int32, (128, 128), 0)
    col = lax.broadcasted_iota(jnp.int32, (128, 128), 1)
    return jnp.where(keep(row, col), 0.0, -1e30)


def mix_forward(
    proj_ref, taps_ref, heads_ref, skip_ref, act_ref, table_ref, y_ref, start_ref,
    state, halo, gram, bias, scores,
):
    pairs = state.shape[0]
    heads, width = 2 * pairs, pairs * PAIR
    core = width + 2 * STATE

    @pl.when(pl.program_id(0) == 0)
    def _():
        state[...] = jnp.zeros_like(state)
        halo[...] = jnp.zeros_like(halo)
        scores[...] = jnp.zeros_like(scores)
        bias[...] = diagonal(lambda row, col: row >= col)

    def activate(cols):
        current = proj_ref[:, cols].astype(F32)
        conv = conv_tile(jnp.concatenate([halo[:, cols], current], axis=0), taps_ref, cols)
        halo[:, cols] = current[GROUP - HALO :]
        act = (conv * sigmoid(conv)).astype(BF16)
        act_ref[:, cols] = act
        return act

    bs = activate(slice(width, width + STATE))
    cs = activate(slice(width + STATE, core))
    raw = proj_ref[:, core : core + ENDS].astype(F32).T[:heads]
    dt = softplus(raw + heads_ref[:heads, 0:1])
    upto = ones_where(lambda row, col: row <= col).astype(F32)
    cum = exact(dt * heads_ref[heads:, 0:1], upto)
    last = cum[:, GROUP - 1 :]
    table = jnp.concatenate([cum, dt, jnp.exp(last - cum) * dt, jnp.exp(cum)], axis=0)
    spread_rows(table_ref.at[0], 0, table)
    gram[...] = nt(cs, bs)
    bs_t = bs.astype(F32).T

    def one(g, unused):
        cols = pl.ds(pl.multiple_of(g * PAIR, PAIR), PAIR)
        rows = pair_rows(table_ref.at[0], g, pairs)
        turned = rows.T
        x = activate(cols)
        first = lanes(x.shape) < HEADDIM
        start = state[g]
        start_ref[0, g] = start
        inner = nn(cs, start.astype(BF16))
        parts, locals_ = [], []
        for e in range(2):
            for at, to, on in tri_units(False):
                differ = turned[at, e : e + 1] - rows[e : e + 1, to]
                if on:
                    differ = differ + bias[at.start % 128 : at.start % 128 + 64, :]
                decay = jnp.exp(differ)
                scores[e, at, to] = (gram[at, to] * decay * rows[2 + e : 3 + e, to]).astype(BF16)
            parts.append(nn(scores[e], x))
            locals_.append(nn((bs_t * rows[4 + e : 5 + e, :]).astype(BF16), x))
        grow = jnp.where(first, turned[:, 6:7], turned[:, 7:8])
        y_ref[:, cols] = (
            jnp.where(first, parts[0], parts[1]) + grow * inner + skip_ref[:, cols] * x.astype(F32)
        )
        shrink = jnp.where(first[:1], rows[6:7, GROUP - 1 :], rows[7:8, GROUP - 1 :])
        state[g] = shrink * start + jnp.where(first[:STATE], locals_[0], locals_[1])
        return unused

    lax.fori_loop(0, pairs, one, 0, unroll=2)


def run_mix_forward(proj, taps, heads_in, skip, pairs):
    length = proj.shape[0]
    blocks, width = length // GROUP, pairs * PAIR
    core = width + 2 * STATE
    whole = lambda i: (0, 0)
    return pl.pallas_call(
        mix_forward,
        grid=(blocks,),
        in_specs=[
            pl.BlockSpec((GROUP, proj.shape[1]), lambda i: (i, 0)),
            pl.BlockSpec(taps.shape, whole),
            pl.BlockSpec(heads_in.shape, whole),
            pl.BlockSpec(skip.shape, whole),
        ],
        out_specs=[
            pl.BlockSpec((GROUP, core), lambda i: (i, 0)),
            pl.BlockSpec((1, 16 * pairs, 128), lambda i: (i, 0, 0)),
            pl.BlockSpec((GROUP, width), lambda i: (i, 0)),
            pl.BlockSpec((1, pairs, STATE, PAIR), lambda i: (i, 0, 0, 0)),
        ],
        out_shape=[
            jax.ShapeDtypeStruct((length, core), BF16),
            jax.ShapeDtypeStruct((blocks, 16 * pairs, 128), F32),
            jax.ShapeDtypeStruct((length, width), F32),
            jax.ShapeDtypeStruct((blocks, pairs, STATE, PAIR), F32),
        ],
        scratch_shapes=[
            pltpu.VMEM((pairs, STATE, PAIR), F32),
            pltpu.VMEM((HALO, core), F32),
            pltpu.VMEM((GROUP, GROUP), F32),
            pltpu.VMEM((128, 128), F32),
            pltpu.VMEM((2, GROUP, GROUP), BF16),
        ],
        compiler_params=pltpu.CompilerParams(vmem_limit_bytes=VMEM_LIMIT),
        cost_estimate=busy(18, 15),
        name="mix_forward",
    )(proj, taps, heads_in, skip)


def mix_backward(
    top, follows, act_ref, proj_ref, prev_ref, taps_ref, heads_ref, skip_ref, table_ref, start_ref, dy_ref,
    carry_in, halo_in, held_ref, dx_ref, grads_ref, dheads_ref, carried, halo,
    gram, dgram, bias, d_scores, scores, db, dc, found, ends,
):
    pairs = carried.shape[0]
    heads, width = 2 * pairs, pairs * PAIR
    core = width + 2 * STATE
    step = pl.program_id(0)

    @pl.when(step == 0)
    def _():
        carried[...] = carry_in[...] if follows else jnp.zeros_like(carried)
        halo[...] = halo_in[...] if follows else jnp.zeros_like(halo)
        grads_ref[...] = jnp.zeros_like(grads_ref)
        dheads_ref[...] = jnp.zeros_like(dheads_ref)
        scores[...] = jnp.zeros_like(scores)
        bias[...] = diagonal(lambda row, col: row <= col)

    has_prev = jnp.where(top - step > 0, 1.0, 0.0)
    bs, cs = act_ref[:, width : width + STATE], act_ref[:, width + STATE : core]
    bs_float = bs.astype(F32)
    cs_t = cs.astype(F32).T.astype(BF16)
    gram[...] = nt(bs, cs)
    for ref in (dgram, db, dc):
        ref[...] = jnp.zeros_like(ref)

    def conv_back(d_act, cols):
        before = prev_ref[:, cols].astype(F32)[prev_ref.shape[0] - HALO :] * has_prev
        extended = jnp.concatenate([before, proj_ref[:, cols].astype(F32)], axis=0)
        conv = conv_tile(extended, taps_ref, cols)
        sig = sigmoid(conv)
        d_conv = d_act * (sig * (1.0 + conv * (1.0 - sig)))
        onward = jnp.concatenate([d_conv, halo[:, cols]], axis=0)
        d_in = taps_ref[KW - 1 : KW, cols] * d_conv
        for k in range(KW - 1):
            at = KW - 1 - k
            d_in = d_in + taps_ref[k : k + 1, cols] * onward[at : at + GROUP]
        dx_ref[:, cols] = d_in.astype(BF16)
        sums = []
        for k in range(KW):
            at = HALO - KW + 1 + k
            sums.append(jnp.sum(d_conv * extended[at : at + GROUP], axis=0, keepdims=True))
        sums.append(jnp.sum(d_conv, axis=0, keepdims=True))
        sums.append(jnp.zeros((8 - KW - 1, sums[0].shape[1]), F32))
        grads_ref[:, cols] += jnp.concatenate(sums, axis=0)
        halo[:, cols] = d_conv[:HALO]

    def one(g, unused):
        cols = pl.ds(pl.multiple_of(g * PAIR, PAIR), PAIR)
        rows = pair_rows(table_ref.at[0], g, pairs)
        turned = rows.T
        x, dy = act_ref[:, cols], dy_ref[:, cols]
        first = lanes(x.shape) < HEADDIM
        dy_float = dy.astype(F32)
        start, grad = start_ref[0, g], carried[g]
        start_low, grad_low = start.astype(BF16), grad.astype(BF16)
        inner = nn(cs, start_low)
        grow = jnp.where(first, turned[:, 6:7], turned[:, 7:8])
        d_inner = (dy_float * grow).astype(BF16)
        dc[...] += nt(d_inner, start_low)
        touched = dy_float * inner
        held = jnp.sum(grad * start, axis=0, keepdims=True)
        zero = jnp.zeros_like(x)
        reach = nn(bs, grad_low)
        sent = x.astype(F32) * jnp.where(first, turned[:, 4:5], turned[:, 5:6])
        for half in high_low(sent):
            db[...] += nt(half, grad_low)
        parts, sums_j, linked = [], [], []
        for e in range(2):
            own = first if e == 0 else jnp.logical_not(first)
            d_scores[e] = nt(jnp.where(own, x, zero), dy)
            linked_i, linked_j = {}, {}
            for at, to, on in tri_units(True):
                dt_col = turned[at, 2 + e : 3 + e]
                differ = rows[e : e + 1, to] - turned[at, e : e + 1]
                if on:
                    differ = differ + bias[at.start % 128 : at.start % 128 + 64, :]
                decay = jnp.exp(differ)
                grown = gram[at, to] * decay
                d_score = d_scores[e, at, to]
                score = grown * dt_col
                scores[e, at, to] = score.astype(BF16)
                dgram[at, to] += d_score * decay * dt_col
                along_i = d_score * grown
                along_j = jnp.sum(d_score * score, axis=0, keepdims=True)
                key_i, key_j = at.start, to.start
                linked_i[key_i] = along_i if key_i not in linked_i else linked_i[key_i] + along_i
                linked_j[key_j] = along_j if key_j not in linked_j else linked_j[key_j] + along_j
            sums_j.append(jnp.concatenate([linked_j[k] for k in sorted(linked_j)], axis=1))
            linked.append(jnp.concatenate([linked_i[k] for k in sorted(linked_i)], axis=0))
            tail_col = turned[:, 4 + e : 5 + e]
            parts.append(nn(scores[e], dy) + nn((bs_float * tail_col).astype(BF16), grad_low))
        pick = lax.broadcasted_iota(jnp.int32, (8, 2 * PAIR), 0)
        lane = lanes((8, 2 * PAIR))
        by_head = (pick == lane // HEADDIM).astype(BF16)
        by_pair = (pick == 4 + lane // PAIR).astype(BF16)
        kept = jnp.zeros((8, GROUP), F32)
        for sums, select in (
            ((x.astype(F32) * reach, touched), by_head),
            (linked, by_pair),
        ):
            for half in high_low(jnp.concatenate(sums, axis=1)):
                kept = kept + nt(select, half)
        kept = jnp.concatenate([kept[:6]] + sums_j, axis=0)
        found[pl.ds(g, 8, stride=pairs), :] = kept[:, :128]
        found[pl.ds(8 * pairs + g, 8, stride=pairs), :] = kept[:, 128:]
        ends[pl.ds(g, 2, stride=pairs), :] = jnp.concatenate(
            [jnp.where(first[:1], held, 0.0), jnp.where(first[:1], 0.0, held)], axis=0
        )
        conv_back(jnp.where(first, parts[0], parts[1]) + skip_ref[:, cols] * dy_float, cols)
        shrink = jnp.where(first[:1], rows[6:7, GROUP - 1 :], rows[7:8, GROUP - 1 :])
        carried[g] = shrink * grad + nn(cs_t, d_inner)
        return unused

    lax.fori_loop(0, pairs, one, 0, unroll=2)
    low = dgram[...].astype(BF16)
    conv_back(db[...] + nn(low, cs), slice(width, width + STATE))
    conv_back(dc[...] + tn(low, bs), slice(width + STATE, core))

    rows, sums = all_rows(table_ref[0]), all_rows(found[...])
    d_tail, touched, sum_i, sum_j = (sums[k * heads : (k + 1) * heads] for k in range(4))
    cum, dt, tail, growth = (rows[k * heads : (k + 1) * heads] for k in range(4))
    a_neg = heads_ref[heads:, 0:1]
    tail_log = d_tail * tail
    d_last = jnp.sum(tail_log, axis=1, keepdims=True)
    d_last = d_last + jnp.sum(ends[...], axis=1, keepdims=True) * growth[:, GROUP - 1 :]
    d_cum = touched * growth - tail_log + sum_j - dt * sum_i
    d_cum = d_cum + jnp.where(lanes(d_cum.shape) == GROUP - 1, d_last, 0.0)
    d_rate = exact(d_cum, ones_where(lambda row, col: row >= col).astype(F32))
    raw = proj_ref[:, core : core + ENDS].astype(F32).T[:heads]
    d_step = d_tail * jnp.exp(cum[:, GROUP - 1 :] - cum) + sum_i
    d_dt = (d_step + d_rate * a_neg) * sigmoid(raw + heads_ref[:heads, 0:1])
    dheads_ref[:heads, :] += d_dt
    dheads_ref[heads:, :] += d_rate * dt
    filled = jnp.concatenate([d_dt, jnp.zeros((ENDS - heads, GROUP), F32)], axis=0)
    dx_ref[:, core : core + ENDS] = filled.T.astype(BF16)


def run_mix_backward(span, top, act, proj, taps, heads_in, skip, table, starts, dy, before):
    pairs = starts.shape[1]
    follows = before is not None
    held, carry, halo = before if follows else (dy, skip[:, :128], skip[:, :128])
    heads, width = 2 * pairs, pairs * PAIR
    core = width + 2 * STATE
    whole = lambda i: (0, 0)
    block = lambda i: (top - i, 0)
    above = GROUP // 16
    return pl.pallas_call(
        lambda *refs: mix_backward(top, follows, *refs),
        grid=(span,),
        in_specs=[
            pl.BlockSpec((GROUP, core), block),
            pl.BlockSpec((GROUP, proj.shape[1]), block),
            pl.BlockSpec((16, proj.shape[1]), lambda i: (jnp.maximum((top - i) * above - 1, 0), 0)),
            pl.BlockSpec(taps.shape, whole),
            pl.BlockSpec(heads_in.shape, whole),
            pl.BlockSpec(skip.shape, whole),
            pl.BlockSpec((1, 16 * pairs, 128), lambda i: (top - i, 0, 0)),
            pl.BlockSpec((1, pairs, STATE, PAIR), lambda i: (top - i, 0, 0, 0)),
            pl.BlockSpec((GROUP, width), block),
            pl.BlockSpec(carry.shape, lambda i: (0,) * carry.ndim),
            pl.BlockSpec(halo.shape, whole),
            pl.BlockSpec(memory_space=pl.ANY),
        ],
        out_specs=[
            pl.BlockSpec((GROUP, proj.shape[1]), block),
            pl.BlockSpec((8, core), whole),
            pl.BlockSpec((2 * heads, GROUP), whole),
            pl.BlockSpec((pairs, STATE, PAIR), lambda i: (0, 0, 0)),
            pl.BlockSpec((HALO, core), whole),
        ],
        out_shape=[
            jax.ShapeDtypeStruct(proj.shape, BF16),
            jax.ShapeDtypeStruct((8, core), F32),
            jax.ShapeDtypeStruct((2 * heads, GROUP), F32),
            jax.ShapeDtypeStruct((pairs, STATE, PAIR), F32),
            jax.ShapeDtypeStruct((HALO, core), F32),
        ],
        scratch_shapes=[
            pltpu.VMEM((GROUP, GROUP), F32),
            pltpu.VMEM((GROUP, GROUP), F32),
            pltpu.VMEM((128, 128), F32),
            pltpu.VMEM((2, GROUP, GROUP), F32),
            pltpu.VMEM((2, GROUP, GROUP), BF16),
            pltpu.VMEM((GROUP, STATE), F32),
            pltpu.VMEM((GROUP, STATE), F32),
            pltpu.VMEM((8 * heads, 128), F32),
            pltpu.VMEM((heads, PAIR), F32),
        ],
        compiler_params=pltpu.CompilerParams(vmem_limit_bytes=VMEM_LIMIT),
        input_output_aliases={11: 0} if follows else {},
        cost_estimate=busy(12 * span, 5 * span),
        name="mix_backward",
    )(act, proj, proj, taps, heads_in, skip, table, starts, dy, carry, halo, held)


def gate_sums(members_ref, seed_ref, z_ref, y_ref, gain_ref, *refs):
    parts, (w_ref, scaled_ref, sums_ref, squares, along) = refs[:-5], refs[-5:]
    step, n = pl.program_id(0), len(refs[:-5]) - 1

    @pl.when(step == 0)
    def _():
        squares[...] = jnp.zeros_like(squares)
        along[...] = jnp.zeros_like(along)
        places = list(range(n // 2)) + [n // 2] * 2 + list(range(n // 2 + 1, n))
        for k, (o, part) in enumerate(zip(places, parts)):
            at = pl.multiple_of(members_ref[o] * PAIR, PAIR)
            if k == n // 2 + 1:
                at = at + PAIR - part.shape[0]
            w_ref[pl.ds(at, part.shape[0]), :] = part[...]

    tile = z_ref.shape[1]
    scaled = nt(seed_ref[...], w_ref[pl.ds(pl.multiple_of(step * tile, tile), tile), :])
    scaled_ref[...] = scaled
    z = z_ref[...].astype(F32)
    gated = y_ref[...] * (z * sigmoid(z))
    square = gated * gated
    lean = scaled * gain_ref[...] * gated
    for cols in tiles(square.shape[1]):
        squares[...] += square[:, cols]
        along[...] += lean[:, cols]

    @pl.when(step == pl.num_programs(0) - 1)
    def _():
        spot = lanes(squares.shape)
        both = jnp.where(
            spot == 0,
            jnp.sum(squares[...], axis=1, keepdims=True),
            jnp.where(spot == 1, jnp.sum(along[...], axis=1, keepdims=True), 0.0),
        )
        sums_ref[...] = both.T[:8]


def run_gate_sums(members, seed, parts, z, y, gain):
    length, width = y.shape
    tile = 2 * PAIR
    col = pl.BlockSpec((length, tile), lambda i, t: (0, i))
    return pl.pallas_call(
        gate_sums,
        grid_spec=pltpu.PrefetchScalarGridSpec(
            num_scalar_prefetch=1,
            grid=(width // tile,),
            in_specs=[resident(seed, 2), col, col, pl.BlockSpec((1, tile), lambda i, t: (0, i))]
            + [resident(part, 2) for part in parts],
            out_specs=[
                pl.BlockSpec((width, D), lambda i, t: (0, 0)),
                col,
                pl.BlockSpec((8, length), lambda i, t: (0, 0)),
            ],
            scratch_shapes=[pltpu.VMEM((length, PAIR), F32)] * 2,
        ),
        out_shape=[
            jax.ShapeDtypeStruct((width, D), BF16),
            jax.ShapeDtypeStruct(y.shape, F32),
            jax.ShapeDtypeStruct((8, length), F32),
        ],
        compiler_params=pltpu.CompilerParams(vmem_limit_bytes=VMEM_LIMIT),
        cost_estimate=busy(11, 20),
        name="gate_sums",
    )(members, seed, z, y, gain, *parts)


def gate_back(sums_ref, scaled_ref, z_ref, y_ref, x_ref, gain_ref, mixed_ref, dy_ref, dz_ref, cols_ref, turned):
    @pl.when(pl.program_id(0) == 0)
    def _():
        inv = lax.rsqrt(sums_ref[0:1, :] / DI + EPS)
        slope = inv * inv * inv * (sums_ref[1:2, :] / DI)
        rest = jnp.zeros((PAIR - 2, sums_ref.shape[1]), F32)
        both = jnp.concatenate([inv, slope, rest], axis=0).T
        turned[0] = jnp.broadcast_to(both[:, 0:1], turned.shape[1:])
        turned[1] = jnp.broadcast_to(both[:, 1:2], turned.shape[1:])

    inv, slope = turned[0], turned[1]
    z, y, scaled, gain = z_ref[...].astype(F32), y_ref[...], scaled_ref[...], gain_ref[...]
    sig = sigmoid(z)
    silu = z * sig
    gated = y * silu
    normal = gated * inv
    mixed_ref[...] = (normal * gain).astype(BF16)
    d_gated = scaled * gain * inv - gated * slope
    dy = (d_gated * silu).astype(BF16)
    dy_ref[...] = dy
    dz_ref[...] = (d_gated * y * (sig * (1.0 + z * (1.0 - sig)))).astype(BF16)
    cols_ref[0:1, :] = jnp.sum(scaled * normal, axis=0, keepdims=True)
    cols_ref[1:2, :] = jnp.sum(dy.astype(F32) * x_ref[...].astype(F32), axis=0, keepdims=True)
    cols_ref[2:, :] = jnp.zeros_like(cols_ref[2:, :])


def run_gate_back(sums, scaled, z, y, x, gain):
    length, width = y.shape
    tile = 2 * PAIR
    col = pl.BlockSpec((length, tile), lambda i: (0, i))
    low = jax.ShapeDtypeStruct(y.shape, BF16)
    return pl.pallas_call(
        gate_back,
        grid=(width // tile,),
        in_specs=[
            pl.BlockSpec(sums.shape, lambda i: (0, 0)),
            col,
            col,
            col,
            col,
            pl.BlockSpec((1, tile), lambda i: (0, i)),
        ],
        out_specs=[col, col, col, pl.BlockSpec((8, tile), lambda i: (0, i))],
        out_shape=[low, low, low, jax.ShapeDtypeStruct((8, width), F32)],
        scratch_shapes=[pltpu.VMEM((2, length, 2 * PAIR), F32)],
        compiler_params=pltpu.CompilerParams(vmem_limit_bytes=VMEM_LIMIT),
        cost_estimate=busy(11, 20),
        name="gate_back",
    )(sums, scaled, z, y, x, gain)


def keep_or_give(place_ref, value, keep_ref, give_ref):
    mine = place_ref[0] % 2 == pl.program_id(0) % 2

    @pl.when(mine)
    def _():
        keep_ref[0] = value

    @pl.when(jnp.logical_not(mine))
    def _():
        give_ref[0] = value


def back_norm(members_ref, place_ref, tokens_ref, dz_ref, dx_ref, *refs):
    parts, (keep_ref, give_ref, gain_ref, dn_ref) = refs[:-4], refs[-4:]
    count = len(parts) // 2

    @pl.when(pl.program_id(0) == 0)
    def _():
        gain_ref[...] = jnp.zeros_like(gain_ref)

    tokens = tokens_ref[...].astype(F32)
    inv = lax.rsqrt(jnp.mean(tokens * tokens, axis=-1, keepdims=True) + EPS)
    sums = [None] * (D // SEG)
    for source, weights in ((dz_ref, parts[:count]), (dx_ref, parts[count:])):
        for o, at, w in by_segments(weights):
            part = nn(source[:, at : at + w.shape[0]], w[...])
            sums[o] = part if sums[o] is None else sums[o] + part
    for o, d_normed in enumerate(sums):
        at = pl.multiple_of(members_ref[o] * SEG, SEG)
        dn_ref[:, pl.ds(at, SEG)] = d_normed.astype(BF16)
        scaled = tokens_ref[:, pl.ds(at, SEG)].astype(F32) * inv
        gain_ref[0:1, pl.ds(at, SEG)] += jnp.sum(d_normed * scaled, axis=0, keepdims=True)
    keep_or_give(place_ref, dn_ref[...], keep_ref, give_ref)


def run_back_norm(members, place, tokens, dz, dx, weights_z, weights_x):
    length = tokens.shape[0]
    row = lambda i, t, p: (i, 0)
    half = pl.BlockSpec((1, GROUP, D), lambda i, t, p: (i // 2, 0, 0))
    halves_shape = jax.ShapeDtypeStruct((length // GROUP // 2, GROUP, D), BF16)
    return pl.pallas_call(
        back_norm,
        grid_spec=pltpu.PrefetchScalarGridSpec(
            num_scalar_prefetch=2,
            grid=(length // GROUP,),
            in_specs=[
                pl.BlockSpec((GROUP, D), row),
                pl.BlockSpec((GROUP, dz.shape[1]), row),
                pl.BlockSpec((GROUP, dx.shape[1]), row),
            ]
            + [resident(w, 3) for w in weights_z + weights_x],
            out_specs=[half, half, pl.BlockSpec((8, D), lambda i, t, p: (0, 0))],
            scratch_shapes=[pltpu.VMEM((GROUP, D), BF16)],
        ),
        out_shape=[halves_shape, halves_shape, jax.ShapeDtypeStruct((8, D), F32)],
        compiler_params=pltpu.CompilerParams(vmem_limit_bytes=VMEM_LIMIT),
        cost_estimate=busy(18, 24),
        name="back_norm",
    )(members, place, tokens, dz, dx, *weights_z, *weights_x)


def assemble_o(place_ref, o0, o1, o2, o3, out_ref):
    for k, ref in enumerate((o0, o1, o2, o3)):

        @pl.when(pl.program_id(0) == k)
        def _():
            out_ref[...] = ref[...].astype(F32)


def run_assemble_o(place, shares):
    m, (rows, cols) = len(shares), shares[0].shape
    return pl.pallas_call(
        assemble_o,
        grid_spec=pltpu.PrefetchScalarGridSpec(
            num_scalar_prefetch=1,
            grid=(m,),
            in_specs=[resident(share, 2) for share in shares],
            out_specs=pl.BlockSpec((rows, cols), lambda i, t: (t[0] ^ i, 0)),
        ),
        out_shape=jax.ShapeDtypeStruct((m * rows, cols), F32),
        compiler_params=pltpu.CompilerParams(vmem_limit_bytes=VMEM_LIMIT),
        cost_estimate=busy(3, 3),
        name="assemble_o",
    )(place, *shares)


def put_pairs(place_ref, refs, out_ref, g):
    m = len(refs)
    for k, ref in enumerate(refs):
        to = pl.multiple_of((place_ref[0] ^ k) * PAIR, PAIR)
        out_ref[pl.ds(to, PAIR), :] = ref[pl.ds(pl.multiple_of(g * PAIR, PAIR), PAIR), :].astype(F32)


def assemble_z(place_ref, z0, z1, z2, z3, out_ref):
    put_pairs(place_ref, (z0, z1, z2, z3), out_ref, pl.program_id(0))


def assemble_a(place_ref, held_ref, a0, a1, a2, a3, out_ref):
    put_pairs(place_ref, (a0, a1, a2, a3), out_ref, pl.program_id(0))


def assemble_b(place_ref, order_ref, held_ref, b0, b1, b2, b3, out_ref):
    step, last = pl.program_id(0), pl.num_programs(0) - 1
    refs = (b0, b1, b2, b3)
    width = last * PAIR
    core = width + 2 * STATE

    @pl.when(step < last)
    def _():
        put_pairs(place_ref, refs, out_ref, step)

    @pl.when(step == last)
    def _():
        total = jnp.zeros((2 * STATE, out_ref.shape[1]), F32)
        steps = jnp.zeros((HEADS, out_ref.shape[1]), F32)
        for k, x in enumerate(refs):
            total = total + x[width:core].astype(F32)
            steps = steps + nn(order_ref[place_ref[0] ^ k], x[core : core + TAIL])
        out_ref[: 2 * STATE] = total
        out_ref[2 * STATE : 2 * STATE + HEADS] = steps


def run_assemble_z(place, shares, columns):
    m, rows = len(shares), shares[0].shape[1]
    tile = m * PAIR
    return pl.pallas_call(
        assemble_z,
        grid_spec=pltpu.PrefetchScalarGridSpec(
            num_scalar_prefetch=1,
            grid=(DI // tile,),
            in_specs=[resident(s, 2) for s in shares],
            out_specs=pl.BlockSpec((tile, rows), lambda i, t: (i, 0)),
        ),
        out_shape=jax.ShapeDtypeStruct((columns, rows), F32),
        compiler_params=pltpu.CompilerParams(vmem_limit_bytes=VMEM_LIMIT),
        cost_estimate=busy(4, 6),
        name="assemble_z",
    )(place, *shares)


def run_assemble_b(place, order, held, shares, count):
    m, rows = len(shares), shares[0].shape[1]
    tile = m * PAIR
    first = 2 * (DI // tile) - count
    return pl.pallas_call(
        assemble_b,
        grid_spec=pltpu.PrefetchScalarGridSpec(
            num_scalar_prefetch=1,
            grid=(count + 1,),
            in_specs=[resident(order, 2), pl.BlockSpec(memory_space=pl.ANY)]
            + [resident(s, 2) for s in shares],
            out_specs=pl.BlockSpec((tile, rows), lambda i, t: (i + first, 0)),
        ),
        out_shape=jax.ShapeDtypeStruct(held.shape, F32),
        input_output_aliases={2: 0},
        compiler_params=pltpu.CompilerParams(vmem_limit_bytes=VMEM_LIMIT),
        cost_estimate=busy(3, 2),
        name="assemble_b",
    )(place, order, held, *shares)


def run_assemble_a(place, held, shares):
    m, rows = len(shares), shares[0].shape[1]
    tile = m * PAIR
    return pl.pallas_call(
        assemble_a,
        grid_spec=pltpu.PrefetchScalarGridSpec(
            num_scalar_prefetch=1,
            grid=(shares[0].shape[0] // PAIR,),
            in_specs=[pl.BlockSpec(memory_space=pl.ANY)] + [resident(s, 2) for s in shares],
            out_specs=pl.BlockSpec((tile, rows), lambda i, t: (i + DI // tile, 0)),
        ),
        out_shape=jax.ShapeDtypeStruct(held.shape, F32),
        input_output_aliases={1: 0},
        compiler_params=pltpu.CompilerParams(vmem_limit_bytes=VMEM_LIMIT),
        cost_estimate=busy(4, 5),
        name="assemble_a",
    )(place, held, *shares)


def body(
    tokens, norm_gain, w_in, conv_w, conv_b, dt_bias, a_log, d_skip, gate_gain, w_out, cotangent
):
    n, m = lax.axis_size("fsdp"), lax.axis_size("ctx")
    place = lax.axis_index("ctx")
    piece = tokens.shape[1]
    length = piece * m
    blocks = length // GROUP
    pairs = DI // PAIR // m
    width = pairs * PAIR
    heads = 2 * pairs
    rows = w_in.shape[0]
    core_cols = width + 2 * STATE
    head_cols = core_cols + heads
    ring = rows == SEG and (DI // PAIR) // n == m

    def of_pairs(array, axis):
        shape = array.shape
        each = shape[axis] // (pairs * m)
        split = array.reshape(shape[:axis] + (pairs, m, each) + shape[axis + 1 :])
        mine = lax.dynamic_index_in_dim(split, place, axis + 1, False)
        return mine.reshape(shape[:axis] + (pairs * each,) + shape[axis + 1 :])

    def of_heads(array):
        mine = of_pairs(array, 0)
        split = mine.reshape((pairs, 2) + mine.shape[1:]).swapaxes(0, 1)
        return split.reshape(mine.shape)

    all_tokens = lax.all_gather(tokens[0], "ctx", axis=0, tiled=True)
    seed = lax.all_gather(cotangent[0], "ctx", axis=0, tiled=True)


    columns = w_in.T
    total_cols = core_cols + ENDS
    cut = halves(total_cols)[0]
    place_ref = place.reshape(1).astype(jnp.int32)
    smalls = [norm_gain[None], gate_gain[None], conv_b[None], conv_w]
    small_rows = [-(-v.shape[1] // SEG) for v in smalls]

    def split(whole):
        upper, _ = halves(whole.shape[0])
        parts = [whole[:, o * SEG : (o + 1) * SEG] for o in range(D // SEG)]
        middle = parts[len(parts) // 2]
        return parts[: len(parts) // 2] + [middle[:upper], middle[upper:]] + parts[len(parts) // 2 + 1 :]

    if ring:
        me = ring_place(lax.axis_index("fsdp"), n)
        members = ring_member(me + jnp.arange(n), n).astype(jnp.int32)
        padded = [jnp.pad(v, ((0, 0), (0, k * SEG - v.shape[1]))) for v, k in zip(smalls, small_rows)]
        small = jnp.concatenate([v.reshape(-1) for v in padded]).reshape(-1, SEG)
        block_x, block_z, block_o = run_pack(place_ref, columns, w_out, small, pairs)
        ring_x, ring_z, ring_o = Gather(block_x, n), Gather(block_z, n), Gather(block_o, n)
        next_hop([ring_x], ())
        dt_bias, a_log, d_skip = next_hop([ring_x], (dt_bias, a_log, d_skip))
        for _ in range(n // 2 - 4):
            next_hop([ring_x], ())
        next_hop([ring_x, ring_z], ())
        next_hop([ring_x], (), *arrivals(ring_z))
        parts_x = ring_x.parts()
        all_tokens, members_late, parts_late = next_hop(
            [ring_z, ring_o], (all_tokens, members, parts_x), *arrivals(ring_x)
        )
    else:
        members = jnp.arange(D // SEG, dtype=jnp.int32)
        block_x = jnp.concatenate(
            [
                of_pairs(columns[DI : 2 * DI], 0),
                columns[2 * DI : 2 * DI + 2 * STATE],
                of_heads(columns[DI + CONV :]),
                jnp.zeros((ENDS - heads, rows), BF16),
            ],
            axis=0,
        )
        whole_x = lax.all_gather(block_x, "fsdp", axis=1, tiled=True)
        norm_whole = lax.all_gather(norm_gain[None], "fsdp", axis=1, tiled=True)
        at = core_cols + SMALL
        whole_x = jnp.concatenate([whole_x[:at], norm_whole, whole_x[at + 1 :]], axis=0)
        parts_x, parts_z = split(whole_x), split(lax.all_gather(of_pairs(columns[:DI], 0), "fsdp", axis=1, tiled=True))
        w_o = of_pairs(lax.all_gather(w_out, "fsdp", axis=0, tiled=True), 0)
        parts_o = [w_o[o * PAIR : (o + 1) * PAIR] for o in range(pairs)]
        middle, upper = parts_o[pairs // 2], halves(PAIR)[0]
        parts_o = parts_o[: pairs // 2] + [middle[:upper], middle[upper:]] + parts_o[pairs // 2 + 1 :]

    if ring:
        kept = run_collect(members_late, parts_late)
        spans, at = [], 0
        for v, each in zip(smalls, small_rows):
            here = kept[:, at : at + v.shape[0] * each].reshape(n, v.shape[0], each * SEG)
            spans.append(here[:, :, : v.shape[1]].transpose(1, 0, 2).reshape(v.shape[0], -1))
            at += v.shape[0] * each
        norm_full, gate_full, bias_full, taps_full = spans
    else:
        norm_full, gate_full, bias_full, taps_full = (
            lax.all_gather(v, "fsdp", axis=1, tiled=True).astype(F32) for v in smalls
        )
    gate_full = of_pairs(gate_full, 1)
    taps_full = jnp.concatenate([taps_full, bias_full], axis=0)
    taps = jnp.concatenate([of_pairs(taps_full[:, :DI], 1), taps_full[:, DI:]], axis=1)
    taps = jnp.pad(taps, ((0, 8 - KW - 1), (0, 0)))

    dt_bias_own, a_log_own = of_heads(dt_bias), of_heads(a_log)
    skip_own = of_pairs(d_skip, 0)
    a_neg = -jnp.exp(a_log_own)
    heads_in = jnp.broadcast_to(jnp.concatenate([dt_bias_own, a_neg])[:, None], (2 * heads, 128))
    skip_row = jnp.repeat(skip_own, HEADDIM)[None, :]

    normed, proj_x = run_front(members, all_tokens, parts_x)
    if ring:
        proj_x = next_hop([ring_z, ring_o], proj_x, *arrivals(ring_z, ring_o))
    act, table, ssd, starts = run_mix_forward(proj_x, taps, heads_in, skip_row, pairs)
    normed_z = normed
    if ring:
        for _ in range(n // 2 - 3):
            next_hop([ring_z, ring_o], (), ssd, *arrivals(ring_z, ring_o))
        normed_z = next_hop([ring_o], normed, *arrivals(ring_z))
        parts_z, parts_o = ring_z.parts(), ring_o.parts()
    proj_z = run_project(normed_z, parts_z)

    w_o, scaled, sums = run_gate_sums(members, seed, parts_o, proj_z, ssd, gate_full)
    sums = ctx_sum(sums, m)
    mixed, dy, d_z, gate_cols = run_gate_back(sums, scaled, proj_z, ssd, act, gate_full)

    grads_o = tn(mixed, seed).astype(BF16)
    conv_grads, head_grads, top, before = [], [], blocks - 1, None
    d_z_late, mixed_late = d_z, mixed
    if ring:
        sum_o = Reduce(lambda o: lax.dynamic_slice_in_dim(grads_o, members[o] * PAIR, PAIR, 0), n)
        d_z_late, mixed_late = next_hop([sum_o], (d_z, mixed))
    grads_z = tn(d_z_late, normed).astype(BF16)
    branch = nn(mixed_late, w_o).astype(BF16)
    if ring:
        sum_z = Reduce(lambda o: grads_z[:, o * SEG : (o + 1) * SEG], n)
    for at in range(2):
        if ring:
            sum_o.join()
            if at > 0:
                sum_z.join()
                branch_own.middle()
                dy, before, branch_own.sent = next_hop(
                    [sum_o, sum_z], (dy, before, branch_own.sent)
                )
                branch_own.send_far()
            else:
                dy, branch = next_hop([sum_o, sum_z], (dy, branch))
                branch_own = CtxReduce(*by_core(branch.reshape(m, piece, D), m), m)
        span = blocks // 2
        d_x, conv_part, head_part, *before = run_mix_backward(
            span, top, act, proj_x, taps, heads_in, skip_row, table, starts, dy, before
        )
        before = (d_x, *before)
        conv_grads.append(conv_part)
        head_grads.append(head_part)
        top -= span
    normed_late = normed
    if ring:
        sum_o.join()
        sum_z.join()
        d_x, normed_late, branch_own.far = next_hop(
            [sum_o, sum_z], (d_x, normed, branch_own.far)
        )
    else:
        branch_own = CtxReduce(*by_core(branch.reshape(m, piece, D), m), m)
        branch_own.middle()
        branch_own.send_far()
    grads_x = tn(d_x, normed_late).astype(BF16)
    d_x_late = d_x
    if ring:
        used = core_cols + TAIL
        sum_x = Reduce(
            lambda o: grads_x[:used, o * SEG : (o + 1) * SEG], n, run_cut(grads_x, used, n // 2)
        )
        part_o = sum_o.join().astype(BF16)
        sum_z.join()
        d_x_late, part_o, branch_own.far = next_hop(
            [sum_x, sum_z], (d_x, part_o, branch_own.far)
        )
        other_o = far_share(part_o, m)
    kept, given, d_gain = run_back_norm(
        members, place_ref, all_tokens, d_z, d_x_late, parts_z, parts_x
    )
    small = run_gather_small(conv_grads, head_grads, gate_cols, d_gain)

    flip = 1
    steps = []
    while flip < n:
        steps.append(flip)
        flip *= 2

    def small_step(small):
        if steps:
            small = small + lax.ppermute(small, "fsdp", ctx_route(n, steps.pop()))
        return small

    if ring:
        sum_x.join()
        part_z = sum_z.join().astype(BF16)
        kept, given, small, part_o, other_o, part_z, branch_own.far = next_hop(
            [sum_x], (kept, given, small, part_o, other_o, part_z, branch_own.far)
        )
    d_own = CtxReduce(kept, given, m)
    d_own.middle()
    d_own.send_far()
    small = small_step(small)
    output = (tokens[0].astype(F32) + branch_own.total()).astype(BF16)[None]
    if ring:
        sum_x.join()
        small, other_o, part_z, d_own.far = next_hop(
            [sum_x], (small, other_o, part_z, d_own.far), output
        )
        shares_o, other_z = near_share(part_o, other_o, m), far_share(part_z, m)
        grad_w_out = run_assemble_o(place_ref, shares_o)
    small = small_step(small)
    own = tokens[0].astype(F32)
    inv = lax.rsqrt(jnp.mean(own * own, axis=-1, keepdims=True) + EPS)
    d_direct = d_own.total() * norm_full
    along = jnp.mean(d_direct * own, axis=-1, keepdims=True)
    grad_tokens = (cotangent[0].astype(F32) + d_direct * inv - own * (inv * inv * inv * along))[None]
    if ring:
        for at in range(n // 2 - 3):
            sum_x.join()
            small, part_z, other_z = next_hop(
                [sum_x], (small, part_z, other_z), grad_tokens, grad_w_out
            )
        shares_z = near_share(part_z, other_z, m)
    while steps:
        small = small_step(small)
    if not ring:
        smalls_of = ctx_share(small, m)
    if ring:
        part_x = sum_x.join().astype(BF16)
        part_a, part_b = part_x[:cut], part_x[cut:]
        part_a, part_b, small, shares_z = barrier((part_a, part_b, small, shares_z))
        smalls_of = ctx_share(small, m)
        held = run_assemble_z(place_ref, shares_z, w_in.shape[1])
    by_place = jnp.zeros((m,) + small.shape, F32)
    for k in range(m):
        by_place = lax.dynamic_update_slice(by_place, smalls_of[k][None], (place ^ k, 0, 0))

    mine = lax.axis_index("fsdp")
    lines = [core_cols] * (KW + 1) + [width, width, D]
    found, at = [], 0
    for count in lines:
        found.append(by_place[:, at : at + count // SEG].reshape(m, 1, count))
        at += count // SEG
    conv_lines = jnp.concatenate(found[: KW + 1], axis=1)

    def interleaved(lines):
        return lines.reshape(m, -1, pairs, PAIR).transpose(1, 2, 0, 3).reshape(-1, DI)

    whole = jnp.concatenate(
        [interleaved(conv_lines[:, :, :width]), jnp.sum(conv_lines[:, :, width:], axis=0)], axis=1
    )
    each = conv_b.shape[0]
    grad_conv = lax.dynamic_slice_in_dim(whole, mine * each, each, 1)
    each = gate_gain.shape[0]
    grad_gate_gain = lax.dynamic_slice_in_dim(interleaved(found[KW + 1]), mine * each, each, 1)[0]
    grad_gain = lax.dynamic_slice_in_dim(jnp.sum(found[KW + 3], axis=0)[0], mine * rows, rows, 0)
    skips = jnp.sum(found[KW + 2].reshape(m, pairs, 2, HEADDIM), axis=3).reshape(m, 1, pairs, 2)
    of_steps = jnp.sum(by_place[:, by_place.shape[1] - 2 * heads :], axis=2)
    of_steps = of_steps.reshape(m, 2, 2, pairs).transpose(0, 1, 3, 2)
    per_head = jnp.concatenate([of_steps, skips], axis=1).transpose(1, 2, 0, 3).reshape(3, HEADS)
    grad_a_log = per_head[1] * -jnp.exp(a_log)
    if not ring:
        part_z = lax.psum_scatter(grads_z.astype(F32), "fsdp", scatter_dimension=1, tiled=True)
        part_x = lax.psum_scatter(grads_x.astype(F32), "fsdp", scatter_dimension=1, tiled=True)
        whole_o = jnp.zeros((pairs, m, PAIR, D), F32)
        whole_o = lax.dynamic_update_index_in_dim(
            whole_o, grads_o.astype(F32).reshape(pairs, PAIR, D), place, 1
        )
        grad_w_out = lax.psum_scatter(whole_o.reshape(DI, D), "fsdp", scatter_dimension=0, tiled=True)
        grad_w_out = lax.psum(grad_w_out, "ctx")
        held = run_assemble_z(place_ref, ctx_share(part_z.astype(BF16), m), w_in.shape[1])
        part_x = part_x.astype(BF16)
        part_a, part_b = part_x[:cut], part_x[cut : core_cols + TAIL]
    other_b, other_a = far_share(part_b, m), far_share(part_a, m)
    order = np.zeros((m, HEADS, TAIL), np.float32)
    for member in range(m):
        for h in range(heads):
            order[member, (h % pairs) * 2 * m + 2 * member + h // pairs, h] = 1.0
    shares_b = near_share(part_b, other_b, m)
    held = run_assemble_b(place_ref, jnp.asarray(order, BF16), held, shares_b, pairs - cut // PAIR)
    shares_a = near_share(part_a, other_a, m)
    grad_w_in = run_assemble_a(place_ref, held, shares_a)
    return (
        output,
        grad_tokens,
        grad_gain,
        grad_w_in.T,
        grad_conv[:KW],
        grad_conv[KW],
        per_head[0],
        grad_a_log,
        per_head[2],
        grad_gate_gain,
        grad_w_out,
    )


def solution(mesh):
    in_specs = (
        P("fsdp", "ctx", None),
        P("fsdp"),
        P("fsdp", None),
        P(None, "fsdp"),
        P("fsdp"),
        P(),
        P(),
        P(),
        P("fsdp"),
        P("fsdp", None),
        P("fsdp", "ctx", None),
    )
    out_specs = (
        P("fsdp", "ctx", None),
        P("fsdp", "ctx", None),
        P("fsdp"),
        P("fsdp", None),
        P(None, "fsdp"),
        P("fsdp"),
        P(),
        P(),
        P(),
        P("fsdp"),
        P("fsdp", None),
    )
    return jax.shard_map(body, mesh=mesh, in_specs=in_specs, out_specs=out_specs, check_vma=False)
```
